256 devices in a mesh: dp: 16 (over z_hi, x, core), head: 16 (over z_lo, y).
Axes of the slice: x: 4, y: 4, z: 8 (z_hi: 2, z_lo: 4; z = z_hi * 4 + z_lo), core: 2. Of those that a mesh axis runs over, the one named last changes fastest.
Arguments:
- hidden: bfloat16 [8192, 1536], P('dp'), may hold values from -6 to 6
- token_prompt: int32 [8192], replicated, may hold values from 0 to 7, never falling along the last dimension, each value on 1 to 2048 neighbouring positions
- request_prompt: int32 [64], P('dp'), may hold values from 0 to 7
- in_gain: float32 [1536], replicated, may hold values from 0.1 to 1.9
- w_zx: float32 [1536, 2, 3072], P('dp', None, 'head'), may hold values from -0.15625 to 0.15625
- w_bc: float32 [1536, 256], P('dp'), may hold values from -0.0390625 to 0.0390625
- w_dt: float32 [1536, 48], P('dp', 'head'), may hold values from -0.15625 to 0.15625
- dt_bias: float32 [48], P('head'), may hold values from -3 to -0.5
- a_log: float32 [48], P('head'), may hold values from -9.5 to -1.6
- conv_x: float32 [4, 3072], P(None, 'head'), may hold values from -3 to 3
- conv_bc: float32 [4, 256], replicated, may hold values from -3 to 3
- skip_gain: float32 [48], P('head'), may hold values from 0.5 to 2
- out_gain: float32 [3072], P('head'), may hold values from 0.1 to 1.9
- w_out: bfloat16 [3072, 1536], P('head'), may hold values from -0.109375 to 0.109375
Outputs:
- layer_out: bfloat16 [8192, 1536], P(('dp', 'head'))
- request_states: float32 [64, 48, 64, 128], P('dp', 'head')
The draws below stay inside these ranges and needn't reach their ends.
Inputs may be any that keep to these rules, and one draw needn't show every extreme that they name: `token_prompt`: prompt ids never fall along the tokens; each of the 8 prompts has at least one token.
All inputs are finite; a program needn't handle non-finite values.
Results may differ from the reference program's by a relative error of at most 0.012.
Values may be sent and summed in bfloat16 or wider, within the bound.
A program may use at most 64 MiB of HBM per device.

```python
import math
import jax
import jax.numpy as jnp
import numpy as np
from jax import lax

D = 1536
HEADS = 48
HDIM = 64
NSTATE = 128
KCONV = 4
BLOCK = 256
PROMPTS = 8
INNER = 3072
TOKENS = 8192
REQUESTS = 64


def set_ends(drawn, own_key, low, high):
    longest = drawn.shape.index(max(drawn.shape))
    spots = []
    for shift in (0, 1):
        where = [jax.random.randint(jax.random.fold_in(own_key, axis), (), 0, length) for axis, length in enumerate(drawn.shape)]
        where[longest] = (where[longest] + shift) % drawn.shape[longest]
        spots.append(tuple(where))
    return drawn.at[spots[0]].set(low).at[spots[1]].set(high)


def block_scale(stream_key, shape, split, smallest, top_value):
    gain, own = 1.0, jax.random.fold_in(stream_key, 6)
    for dim, parts in split:
        draws = jnp.exp(jax.random.uniform(jax.random.fold_in(own, dim), (parts,), jnp.float32, smallest / len(split), top_value / len(split)))
        gain = gain * jnp.repeat(draws, shape[dim] // parts).reshape([-1 if axis == dim else 1 for axis in range(len(shape))])
    return gain


def length_profile(count, total, reach, skew):
    loads = [(1 << 20) // math.isqrt(grade ** skew) + 1 for grade in range(2, count + 1)]
    rest, given = total - reach - (count - 1), [1] * (count - 1)
    while rest > 0:
        movable = [i for i in range(count - 1) if given[i] < reach]
        pool, remaining = sum([loads[i] for i in movable]), rest
        for i in movable:
            extra = min(reach - given[i], max(1, remaining * loads[i] // pool), rest)
            given[i] = given[i] + extra
            rest = rest - extra
    return np.array([reach] + given)


def uneven(key, amount, total, most, skew):
    if amount == 2:
        one = jax.random.randint(key, (), max(1, total - most), min(most, total - 1) + 1)
        return jnp.stack([one, total - one])
    tallies = jnp.asarray(length_profile(amount, total, most, skew), jnp.int32)
    twos = (amount - 1) // 2
    source_of, receiver = tallies[1:1 + 2 * twos:2], tallies[2:2 + 2 * twos:2]
    room = jnp.minimum(source_of - 1, most - receiver)
    moved = jax.random.randint(jax.random.fold_in(key, 1), (twos,), 0, 1 << 20) % (room + 1)
    tallies = tallies.at[1:1 + 2 * twos:2].set(source_of - moved).at[2:2 + 2 * twos:2].set(receiver + moved)
    return tallies[jax.random.permutation(jax.random.fold_in(key, 2), amount)]


def bell_draw(rng, dims, scale, most, shards=(), kind=jnp.bfloat16):
    level = block_scale(rng, dims, shards, -0.22, 0.18) if shards else 1.0
    result = jax.random.normal(rng, dims, jnp.float32) * scale * level
    return jnp.minimum(jnp.maximum(result, -most), most).astype(kind)


def setup_inputs(seed: int = 0) -> dict:
    seeds = jax.random.split(jax.random.key(seed), 15)
    hidden = bell_draw(seeds[0], (TOKENS, D), 1.0, 6.0, ((0, 16),))
    token_prompt = jnp.searchsorted(jnp.cumsum(uneven(seeds[1], PROMPTS, TOKENS, TOKENS // 4, 2)), jnp.arange(TOKENS), side="right").astype(jnp.int32)
    request_prompt = set_ends(jax.random.randint(seeds[2], (REQUESTS,), 0, PROMPTS), jax.random.fold_in(seeds[2], 1), 0, PROMPTS - 1).astype(jnp.int32)
    in_gain = jnp.clip(1.0 + 0.18 * jax.random.normal(seeds[3], (D,), jnp.float32), 0.1, 1.9)
    w_zx = bell_draw(seeds[4], (D, 2, INNER), D ** -0.5, 0.15625, ((0, 16), (2, 16)), jnp.float32)
    w_bc = bell_draw(seeds[5], (D, 2 * NSTATE), (16 * D) ** -0.5, 0.0390625, ((0, 16),), jnp.float32)
    w_dt = bell_draw(seeds[6], (D, HEADS), D ** -0.5, 0.15625, ((0, 16), (1, 16)), jnp.float32)
    dt_bias = jnp.clip(-3.0 + 2.5 * jax.random.uniform(seeds[7], (HEADS,), jnp.float32) ** block_scale(seeds[7], (HEADS,), ((0, 16),), -0.2, 0.2), -3.0, -0.5)
    a_log = jnp.clip(-9.5 + 7.9 * jax.random.uniform(seeds[8], (HEADS,), jnp.float32) ** block_scale(seeds[8], (HEADS,), ((0, 16),), -0.2, 0.2), -9.5, -1.6)
    conv_x = bell_draw(seeds[9], (KCONV, INNER), KCONV ** -0.5, 3.0, ((1, 16),), jnp.float32)
    conv_bc = bell_draw(seeds[10], (KCONV, 2 * NSTATE), KCONV ** -0.5, 3.0, (), jnp.float32)
    skip_gain = jnp.clip(0.5 + 1.5 * jax.random.uniform(seeds[11], (HEADS,), jnp.float32) ** block_scale(seeds[11], (HEADS,), ((0, 16),), -0.2, 0.2), 0.5, 2.0)
    out_gain = jnp.clip(1.0 + 0.18 * jax.random.normal(seeds[12], (INNER,), jnp.float32), 0.1, 1.9)
    w_out = bell_draw(seeds[13], (INNER, D), INNER ** -0.5, 0.109375, ((0, 16),))
    return {"hidden": hidden, "token_prompt": token_prompt, "request_prompt": request_prompt, "in_gain": in_gain, "w_zx": w_zx, "w_bc": w_bc, "w_dt": w_dt, "dt_bias": dt_bias, "a_log": a_log, "conv_x": conv_x, "conv_bc": conv_bc, "skip_gain": skip_gain, "out_gain": out_gain, "w_out": w_out}


EPSILON = 1e-05

def rms_scale(values):
    return lax.rsqrt(lax.optimization_barrier(jnp.mean(values * values, axis=-1, keepdims=True)) + EPSILON)

def conv_core(extended, extended_ids, token_ids, weights):
    length = token_ids.shape[0]
    total = jnp.zeros((length, extended.shape[1]), jnp.float32)
    for offset in range(weights.shape[0]):
        same = (extended_ids[offset:offset + length] == token_ids)[:, None]
        total = total + jnp.where(same, weights[offset] * extended[offset:offset + length].astype(jnp.float32), 0.0)
    return jax.nn.silu(total).astype(jnp.bfloat16)

def causal_conv(signal, weights, token_ids):
    margin = weights.shape[0] - 1
    padded = jnp.concatenate([jnp.zeros((margin, signal.shape[1]), signal.dtype), signal], axis=0)
    padded_ids = jnp.concatenate([jnp.full((margin,), -1, jnp.int32), token_ids])
    return conv_core(padded, padded_ids, token_ids, weights)

def reference(hidden, token_prompt, request_prompt, in_gain, w_zx, w_bc, w_dt, dt_bias, a_log, conv_x, conv_bc, skip_gain, out_gain, w_out):
    hidden_f = hidden.astype(jnp.float32)
    normed = (hidden_f * rms_scale(hidden_f) * in_gain).astype(jnp.bfloat16)
    proj_zx = jnp.dot(normed, w_zx.astype(jnp.bfloat16).reshape(D, 2 * INNER), preferred_element_type=jnp.float32).astype(jnp.bfloat16)
    gate_z = proj_zx[:, :INNER]
    inner_x = proj_zx[:, INNER:]
    proj_bc = jnp.dot(normed, w_bc.astype(jnp.bfloat16), preferred_element_type=jnp.float32).astype(jnp.bfloat16)
    proj_dt = jnp.dot(normed, w_dt.astype(jnp.bfloat16), preferred_element_type=jnp.float32).astype(jnp.bfloat16)
    step_size = jax.nn.softplus(proj_dt.astype(jnp.float32) + dt_bias)
    rate = step_size * -jnp.exp(a_log)
    conv_inner = causal_conv(inner_x, conv_x, token_prompt)
    conv_bc_out = causal_conv(proj_bc, conv_bc, token_prompt)
    blocks = TOKENS // BLOCK
    x_heads = conv_inner.reshape(blocks, BLOCK, HEADS, HDIM)
    b_conv = conv_bc_out[:, :NSTATE].reshape(blocks, BLOCK, NSTATE)
    c_conv = conv_bc_out[:, NSTATE:].reshape(blocks, BLOCK, NSTATE)
    before_ids = jnp.concatenate([jnp.full((1,), -1, jnp.int32), token_prompt[BLOCK - 1:TOKENS - 1:BLOCK]])
    start_pos = jnp.arange(blocks, dtype=jnp.int32) * BLOCK
    prompt_ids = jnp.arange(PROMPTS, dtype=jnp.int32)
    last_index = (lax.optimization_barrier(jnp.sum((token_prompt[None, :] <= prompt_ids[:, None]).astype(jnp.int32), axis=1)) - 1).astype(jnp.int32)
    position = jnp.arange(BLOCK, dtype=jnp.int32)

    def advance(carry, inputs):
        state, table = carry
        x_blk, b_blk, c_blk, step_blk, rate_blk, ids_blk, before_id, start = inputs
        prefix = jnp.cumsum(rate_blk, axis=0)
        prefix_t = prefix.T
        same = (ids_blk[:, None] == ids_blk[None, :]) & (position[None, :] <= position[:, None])
        gaps = prefix_t[:, :, None] - prefix_t[:, None, :]
        decay = jnp.where(same[None], jnp.exp(jnp.where(same[None], gaps, 0.0)), 0.0)
        scores = jnp.dot(c_blk, b_blk.T, preferred_element_type=jnp.float32)
        mixing = (scores[None] * decay * step_blk.T[:, None, :]).astype(jnp.bfloat16)
        y_intra = jnp.einsum('hts,shp->thp', mixing.astype(jnp.float32), x_blk.astype(jnp.float32))
        entering = ids_blk == before_id
        inter_scale = jnp.where(entering[:, None], jnp.exp(prefix), 0.0)
        y_inter = inter_scale[:, :, None] * jnp.einsum('tn,hpn->thp', c_blk.astype(jnp.float32), state, precision=lax.Precision.HIGHEST)
        end_id = ids_blk[-1]
        alive = ids_blk == end_id
        weight_end = jnp.where(alive[None, :], jnp.exp(jnp.where(alive[None, :], prefix_t[:, -1:] - prefix_t, 0.0)), 0.0) * step_blk.T
        b_weighted = (weight_end[:, :, None] * b_blk.astype(jnp.float32)[None]).astype(jnp.bfloat16)
        local_state = jnp.einsum('hsn,shp->hpn', b_weighted.astype(jnp.float32), x_blk.astype(jnp.float32))
        carry_gain = jnp.where(end_id == before_id, jnp.exp(prefix_t[:, -1]), 0.0)
        local_last = last_index - start
        ends_here = (local_last >= 0) & (local_last < BLOCK)
        clipped = jnp.clip(local_last, 0, BLOCK - 1)

        def with_ends():
            prefix_last = prefix[clipped]
            pick = ends_here[:, None] & (ids_blk[None, :] == prompt_ids[:, None]) & (position[None, :] <= clipped[:, None])
            spans = prefix_last[:, :, None] - prefix_t[None]
            weight_last = jnp.where(pick[:, None, :], jnp.exp(jnp.where(pick[:, None, :], spans, 0.0)), 0.0) * step_blk.T[None]
            b_last = (weight_last[..., None] * b_blk.astype(jnp.float32)[None, None]).astype(jnp.bfloat16)
            last_local = jnp.einsum('ghsn,shp->ghpn', b_last.astype(jnp.float32), x_blk.astype(jnp.float32))
            last_gain = jnp.where((ends_here & (prompt_ids == before_id))[:, None], jnp.exp(prefix_last), 0.0)
            return last_local + last_gain[:, :, None, None] * state[None]

        def without_ends():
            return jnp.zeros(table.shape, jnp.float32)
        last_states = lax.cond(jnp.any(ends_here), with_ends, without_ends)
        new_state = carry_gain[:, None, None] * state + local_state
        return ((new_state, table + last_states), y_intra + y_inter)
    init = (jnp.zeros((HEADS, HDIM, NSTATE), jnp.float32), jnp.zeros((PROMPTS, HEADS, HDIM, NSTATE), jnp.float32))
    inputs = (x_heads, b_conv, c_conv, step_size.reshape(blocks, BLOCK, HEADS), rate.reshape(blocks, BLOCK, HEADS), token_prompt.reshape(blocks, BLOCK), before_ids, start_pos)
    (final_state, table), y_blocks = lax.scan(advance, init, inputs)
    ssd_out = y_blocks.reshape(TOKENS, HEADS, HDIM) + skip_gain[None, :, None] * conv_inner.astype(jnp.float32).reshape(TOKENS, HEADS, HDIM)
    gated = ssd_out.reshape(TOKENS, INNER) * jax.nn.silu(gate_z.astype(jnp.float32))
    normed_out = (gated * rms_scale(gated) * out_gain).astype(jnp.bfloat16)
    mixed = jnp.dot(normed_out, w_out, preferred_element_type=jnp.float32)
    layer_out = (hidden_f + mixed).astype(jnp.bfloat16)
    one_hot = (request_prompt[:, None] == prompt_ids[None, :]).astype(jnp.float32)
    request_states = jnp.einsum('rg,ghpn->rhpn', one_hot, table, precision=lax.Precision.HIGHEST)
    return (layer_out, request_states)
```

```python
import jax
import jax.numpy as jnp
from jax import lax
from jax.experimental import pallas as pl
from jax.experimental.pallas import tpu as pltpu
from jax.sharding import PartitionSpec as P

MESH = pl.DeviceIdType.MESH
F32 = jnp.float32
BF16 = jnp.bfloat16
EPSILON = 1e-05

DP = 16
HD = 16
D = 1536
TOK = 512
EXT = TOK + 16
ROWS = 96
HEADS = 3
FEAT = 192
NSTATE = 128
PROMPTS = 8
OUTW = D + 128

W_IDS = 0
T_IDS = 15
F_IDS = 30
HALO = 45
INFO_UP = 46
INFO_DN = 50
STATE = 54
WO_UP = 58
WO_DN = 64
WO_UPP = 70
WO_DNP = 76
TAB0 = 82
TABZ = 83
TABX = 84
A2A = 87
RSY = 90
N_MSG = 93


def dot(a, b):
    return lax.dot_general(a, b, (((1,), (0,)), ((), ())), preferred_element_type=F32)


def dot_t(a, b):
    return lax.dot_general(a, b, (((1,), (1,)), ((), ())), preferred_element_type=F32)


def lane_cumsum(v):
    width = v.shape[1]
    lane = lax.broadcasted_iota(jnp.int32, v.shape, 1)
    step = 1
    while step < width:
        v = v + jnp.where(lane >= step, pltpu.roll(v, step, 1), 0.0)
        step *= 2
    return v


def run_end(v, ids):
    width = v.shape[1]
    lane = lax.broadcasted_iota(jnp.int32, v.shape, 1)
    step = 1
    while step < width:
        same = (pltpu.roll(ids, width - step, 1) == ids) & (lane < width - step)
        v = jnp.where(same, pltpu.roll(v, width - step, 1), v)
        step *= 2
    return v


def body(
    ids_ref, req_ref, dtb_ref, alog_ref, skip_ref, hid_ref, gain_ref, wzx_ref, wbc_ref,
    wdt_ref, cx_ref, cbc_ref, og_ref, wout_ref, out_ref, st_ref,
    w_buf, wst, wdt_all, wdt_mat, halo, nrm, idc, u_buf, taps, x_t, x_b, b_b, c_b, b_all,
    info_tx, info_rx, l_tx, l_rx, s_in, cols, smask, loc, tab0, tabs, tabz, tabm, tabx, fin,
    g_send, a_rx, wo, part, own_acc, rs_rx, send_sem, recv_sem, local_sem,
):
    dp = lax.axis_index("dp")
    hd = lax.axis_index("head")
    zh = dp // 8
    x = (dp // 2) % 4
    c = dp % 2
    zl = hd // 4
    y = hd % 4
    sgn = 1 - 2 * c

    def dev(z_, x_, c_):
        return z_ * 8 + lax.rem(x_ + 8, 4) * 2 + c_

    ahead = dev(zh, x + sgn, c)
    behind = dev(zh, x - sgn, c)
    across = dev(1 - zh, x, c)
    mate = dev(zh, x, 1 - c)

    def dpid(d):
        return {"dp": d}

    def hdid(z_, y_):
        return {"head": z_ * 4 + y_}

    def msg(m, src, dst, to):
        return pltpu.make_async_remote_copy(
            src_ref=src, dst_ref=dst, send_sem=send_sem.at[m], recv_sem=recv_sem.at[m],
            device_id=to, device_id_type=MESH,
        )

    pending = []

    def send(m, src, dst, to, cond=None):
        if cond is None:
            msg(m, src, dst, to).start()
        else:
            @pl.when(cond)
            def _():
                msg(m, src, dst, to).start()
        pending.append((m, src, dst, to, cond))

    def recv(m, dst, to, cond=None):
        if cond is None:
            msg(m, dst, dst, to).wait_recv()
        else:
            @pl.when(cond)
            def _():
                msg(m, dst, dst, to).wait_recv()

    class Gather:
        def __init__(self, families):
            self.families = families

        def send(self, k, owner, to):
            for base, ref_of in self.families:
                r = ref_of(owner)
                send(base + k, r, r, dpid(to))

        def recv(self, k, owner):
            for base, ref_of in self.families:
                recv(base + k, ref_of(owner), dpid(mate))

        def own(self):
            self.send(3, dp, across)
            self.send(0, dp, ahead)
            self.send(1, dp, behind)
            self.send(7, dp, mate)

        def near(self):
            self.recv(0, dev(zh, x - sgn, c))
            self.send(2, dev(zh, x - sgn, c), ahead)
            self.send(8, dev(zh, x - sgn, c), mate)
            self.recv(1, dev(zh, x + sgn, c))
            self.send(9, dev(zh, x + sgn, c), mate)

        def cross(self):
            self.recv(3, dev(1 - zh, x, c))
            self.send(4, dev(1 - zh, x, c), ahead)
            self.send(5, dev(1 - zh, x, c), behind)
            self.send(11, dev(1 - zh, x, c), mate)

        def near_rest(self):
            self.recv(2, dev(zh, x + 2, c))
            self.send(10, dev(zh, x + 2, c), mate)
            self.recv(7, dev(zh, x, 1 - c))
            self.recv(8, dev(zh, x + sgn, 1 - c))
            self.recv(9, dev(zh, x - sgn, 1 - c))
            self.recv(10, dev(zh, x + 2, 1 - c))

        def far(self):
            o = 1 - zh
            self.recv(4, dev(o, x - sgn, c))
            self.send(6, dev(o, x - sgn, c), ahead)
            self.send(12, dev(o, x - sgn, c), mate)
            self.recv(5, dev(o, x + sgn, c))
            self.send(13, dev(o, x + sgn, c), mate)
            self.recv(6, dev(o, x + 2, c))
            self.send(14, dev(o, x + 2, c), mate)
            self.recv(11, dev(o, x, 1 - c))
            self.recv(12, dev(o, x + sgn, 1 - c))
            self.recv(13, dev(o, x - sgn, 1 - c))
            self.recv(14, dev(o, x + 2, 1 - c))

    barrier = pltpu.get_barrier_semaphore()
    for k in range(1, DP):
        pl.semaphore_signal(
            barrier, inc=1, device_id=dpid(lax.rem(dp + k, DP)), device_id_type=MESH
        )
    for k in range(1, 4):
        pl.semaphore_signal(
            barrier, inc=1, device_id=hdid(zl, lax.rem(y + k, 4)), device_id_type=MESH
        )
        pl.semaphore_signal(
            barrier, inc=1, device_id=hdid(lax.rem(zl + k, 4), y), device_id_type=MESH
        )

    zw = wzx_ref[:, 0, :]
    xw = wzx_ref[:, 1, :]
    wst[:, 0:128] = xw[:, 0:128]
    wst[:, 128:256] = jnp.concatenate([xw[:, 128:192], zw[:, 128:192]], axis=1)
    wst[:, 256:384] = zw[:, 0:128]
    wst[:, 384:640] = wbc_ref[...]
    own_rows = pl.multiple_of(dp * ROWS, ROWS)
    w_buf[pl.ds(own_rows, ROWS), :] = wst[...].astype(BF16)
    wdt_pad = jnp.concatenate(
        [
            jnp.concatenate([wdt_ref[...], jnp.zeros((ROWS, 125), F32)], axis=1),
            jnp.zeros((32, 128), F32),
        ],
        axis=0,
    )
    wdt_all[dp] = wdt_pad.T[0:8, :]

    def w_rows(owner):
        return w_buf.at[pl.ds(pl.multiple_of(owner * ROWS, ROWS), ROWS), :]

    def t_rows(owner):
        return wdt_all.at[owner]

    weights = Gather([(W_IDS, w_rows), (T_IDS, t_rows)])
    own_copy = pltpu.make_async_copy(wout_ref, wo.at[zl], local_sem)
    own_copy.start()

    @pl.when(dp == 0)
    def _():
        halo[...] = jnp.zeros_like(halo)

    for j in range(4):
        @pl.when(dp < j + 1)
        def _():
            info_rx[j] = jnp.zeros((16, 128), F32)
            l_rx[j] = jnp.zeros((FEAT, NSTATE), BF16)

        @pl.when(dp + j + 1 > DP - 1)
        def _():
            info_rx[4 + j] = jnp.zeros((16, 128), F32)

    pl.semaphore_wait(barrier, DP - 1 + 6)

    weights.own()
    send(HALO, hid_ref.at[pl.ds(TOK - 16, 16), :], halo, dpid(lax.rem(dp + 1, DP)), dp < DP - 1)

    own_ids = ids_ref[dp].astype(F32)
    prev_ids = ids_ref[jnp.maximum(dp - 1, 0)].astype(F32)
    prev_col = jnp.broadcast_to(prev_ids[3:4, :], (128, 128)).T[112:128, :]
    first_dev = jnp.zeros((16, 128), jnp.int32) + dp == 0
    idc[0:16, :] = jnp.where(first_dev, -1.0, prev_col)
    for q in range(4):
        idc[16 + 128 * q : 144 + 128 * q, :] = jnp.broadcast_to(own_ids[q : q + 1, :], (128, 128)).T
    id_row = jnp.concatenate([own_ids[q : q + 1, :] for q in range(4)], axis=1)

    taps[...] = jnp.zeros_like(taps)
    taps[0:4, 0:128] = cx_ref[:, 0:128]
    taps[0:4, 128:192] = cx_ref[:, 128:192]
    taps[0:4, 256:512] = cbc_ref[...]

    gain = gain_ref[...]

    def norm_rows(rows):
        h = rows.astype(F32)
        scale = lax.rsqrt(jnp.mean(h * h, axis=1, keepdims=True) + EPSILON)
        return (h * scale * gain).astype(BF16)

    def norm_step(i, carry):
        r = pl.multiple_of(i * 32, 32)
        nrm[pl.ds(pl.multiple_of(16 + r, 16), 32), :] = norm_rows(hid_ref[pl.ds(r, 32), :])
        return carry

    lax.fori_loop(0, TOK // 32, norm_step, 0)
    recv(HALO, halo, dpid(mate), dp > 0)
    nrm[0:16, :] = norm_rows(halo[...])

    half = pl.multiple_of(c * 96, 96)

    def wo_rows(z_):
        return wo.at[jnp.clip(z_, 0, 3), pl.ds(half, 96), :]

    def wo_mate_rows(z_):
        return wo.at[jnp.clip(z_, 0, 3), pl.ds(pl.multiple_of((1 - c) * 96, 96), 96), :]

    def wo_start():
        send(WO_UP, wo_rows(zl), wo_rows(zl), hdid(jnp.minimum(zl + 1, 3), y), zl < 3)
        send(WO_DN, wo_rows(zl), wo_rows(zl), hdid(jnp.maximum(zl - 1, 0), y), zl > 0)

    def wo_step(d):
        up, dn = zl >= d, zl + d <= 3
        recv(WO_UP + d - 1, wo_rows(zl - d), dpid(mate), up)
        if d < 3:
            send(WO_UP + d, wo_rows(zl - d), wo_rows(zl - d), hdid(jnp.minimum(zl + 1, 3), y), up & (zl < 3))
        send(WO_UPP + d - 1, wo_rows(zl - d), wo_rows(zl - d), dpid(mate), up)
        recv(WO_DN + d - 1, wo_rows(zl + d), dpid(mate), dn)
        if d < 3:
            send(WO_DN + d, wo_rows(zl + d), wo_rows(zl + d), hdid(jnp.maximum(zl - 1, 0), y), dn & (zl > 0))
        send(WO_DNP + d - 1, wo_rows(zl + d), wo_rows(zl + d), dpid(mate), dn)

    def wo_finish():
        for d in range(1, 4):
            recv(WO_UPP + d - 1, wo_mate_rows(zl - d), dpid(mate), zl >= d)
            recv(WO_DNP + d - 1, wo_mate_rows(zl + d), dpid(mate), zl + d <= 3)

    weights.near()
    weights.cross()
    own_copy.wait()
    wo_start()
    weights.near_rest()

    k_half = D // 2
    k_own = pl.multiple_of(zh * k_half, k_half)
    k_far = pl.multiple_of((1 - zh) * k_half, k_half)
    for n in range(0, 640, 128):
        u_buf[:, n : n + 128] = dot(nrm[:, pl.ds(k_own, k_half)], w_buf[pl.ds(k_own, k_half), n : n + 128])

    weights.far()

    for j in range(DP):
        rows = jnp.concatenate([wdt_all[j], jnp.zeros((120, 128), F32)], axis=0).T
        wdt_mat[ROWS * j : ROWS * j + ROWS, :] = rows[0:ROWS, :].astype(BF16)
    dt_cols = dot(nrm[16:EXT, :], wdt_mat[...])
    dt_rows = dt_cols.T[0:8, :].astype(BF16).astype(F32)
    sub = lax.broadcasted_iota(jnp.int32, (8, TOK), 0)
    lane = lax.broadcasted_iota(jnp.int32, (8, TOK), 1)

    def by_head(ref, s):
        return jnp.where(s == 0, ref[0], jnp.where(s == 1, ref[1], ref[2]))

    pre = dt_rows + by_head(dtb_ref, sub)
    step_rows = jnp.maximum(pre, 0.0) + jnp.log1p(jnp.exp(-jnp.abs(pre)))
    rate_rows = -step_rows * jnp.exp(by_head(alog_ref, sub))
    prefix = lane_cumsum(rate_rows)
    id8 = jnp.broadcast_to(id_row, (8, TOK))
    at_end = run_end(prefix, id8)
    first_end = at_end[:, 0:1]
    total = prefix[:, TOK - 1 : TOK]
    info_tx[0:8, :] = jnp.broadcast_to(first_end, (8, 128))
    info_tx[8:16, :] = jnp.broadcast_to(total, (8, 128))
    for j in range(4):
        send(INFO_UP + j, info_tx, info_rx.at[j], dpid(lax.rem(dp + j + 1, DP)), dp + j + 1 < DP)
        send(INFO_DN + j, info_tx, info_rx.at[4 + j], dpid(lax.rem(dp - j - 1 + DP, DP)), dp >= j + 1)

    to_end = jnp.exp(at_end - prefix) * step_rows
    cols[...] = jnp.concatenate([prefix, jnp.zeros((120, TOK), F32)], axis=0).T

    for n in range(0, 640, 128):
        u_buf[:, n : n + 128] += dot(nrm[:, pl.ds(k_far, k_half)], w_buf[pl.ds(k_far, k_half), n : n + 128])

    for r in range(0, EXT, 176):
        u_buf[r : r + 176, :] = u_buf[r : r + 176, :].astype(BF16).astype(F32)

    for q in range(4):
        r = 128 * q
        now = idc[16 + r : 144 + r, :]
        same = [jnp.where(idc[13 + k + r : 141 + k + r, :] == now, 1.0, 0.0) for k in range(3)]

        def conv(col, tap):
            acc = taps[3:4, tap : tap + 128] * u_buf[16 + r : 144 + r, col : col + 128]
            for k in range(3):
                acc = acc + same[k] * (
                    taps[k : k + 1, tap : tap + 128] * u_buf[13 + k + r : 141 + k + r, col : col + 128]
                )
            return (acc * jax.nn.sigmoid(acc)).astype(BF16)

        x0 = conv(0, 0)
        x1 = conv(128, 128)
        x_b[r : r + 128, 0:128] = x0
        x_b[r : r + 128, 128:256] = x1
        x_t[0:128, r : r + 128] = x0.astype(F32).T
        x_t[128:192, r : r + 128] = x1.astype(F32).T[0:64, :]
        b_b[r : r + 128, :] = conv(384, 256)
        c_b[r : r + 128, :] = conv(512, 384)

    last_id = id_row[:, TOK - 1 : TOK]
    is_last = id8 == jnp.broadcast_to(last_id, (8, TOK))

    def weighted_x(weight):
        return jnp.concatenate(
            [x_t[64 * h : 64 * h + 64, :] * weight[h : h + 1, :] for h in range(HEADS)], axis=0
        ).astype(BF16)

    l_tx[...] = dot(weighted_x(jnp.where(is_last, to_end, 0.0)), b_b[...]).astype(BF16)
    for j in range(4):
        send(STATE + j, l_tx, l_rx.at[j], dpid(lax.rem(dp + j + 1, DP)), dp + j + 1 < DP)

    def first_id(k):
        return ids_ref[jnp.clip(k, 0, DP - 1)][0:1, 0:1]

    def final_id(k):
        return ids_ref[jnp.clip(k, 0, DP - 1)][3:4, 127:128]

    one = jnp.zeros((1, 1), jnp.int32)
    for j in range(4):
        recv(INFO_DN + j, info_rx.at[4 + j], dpid(mate), dp + j + 1 < DP)
    after = jnp.zeros((8, 128), F32)
    for j in range(4):
        goes_on = (first_id(dp + j + 1) == final_id(dp)) & (one + dp + j + 1 < DP)
        after = after + jnp.where(goes_on, info_rx[4 + j, 0:8, :], 0.0)
    carry_on = jnp.broadcast_to(jnp.exp(after)[:, 0:1], (8, TOK))
    xw_end = weighted_x(to_end * jnp.where(is_last, carry_on, 1.0))
    for g in range(PROMPTS):
        mine = jnp.where(idc[16:EXT, :] == float(g), 1.0, 0.0).astype(BF16)
        b_all[:, 128 * g : 128 * g + 128] = b_b[...] * mine
    for g in range(PROMPTS):
        loc[g] = dot(xw_end, b_all[:, 128 * g : 128 * g + 128]).astype(BF16)
    mate_half = pl.multiple_of((1 - c) * 96, 96)
    send(TAB0, loc.at[:, pl.ds(mate_half, 96), :], tab0, dpid(mate))

    scol = lax.broadcasted_iota(jnp.int32, (128, TOK), 1)
    srow = lax.broadcasted_iota(jnp.int32, (128, TOK), 0)
    for q in range(4):
        r = 128 * q
        w = r + 128
        scores = dot_t(c_b[r:w, :], b_b[0:w, :])
        ok = (jnp.broadcast_to(idc[16 + r : 16 + w, 0:1], (128, w)) == jnp.broadcast_to(id_row[:, 0:w], (128, w))) & (
            scol[:, 0:w] <= srow[:, 0:w] + r
        )
        scores = jnp.where(ok, scores, 0.0)
        parts = []
        for h in range(HEADS):
            gap = jnp.broadcast_to(cols[r:w, h : h + 1], (128, w)) - prefix[h : h + 1, 0:w]
            mix = (scores * (jnp.exp(jnp.minimum(gap, 0.0)) * step_rows[h : h + 1, 0:w])).astype(BF16)
            col = 0 if h < 2 else 128
            parts.append(dot(mix, x_b[0:w, col : col + 128]))
        low = lax.broadcasted_iota(jnp.int32, (128, 128), 1) < 64
        smask[r:w, 0:128] = jnp.where(low, parts[0], parts[1])
        smask[r:w, 128:256] = parts[2]

    my_half = pl.multiple_of(c * 96, 96)
    recv(TAB0, tab0, dpid(mate))
    for g in range(PROMPTS):
        tabs[g] = (loc[g, pl.ds(my_half, 96), :].astype(F32) + tab0[g].astype(F32)).astype(BF16)
    send(TABZ, tabs.at[pl.ds(4 - 2 * zh, 2)], tabz, dpid(across))

    wo_step(1)

    for j in range(4):
        recv(INFO_UP + j, info_rx.at[j], dpid(mate), dp >= j + 1)
        recv(STATE + j, l_rx.at[j], dpid(mate), dp >= j + 1)
    state = l_rx[3].astype(F32)
    for j in (2, 1, 0):
        joined = (final_id(dp - j - 1) == final_id(dp - j - 2)) & (one + dp - j - 2 >= 0)
        gain_j = jnp.where(joined, jnp.exp(info_rx[j, 8:16, :]), 0.0)
        rows = jnp.concatenate(
            [jnp.broadcast_to(gain_j[h : h + 1, :], (64, 128)) for h in range(HEADS)], axis=0
        )
        state = l_rx[j].astype(F32) + rows * state
    s_in[0:FEAT, :] = state.astype(BF16)
    s_in[FEAT:256, :] = jnp.zeros((64, NSTATE), BF16)

    before_id = jnp.where(one + dp > 0, final_id(dp - 1), -1).astype(F32)
    lane1 = lax.broadcasted_iota(jnp.int32, (128, 128), 1)
    low = lane1 < 64
    skip0 = jnp.where(low, skip_ref[0], skip_ref[1])
    skip1 = jnp.where(low, skip_ref[2], 0.0)
    og0 = og_ref[:, 0:128]
    og1 = jnp.concatenate([og_ref[:, 128:192], jnp.zeros((1, 64), F32)], axis=1)
    for q in range(4):
        r = 128 * q
        w = r + 128
        inter = dot_t(c_b[r:w, :], s_in[...])
        enters = jnp.where(idc[16 + r : 16 + w, :] == before_id, 1.0, 0.0)
        decay = jnp.exp(cols[r:w, :])
        e0 = jnp.broadcast_to(decay[:, 0:1], (128, 128))
        e1 = jnp.broadcast_to(decay[:, 1:2], (128, 128))
        e2 = jnp.broadcast_to(decay[:, 2:3], (128, 128))
        y0 = smask[r:w, 0:128] + enters * jnp.where(low, e0, e1) * inter[:, 0:128]
        y1 = smask[r:w, 128:256] + enters * e2 * inter[:, 128:256]
        y0 = y0 + skip0 * x_b[r:w, 0:128].astype(F32)
        y1 = y1 + skip1 * x_b[r:w, 128:256].astype(F32)
        z0 = u_buf[16 + r : 16 + w, 256:384]
        z1 = jnp.where(low, pltpu.roll(u_buf[16 + r : 16 + w, 128:256], 64, 1), 0.0)
        g0 = y0 * (z0 * jax.nn.sigmoid(z0))
        g1 = y1 * (z1 * jax.nn.sigmoid(z1))
        sq = jnp.sum(g0 * g0 + g1 * g1, axis=1, keepdims=True)
        hi = sq.astype(BF16).astype(F32)
        g_send[r:w, 0:128] = (g0 * og0).astype(BF16)
        g_send[r:w, 128:256] = jnp.where(
            low, g1 * og1, jnp.where(lane1 == 64, hi, jnp.where(lane1 == 65, sq - hi, 0.0))
        ).astype(BF16)
    for k in range(1, 4):
        zt = lax.rem(zl + k, 4)
        send(
            A2A + k - 1, g_send.at[pl.ds(pl.multiple_of(zt * 128, 128), 128), :], a_rx.at[zl],
            hdid(zt, y),
        )
    a_rx[zl] = g_send[pl.ds(pl.multiple_of(zl * 128, 128), 128), :]

    wo_step(2)
    wo_step(3)

    recv(TABZ, tabz, dpid(across))
    tabm[...] = tabs[pl.ds(4 * zh, 4)]
    mid = 2 - 2 * zh
    tabm[pl.ds(mid, 2)] = (tabs[pl.ds(4 * zh + mid, 2)].astype(F32) + tabz[...].astype(F32)).astype(BF16)
    for k in range(1, 4):
        xt = lax.rem(x + k, 4)
        send(TABX + k - 1, tabm.at[xt], tabx.at[k - 1], dpid(dev(zh, xt, c)))

    wo_finish()

    for k in range(1, 4):
        zs = lax.rem(zl + 4 - k, 4)
        recv(A2A + k - 1, a_rx.at[zs], hdid(zs, y))
    sq = jnp.zeros((128, 1), F32)
    picked = (lane1 == 64) | (lane1 == 65)
    for z_ in range(4):
        sq = sq + jnp.sum(jnp.where(picked, a_rx[z_, :, 128:256].astype(F32), 0.0), axis=1, keepdims=True)
    hi = sq.astype(BF16).astype(F32)
    tail = jnp.where(lane1 == 0, hi, jnp.where(lane1 == 1, sq - hi, 0.0))
    own_acc[:, D : D + 128] = tail
    part[:, :, D : D + 128] = tail.astype(BF16).reshape(4, 32, 128)
    for n in range(0, D, 256):
        acc = dot(a_rx[0, :, 0:FEAT], wo[0, :, n : n + 256])
        for z_ in range(1, 4):
            acc = acc + dot(a_rx[z_, :, 0:FEAT], wo[z_, :, n : n + 256])
        own_acc[:, n : n + 256] = acc
        part[:, :, n : n + 256] = acc.astype(BF16).reshape(4, 32, 256)
    for k in range(1, 4):
        yt = lax.rem(y + k, 4)
        send(RSY + k - 1, part.at[yt], rs_rx.at[k - 1], hdid(zl, yt))

    for k in range(1, 4):
        recv(TABX + k - 1, tabx.at[k - 1], dpid(mate))
    done = tabm[x].astype(F32)
    for k in range(3):
        done = done + tabx[k].astype(F32)
    fin[dp // 2, pl.ds(my_half, 96), :] = done.astype(BF16)

    def f_rows(owner):
        return fin.at[owner // 2, pl.ds(pl.multiple_of(lax.rem(owner, 2) * 96, 96), 96), :]

    finals = Gather([(F_IDS, f_rows)])
    finals.own()

    for k in range(1, 4):
        recv(RSY + k - 1, rs_rx.at[k - 1], hdid(zl, lax.rem(y + 4 - k, 4)))
    y_rows = pl.ds(pl.multiple_of(y * 32, 32), 32)
    sq = own_acc[y_rows, D : D + 128]
    for k in range(3):
        sq = sq + rs_rx[k, :, D : D + 128].astype(F32)
    scale = lax.rsqrt(jnp.sum(sq, axis=1, keepdims=True) / (FEAT * HD) + EPSILON)
    acc = own_acc[y_rows, 0:D]
    for k in range(3):
        acc = acc + rs_rx[k, :, 0:D].astype(F32)
    resid = hid_ref[pl.ds(pl.multiple_of(hd * 32, 32), 32), :].astype(F32)
    out_ref[...] = (resid + scale * acc).astype(BF16)

    finals.near()
    finals.cross()
    finals.near_rest()
    finals.far()
    for r in range(4):
        st_ref[r] = fin[req_ref[r]].astype(F32)

    for m, src, dst, to, cond in pending:
        if cond is None:
            msg(m, src, dst, to).wait_send()
        else:
            @pl.when(cond)
            def _():
                msg(m, src, dst, to).wait_send()


def on_device(
    hidden, token_prompt, request_prompt, in_gain, w_zx, w_bc, w_dt, dt_bias, a_log, conv_x,
    conv_bc, skip_gain, out_gain, w_out,
):
    vmem = pl.BlockSpec(memory_space=pltpu.VMEM)
    smem = pl.BlockSpec(memory_space=pltpu.SMEM)
    layer_out, states = pl.pallas_call(
        body,
        out_shape=(
            jax.ShapeDtypeStruct((TOK // HD, D), BF16),
            jax.ShapeDtypeStruct((4, FEAT, NSTATE), F32),
        ),
        in_specs=[vmem, smem, smem, smem, smem] + [vmem] * 9,
        out_specs=(vmem, vmem),
        scratch_shapes=[
            pltpu.VMEM((D, 640), BF16),
            pltpu.VMEM((ROWS, 640), F32),
            pltpu.VMEM((DP, 8, 128), F32),
            pltpu.VMEM((D, 128), BF16),
            pltpu.VMEM((16, D), BF16),
            pltpu.VMEM((EXT, D), BF16),
            pltpu.VMEM((EXT, 128), F32),
            pltpu.VMEM((EXT, 640), F32),
            pltpu.VMEM((8, 512), F32),
            pltpu.VMEM((FEAT, TOK), F32),
            pltpu.VMEM((TOK, 256), BF16),
            pltpu.VMEM((TOK, 128), BF16),
            pltpu.VMEM((TOK, 128), BF16),
            pltpu.VMEM((TOK, 128 * PROMPTS), BF16),
            pltpu.VMEM((16, 128), F32),
            pltpu.VMEM((8, 16, 128), F32),
            pltpu.VMEM((FEAT, NSTATE), BF16),
            pltpu.VMEM((4, FEAT, NSTATE), BF16),
            pltpu.VMEM((256, NSTATE), BF16),
            pltpu.VMEM((TOK, 128), F32),
            pltpu.VMEM((TOK, 256), F32),
            pltpu.VMEM((PROMPTS, FEAT, NSTATE), BF16),
            pltpu.VMEM((PROMPTS, 96, NSTATE), BF16),
            pltpu.VMEM((PROMPTS, 96, NSTATE), BF16),
            pltpu.VMEM((2, 96, NSTATE), BF16),
            pltpu.VMEM((4, 96, NSTATE), BF16),
            pltpu.VMEM((3, 96, NSTATE), BF16),
            pltpu.VMEM((PROMPTS, FEAT, NSTATE), BF16),
            pltpu.VMEM((TOK, 256), BF16),
            pltpu.VMEM((4, 128, 256), BF16),
            pltpu.VMEM((4, FEAT, D), BF16),
            pltpu.VMEM((4, 32, OUTW), BF16),
            pltpu.VMEM((128, OUTW), F32),
            pltpu.VMEM((3, 32, OUTW), BF16),
            pltpu.SemaphoreType.DMA((N_MSG,)),
            pltpu.SemaphoreType.DMA((N_MSG,)),
            pltpu.SemaphoreType.DMA,
        ],
        compiler_params=pltpu.CompilerParams(
            collective_id=0, has_side_effects=True, vmem_limit_bytes=60 * 2**20
        ),
        name="layer",
    )(
        token_prompt.reshape(DP, 4, 128), request_prompt, dt_bias, a_log, skip_gain, hidden,
        in_gain.reshape(1, D), w_zx, w_bc, w_dt, conv_x, conv_bc, out_gain.reshape(1, FEAT), w_out,
    )
    return layer_out, states.reshape(4, HEADS, 64, NSTATE)


def solution(mesh):
    in_specs = (
        P("dp", None), P(), P("dp"), P(), P("dp", None, "head"), P("dp", None), P("dp", "head"),
        P("head"), P("head"), P(None, "head"), P(), P("head"), P("head"), P("head", None),
    )
    out_specs = (P(("dp", "head"), None), P("dp", "head", None, None))
    return jax.shard_map(on_device, mesh=mesh, in_specs=in_specs, out_specs=out_specs, check_vma=False)
```

```python
import jax
import jax.numpy as jnp
from jax import lax
from jax.experimental import pallas as pl
from jax.experimental.pallas import tpu as pltpu
from jax.sharding import PartitionSpec as P

MESH = pl.DeviceIdType.MESH
F32 = jnp.float32
BF16 = jnp.bfloat16
EPSILON = 1e-05

DP = 16
HD = 16
D = 1536
TOK = 512
EXT = TOK + 16
ROWS = 96
HEADS = 3
FEAT = 192
NSTATE = 128
PROMPTS = 8
OUTW = D + 128

W_IDS = 0
T_IDS = 15
F_IDS = 30
HALO = 45
INFO_UP = 46
INFO_DN = 50
STATE = 54
WO = 58
WO_MATE = 61
TAB0 = 64
TABZ = 65
TABX = 66
A2A = 69
RSZ = 72
N_MSG = 75


def dot(a, b):
    return lax.dot_general(a, b, (((1,), (0,)), ((), ())), preferred_element_type=F32)


def dot_t(a, b):
    return lax.dot_general(a, b, (((1,), (1,)), ((), ())), preferred_element_type=F32)


def lane_cumsum(v):
    width = v.shape[1]
    lane = lax.broadcasted_iota(jnp.int32, v.shape, 1)
    step = 1
    while step < width:
        v = v + jnp.where(lane >= step, pltpu.roll(v, step, 1), 0.0)
        step *= 2
    return v


def run_end(v, ids):
    width = v.shape[1]
    lane = lax.broadcasted_iota(jnp.int32, v.shape, 1)
    step = 1
    while step < width:
        same = (pltpu.roll(ids, width - step, 1) == ids) & (lane < width - step)
        v = jnp.where(same, pltpu.roll(v, width - step, 1), v)
        step *= 2
    return v


SCOPE = []


def phase(name):
    if SCOPE:
        SCOPE.pop().__exit__(None, None, None)
    if name and TRACE:
        SCOPE.append(jax.named_scope(name))
        SCOPE[-1].__enter__()


TRACE = False


def body(
    ids_ref, req_ref, dtb_ref, alog_ref, skip_ref, hid_ref, gain_ref, wzx_ref, wbc_ref,
    wdt_ref, cx_ref, cbc_ref, og_ref, wout_ref, out_ref, st_ref,
    w_buf, wst, wdt_all, wdt_mat, halo, nrm, idc, u_buf, taps, x_t, x_b, b_b, c_b, b_all,
    info_tx, info_rx, l_tx, l_rx, s_in, cols, smask, loc, tab0, tabs, tabz, tabm, tabx, fin,
    g_send, a_rx, wo, part, own_acc, rs_rx, send_sem, recv_sem, local_sem,
):
    dp = lax.axis_index("dp")
    hd = lax.axis_index("head")
    zh = dp // 8
    x = (dp // 2) % 4
    c = dp % 2
    zl = hd // 4
    y = hd % 4
    sgn = 1 - 2 * c

    def dev(z_, x_, c_):
        return z_ * 8 + lax.rem(x_ + 8, 4) * 2 + c_

    ahead = dev(zh, x + sgn, c)
    behind = dev(zh, x - sgn, c)
    across = dev(1 - zh, x, c)
    mate = dev(zh, x, 1 - c)

    def dpid(d):
        return {"dp": d}

    def hdid(z_, y_):
        return {"head": z_ * 4 + y_}

    def msg(m, src, dst, to):
        return pltpu.make_async_remote_copy(
            src_ref=src, dst_ref=dst, send_sem=send_sem.at[m], recv_sem=recv_sem.at[m],
            device_id=to, device_id_type=MESH,
        )

    pending = []

    def send(m, src, dst, to, cond=None):
        if cond is None:
            msg(m, src, dst, to).start()
        else:
            @pl.when(cond)
            def _():
                msg(m, src, dst, to).start()
        pending.append((m, src, dst, to, cond))

    def recv(m, dst, to, cond=None):
        if cond is None:
            msg(m, dst, dst, to).wait_recv()
        else:
            @pl.when(cond)
            def _():
                msg(m, dst, dst, to).wait_recv()

    class Gather:
        def __init__(self, families):
            self.families = families

        def send(self, k, owner, to):
            for base, ref_of in self.families:
                r = ref_of(owner)
                send(base + k, r, r, dpid(to))

        def recv(self, k, owner):
            for base, ref_of in self.families:
                recv(base + k, ref_of(owner), dpid(mate))

        def own(self):
            self.send(3, dp, across)
            self.send(0, dp, ahead)
            self.send(1, dp, behind)
            self.send(7, dp, mate)

        def near(self):
            self.recv(0, dev(zh, x - sgn, c))
            self.send(2, dev(zh, x - sgn, c), ahead)
            self.send(8, dev(zh, x - sgn, c), mate)
            self.recv(1, dev(zh, x + sgn, c))
            self.send(9, dev(zh, x + sgn, c), mate)

        def cross(self):
            self.recv(3, dev(1 - zh, x, c))
            self.send(4, dev(1 - zh, x, c), ahead)
            self.send(5, dev(1 - zh, x, c), behind)
            self.send(11, dev(1 - zh, x, c), mate)

        def near_rest(self):
            self.recv(2, dev(zh, x + 2, c))
            self.send(10, dev(zh, x + 2, c), mate)
            self.recv(7, dev(zh, x, 1 - c))
            self.recv(8, dev(zh, x + sgn, 1 - c))
            self.recv(9, dev(zh, x - sgn, 1 - c))
            self.recv(10, dev(zh, x + 2, 1 - c))

        def far(self):
            o = 1 - zh
            self.recv(4, dev(o, x - sgn, c))
            self.send(6, dev(o, x - sgn, c), ahead)
            self.send(12, dev(o, x - sgn, c), mate)
            self.recv(5, dev(o, x + sgn, c))
            self.send(13, dev(o, x + sgn, c), mate)
            self.recv(6, dev(o, x + 2, c))
            self.send(14, dev(o, x + 2, c), mate)
            self.recv(11, dev(o, x, 1 - c))
            self.recv(12, dev(o, x + sgn, 1 - c))
            self.recv(13, dev(o, x - sgn, 1 - c))
            self.recv(14, dev(o, x + 2, 1 - c))

    phase("entry")
    barrier = pltpu.get_barrier_semaphore()
    for k in range(1, DP):
        pl.semaphore_signal(
            barrier, inc=1, device_id=dpid(lax.rem(dp + k, DP)), device_id_type=MESH
        )
    for k in range(1, 4):
        pl.semaphore_signal(
            barrier, inc=1, device_id=hdid(zl, lax.rem(y + k, 4)), device_id_type=MESH
        )
        pl.semaphore_signal(
            barrier, inc=1, device_id=hdid(lax.rem(zl + k, 4), y), device_id_type=MESH
        )

    zw = wzx_ref[:, 0, :]
    xw = wzx_ref[:, 1, :]
    wst[:, 0:128] = xw[:, 0:128]
    wst[:, 128:256] = jnp.concatenate([xw[:, 128:192], zw[:, 128:192]], axis=1)
    wst[:, 256:384] = zw[:, 0:128]
    wst[:, 384:640] = wbc_ref[...]
    own_rows = pl.multiple_of(dp * ROWS, ROWS)
    w_buf[pl.ds(own_rows, ROWS), :] = wst[...].astype(BF16)
    wdt_all[dp] = jnp.zeros((8, 128), F32)
    wdt_all[dp, 0:HEADS, 0:ROWS] = wdt_ref[...]

    def w_rows(owner):
        return w_buf.at[pl.ds(pl.multiple_of(owner * ROWS, ROWS), ROWS), :]

    def t_rows(owner):
        return wdt_all.at[owner]

    weights = Gather([(W_IDS, w_rows), (T_IDS, t_rows)])
    own_copy = pltpu.make_async_copy(wout_ref, wo.at[y], local_sem)
    own_copy.start()

    @pl.when(dp == 0)
    def _():
        halo[...] = jnp.zeros_like(halo)

    for j in range(4):
        @pl.when(dp < j + 1)
        def _():
            info_rx[j] = jnp.zeros((16, 128), F32)
            l_rx[j] = jnp.zeros((FEAT, NSTATE), BF16)

        @pl.when(dp + j + 1 > DP - 1)
        def _():
            info_rx[4 + j] = jnp.zeros((16, 128), F32)

    pl.semaphore_wait(barrier, DP - 1 + 6)

    weights.own()
    send(HALO, hid_ref.at[pl.ds(TOK - 16, 16), :], halo, dpid(lax.rem(dp + 1, DP)), dp < DP - 1)

    phase("ids")
    def wo_rows(y_, c_):
        return wo.at[lax.rem(y_ + 4, 4), pl.ds(pl.multiple_of(c_ * 96, 96), 96), :]

    own_copy.wait()
    for k in (1, 3, 2):
        send(WO + k - 1, wo_rows(y, c), wo_rows(y, c), hdid(zl, lax.rem(y + k, 4)))

    own_ids = ids_ref[dp].astype(F32)
    prev_ids = ids_ref[jnp.maximum(dp - 1, 0)].astype(F32)
    prev_col = jnp.broadcast_to(prev_ids[3:4, :], (128, 128)).T[112:128, :]
    first_dev = jnp.zeros((16, 128), jnp.int32) + dp == 0
    idc[0:16, :] = jnp.where(first_dev, -1.0, prev_col)
    for q in range(4):
        idc[16 + 128 * q : 144 + 128 * q, :] = jnp.broadcast_to(own_ids[q : q + 1, :], (128, 128)).T
    id_row = jnp.concatenate([own_ids[q : q + 1, :] for q in range(4)], axis=1)

    taps[...] = jnp.zeros_like(taps)
    taps[0:4, 0:128] = cx_ref[:, 0:128]
    taps[0:4, 128:192] = cx_ref[:, 128:192]
    taps[0:4, 256:512] = cbc_ref[...]

    phase("norm")
    gain = gain_ref[...].reshape(1, D)

    def norm_rows(rows):
        h = rows.astype(F32)
        scale = lax.rsqrt(jnp.mean(h * h, axis=1, keepdims=True) + EPSILON)
        return (h * scale * gain).astype(BF16)

    def norm_step(i, carry):
        r = pl.multiple_of(i * 32, 32)
        nrm[pl.ds(pl.multiple_of(16 + r, 16), 32), :] = norm_rows(hid_ref[pl.ds(r, 32), :])
        return carry

    lax.fori_loop(0, TOK // 32, norm_step, 0)
    phase("halo_wait")
    recv(HALO, halo, dpid(mate), dp > 0)
    nrm[0:16, :] = norm_rows(halo[...])

    phase("w_near")
    weights.near()
    phase("w_cross")
    weights.cross()
    phase("w_near_rest")
    weights.near_rest()

    phase("mm1")
    k_half = D // 2
    k_own = pl.multiple_of(zh * k_half, k_half)
    k_far = pl.multiple_of((1 - zh) * k_half, k_half)
    for n in range(0, 640, 128):
        u_buf[:, n : n + 128] = dot(nrm[:, pl.ds(k_own, k_half)], w_buf[pl.ds(k_own, k_half), n : n + 128])

    phase("w_far")
    weights.far()

    phase("dt")
    for j in range(DP):
        rows = jnp.concatenate([wdt_all[j], jnp.zeros((120, 128), F32)], axis=0).T
        wdt_mat[ROWS * j : ROWS * j + ROWS, :] = rows[0:ROWS, :].astype(BF16)
    dt_cols = dot(nrm[16:EXT, :], wdt_mat[...])
    dt_rows = dt_cols.T[0:8, :].astype(BF16).astype(F32)
    sub = lax.broadcasted_iota(jnp.int32, (8, TOK), 0)
    lane = lax.broadcasted_iota(jnp.int32, (8, TOK), 1)

    def by_head(ref, s):
        return jnp.where(s == 0, ref[0], jnp.where(s == 1, ref[1], ref[2]))

    pre = dt_rows + by_head(dtb_ref, sub)
    step_rows = jnp.maximum(pre, 0.0) + jnp.log1p(jnp.exp(-jnp.abs(pre)))
    rate_rows = -step_rows * jnp.exp(by_head(alog_ref, sub))
    prefix = lane_cumsum(rate_rows)
    id8 = jnp.broadcast_to(id_row, (8, TOK))
    at_end = run_end(prefix, id8)
    first_end = at_end[:, 0:1]
    total = prefix[:, TOK - 1 : TOK]
    info_tx[0:8, :] = jnp.broadcast_to(first_end, (8, 128))
    info_tx[8:16, :] = jnp.broadcast_to(total, (8, 128))
    for j in range(4):
        send(INFO_UP + j, info_tx, info_rx.at[j], dpid(lax.rem(dp + j + 1, DP)), dp + j + 1 < DP)
        send(INFO_DN + j, info_tx, info_rx.at[4 + j], dpid(lax.rem(dp - j - 1 + DP, DP)), dp >= j + 1)

    to_end = jnp.exp(at_end - prefix) * step_rows
    cols[...] = jnp.concatenate([prefix, jnp.zeros((120, TOK), F32)], axis=0).T

    phase("mm2")
    for n in range(0, 640, 128):
        u_buf[:, n : n + 128] += dot(nrm[:, pl.ds(k_far, k_half)], w_buf[pl.ds(k_far, k_half), n : n + 128])

    phase("conv")
    for r in range(0, EXT, 176):
        u_buf[r : r + 176, :] = u_buf[r : r + 176, :].astype(BF16).astype(F32)

    for q in range(4):
        r = 128 * q
        now = idc[16 + r : 144 + r, :]
        same = [jnp.where(idc[13 + k + r : 141 + k + r, :] == now, 1.0, 0.0) for k in range(3)]

        def conv(col, tap):
            acc = taps[3:4, tap : tap + 128] * u_buf[16 + r : 144 + r, col : col + 128]
            for k in range(3):
                acc = acc + same[k] * (
                    taps[k : k + 1, tap : tap + 128] * u_buf[13 + k + r : 141 + k + r, col : col + 128]
                )
            return (acc * jax.nn.sigmoid(acc)).astype(BF16)

        x0 = conv(0, 0)
        x1 = conv(128, 128)
        x_b[r : r + 128, 0:128] = x0
        x_b[r : r + 128, 128:256] = x1
        x_t[0:128, r : r + 128] = x0.astype(F32).T
        x_t[128:192, r : r + 128] = x1.astype(F32).T[0:64, :]
        b_b[r : r + 128, :] = conv(384, 256)
        c_b[r : r + 128, :] = conv(512, 384)

    phase("lstate")
    last_id = id_row[:, TOK - 1 : TOK]
    is_last = id8 == jnp.broadcast_to(last_id, (8, TOK))

    def weighted_x(weight):
        return jnp.concatenate(
            [x_t[64 * h : 64 * h + 64, :] * weight[h : h + 1, :] for h in range(HEADS)], axis=0
        ).astype(BF16)

    l_tx[...] = dot(weighted_x(jnp.where(is_last, to_end, 0.0)), b_b[...]).astype(BF16)
    for j in range(4):
        send(STATE + j, l_tx, l_rx.at[j], dpid(lax.rem(dp + j + 1, DP)), dp + j + 1 < DP)

    phase("table_loc")
    def first_id(k):
        return ids_ref[jnp.clip(k, 0, DP - 1)][0:1, 0:1]

    def final_id(k):
        return ids_ref[jnp.clip(k, 0, DP - 1)][3:4, 127:128]

    one = jnp.zeros((1, 1), jnp.int32)
    for j in range(4):
        recv(INFO_DN + j, info_rx.at[4 + j], dpid(mate), dp + j + 1 < DP)
    after = jnp.zeros((8, 128), F32)
    for j in range(4):
        goes_on = (first_id(dp + j + 1) == final_id(dp)) & (one + dp + j + 1 < DP)
        after = after + jnp.where(goes_on, info_rx[4 + j, 0:8, :], 0.0)
    carry_on = jnp.broadcast_to(jnp.exp(after)[:, 0:1], (8, TOK))
    xw_end = weighted_x(to_end * jnp.where(is_last, carry_on, 1.0))
    for g in range(PROMPTS):
        mine = jnp.where(idc[16:EXT, :] == float(g), 1.0, 0.0).astype(BF16)
        b_all[:, 128 * g : 128 * g + 128] = b_b[...] * mine
    for g in range(PROMPTS):
        loc[g] = dot(xw_end, b_all[:, 128 * g : 128 * g + 128]).astype(BF16)
    mate_half = pl.multiple_of((1 - c) * 96, 96)
    send(TAB0, loc.at[:, pl.ds(mate_half, 96), :], tab0, dpid(mate))

    phase("wo_mate")
    for k in (1, 3, 2):
        recv(WO + k - 1, wo_rows(y - k, c), dpid(mate))
        send(WO_MATE + k - 1, wo_rows(y - k, c), wo_rows(y - k, c), dpid(mate))
    phase("scores")
    scol = lax.broadcasted_iota(jnp.int32, (128, TOK), 1)
    srow = lax.broadcasted_iota(jnp.int32, (128, TOK), 0)
    for q in range(4):
        r = 128 * q
        w = r + 128
        scores = dot_t(c_b[r:w, :], b_b[0:w, :])
        ok = (jnp.broadcast_to(idc[16 + r : 16 + w, 0:1], (128, w)) == jnp.broadcast_to(id_row[:, 0:w], (128, w))) & (
            scol[:, 0:w] <= srow[:, 0:w] + r
        )
        scores = jnp.where(ok, scores, 0.0)
        parts = []
        for h in range(HEADS):
            gap = jnp.broadcast_to(cols[r:w, h : h + 1], (128, w)) - prefix[h : h + 1, 0:w]
            mix = (scores * (jnp.exp(jnp.minimum(gap, 0.0)) * step_rows[h : h + 1, 0:w])).astype(BF16)
            col = 0 if h < 2 else 128
            parts.append(dot(mix, x_b[0:w, col : col + 128]))
        low = lax.broadcasted_iota(jnp.int32, (128, 128), 1) < 64
        smask[r:w, 0:128] = jnp.where(low, parts[0], parts[1])
        smask[r:w, 128:256] = parts[2]

    phase("tab0_wait")
    my_half = pl.multiple_of(c * 96, 96)
    recv(TAB0, tab0, dpid(mate))
    for g in range(PROMPTS):
        tabs[g] = (loc[g, pl.ds(my_half, 96), :].astype(F32) + tab0[g].astype(F32)).astype(BF16)
    send(TABZ, tabs.at[pl.ds(4 - 2 * zh, 2)], tabz, dpid(across))

    phase("state_wait")
    for j in range(4):
        recv(INFO_UP + j, info_rx.at[j], dpid(mate), dp >= j + 1)
        recv(STATE + j, l_rx.at[j], dpid(mate), dp >= j + 1)
    state = l_rx[3].astype(F32)
    for j in (2, 1, 0):
        joined = (final_id(dp - j - 1) == final_id(dp - j - 2)) & (one + dp - j - 2 >= 0)
        gain_j = jnp.where(joined, jnp.exp(info_rx[j, 8:16, :]), 0.0)
        rows = jnp.concatenate(
            [jnp.broadcast_to(gain_j[h : h + 1, :], (64, 128)) for h in range(HEADS)], axis=0
        )
        state = l_rx[j].astype(F32) + rows * state
    s_in[0:FEAT, :] = state.astype(BF16)
    s_in[FEAT:256, :] = jnp.zeros((64, NSTATE), BF16)

    phase("yinter")
    before_id = jnp.where(one + dp > 0, final_id(dp - 1), -1).astype(F32)
    lane1 = lax.broadcasted_iota(jnp.int32, (128, 128), 1)
    low = lane1 < 64
    skip0 = jnp.where(low, skip_ref[0], skip_ref[1])
    skip1 = jnp.where(low, skip_ref[2], 0.0)
    og0 = og_ref[:, 0:128]
    og1 = jnp.concatenate([og_ref[:, 128:192], jnp.zeros((1, 64), F32)], axis=1)
    for q in range(4):
        r = 128 * q
        w = r + 128
        inter = dot_t(c_b[r:w, :], s_in[...])
        enters = jnp.where(idc[16 + r : 16 + w, :] == before_id, 1.0, 0.0)
        decay = jnp.exp(cols[r:w, :])
        e0 = jnp.broadcast_to(decay[:, 0:1], (128, 128))
        e1 = jnp.broadcast_to(decay[:, 1:2], (128, 128))
        e2 = jnp.broadcast_to(decay[:, 2:3], (128, 128))
        y0 = smask[r:w, 0:128] + enters * jnp.where(low, e0, e1) * inter[:, 0:128]
        y1 = smask[r:w, 128:256] + enters * e2 * inter[:, 128:256]
        y0 = y0 + skip0 * x_b[r:w, 0:128].astype(F32)
        y1 = y1 + skip1 * x_b[r:w, 128:256].astype(F32)
        z0 = u_buf[16 + r : 16 + w, 256:384]
        z1 = jnp.where(low, pltpu.roll(u_buf[16 + r : 16 + w, 128:256], 64, 1), 0.0)
        g0 = y0 * (z0 * jax.nn.sigmoid(z0))
        g1 = y1 * (z1 * jax.nn.sigmoid(z1))
        sq = jnp.sum(g0 * g0 + g1 * g1, axis=1, keepdims=True)
        hi = sq.astype(BF16).astype(F32)
        g_send[q, :, :, 0:128] = (g0 * og0).astype(BF16).reshape(4, 32, 128)
        g_send[q, :, :, 128:256] = jnp.where(
            low, g1 * og1, jnp.where(lane1 == 64, hi, jnp.where(lane1 == 65, sq - hi, 0.0))
        ).astype(BF16).reshape(4, 32, 128)
    for k in (2, 1, 3):
        yt = lax.rem(y + k, 4)
        send(A2A + k - 1, g_send.at[:, yt], a_rx.at[y], hdid(zl, yt))
    a_rx[y] = g_send[:, y]

    phase("tabz_wait")
    recv(TABZ, tabz, dpid(across))
    tabm[...] = tabs[pl.ds(4 * zh, 4)]
    mid = 2 - 2 * zh
    tabm[pl.ds(mid, 2)] = (tabs[pl.ds(4 * zh + mid, 2)].astype(F32) + tabz[...].astype(F32)).astype(BF16)
    for k in range(1, 4):
        xt = lax.rem(x + k, 4)
        send(TABX + k - 1, tabm.at[xt], tabx.at[k - 1], dpid(dev(zh, xt, c)))

    phase("wo_finish")
    for k in (1, 3, 2):
        recv(WO_MATE + k - 1, wo_rows(y - k, 1 - c), dpid(mate))

    phase("a2a_wait")
    for k in range(1, 4):
        ys = lax.rem(y + 4 - k, 4)
        recv(A2A + k - 1, a_rx.at[ys], hdid(zl, ys))
    phase("outproj")
    sq = jnp.zeros((128, 1), F32)
    picked = (lane1 == 64) | (lane1 == 65)
    for y_ in range(4):
        tails = a_rx[y_, :, :, 128:256].reshape(128, 128).astype(F32)
        sq = sq + jnp.sum(jnp.where(picked, tails, 0.0), axis=1, keepdims=True)
    hi = sq.astype(BF16).astype(F32)
    tail = jnp.where(lane1 == 0, hi, jnp.where(lane1 == 1, sq - hi, 0.0))
    own_acc[:, D : D + 128] = tail
    part[:, :, D : D + 128] = tail.astype(BF16).reshape(4, 32, 128)
    for n in range(0, D, 256):
        acc = jnp.zeros((128, 256), F32)
        for y_ in range(4):
            acc = acc + dot(a_rx[y_, :, :, 0:FEAT].reshape(128, FEAT), wo[y_, :, n : n + 256])
        own_acc[:, n : n + 256] = acc
        part[:, :, n : n + 256] = acc.astype(BF16).reshape(4, 32, 256)
    for k in (2, 1, 3):
        zt = lax.rem(zl + k, 4)
        send(RSZ + k - 1, part.at[zt], rs_rx.at[k - 1], hdid(zt, y))

    phase("tabx_wait")
    for k in range(1, 4):
        recv(TABX + k - 1, tabx.at[k - 1], dpid(mate))
    done = tabm[x].astype(F32)
    for k in range(3):
        done = done + tabx[k].astype(F32)
    fin[dp // 2, pl.ds(my_half, 96), :] = done.astype(BF16)

    def f_rows(owner):
        return fin.at[owner // 2, pl.ds(pl.multiple_of(lax.rem(owner, 2) * 96, 96), 96), :]

    phase("fin_own")
    finals = Gather([(F_IDS, f_rows)])
    finals.own()

    phase("fin_near")
    finals.near()
    phase("fin_cross")
    finals.cross()
    phase("fin_nearrest")
    finals.near_rest()
    phase("fin_far")
    finals.far()
    phase("rsy_wait")
    for k in range(1, 4):
        recv(RSZ + k - 1, rs_rx.at[k - 1], hdid(lax.rem(zl + 4 - k, 4), y))
    phase("out")
    z_rows = pl.ds(pl.multiple_of(zl * 32, 32), 32)
    sq = own_acc[z_rows, D : D + 128]
    for k in range(3):
        sq = sq + rs_rx[k, :, D : D + 128].astype(F32)
    scale = lax.rsqrt(jnp.sum(sq, axis=1, keepdims=True) / (FEAT * HD) + EPSILON)
    acc = own_acc[z_rows, 0:D]
    for k in range(3):
        acc = acc + rs_rx[k, :, 0:D].astype(F32)
    resid = hid_ref[pl.ds(pl.multiple_of(hd * 32, 32), 32), :].astype(F32)
    out_ref[...] = (resid + scale * acc).astype(BF16)

    phase("st_out")
    for r in range(4):
        st_ref[r] = fin[req_ref[r]]

    phase("drain")
    for m, src, dst, to, cond in pending:
        if cond is None:
            msg(m, src, dst, to).wait_send()
        else:
            @pl.when(cond)
            def _():
                msg(m, src, dst, to).wait_send()
    phase(None)


def write_out(rows_ref, states_ref, out_ref, st_ref):
    out_ref[...] = rows_ref[...]
    st_ref[...] = states_ref[...].astype(F32)


def on_device(
    hidden, token_prompt, request_prompt, in_gain, w_zx, w_bc, w_dt, dt_bias, a_log, conv_x,
    conv_bc, skip_gain, out_gain, w_out,
):
    vmem = pl.BlockSpec(memory_space=pltpu.VMEM)
    smem = pl.BlockSpec(memory_space=pltpu.SMEM)
    layer_out, states = pl.pallas_call(
        body,
        out_shape=(
            jax.ShapeDtypeStruct((TOK // HD, D), BF16),
            jax.ShapeDtypeStruct((4, FEAT, NSTATE), BF16),
        ),
        in_specs=[vmem, smem, smem, smem, smem] + [vmem] * 9,
        out_specs=(vmem, vmem),
        scratch_shapes=[
            pltpu.VMEM((D, 640), BF16),
            pltpu.VMEM((ROWS, 640), F32),
            pltpu.VMEM((DP, 8, 128), F32),
            pltpu.VMEM((D, 128), BF16),
            pltpu.VMEM((16, D), BF16),
            pltpu.VMEM((EXT, D), BF16),
            pltpu.VMEM((EXT, 128), F32),
            pltpu.VMEM((EXT, 640), F32),
            pltpu.VMEM((8, 512), F32),
            pltpu.VMEM((FEAT, TOK), F32),
            pltpu.VMEM((TOK, 256), BF16),
            pltpu.VMEM((TOK, 128), BF16),
            pltpu.VMEM((TOK, 128), BF16),
            pltpu.VMEM((TOK, 128 * PROMPTS), BF16),
            pltpu.VMEM((16, 128), F32),
            pltpu.VMEM((8, 16, 128), F32),
            pltpu.VMEM((FEAT, NSTATE), BF16),
            pltpu.VMEM((4, FEAT, NSTATE), BF16),
            pltpu.VMEM((256, NSTATE), BF16),
            pltpu.VMEM((TOK, 128), F32),
            pltpu.VMEM((TOK, 256), F32),
            pltpu.VMEM((PROMPTS, FEAT, NSTATE), BF16),
            pltpu.VMEM((PROMPTS, 96, NSTATE), BF16),
            pltpu.VMEM((PROMPTS, 96, NSTATE), BF16),
            pltpu.VMEM((2, 96, NSTATE), BF16),
            pltpu.VMEM((4, 96, NSTATE), BF16),
            pltpu.VMEM((3, 96, NSTATE), BF16),
            pltpu.VMEM((PROMPTS, FEAT, NSTATE), BF16),
            pltpu.VMEM((4, 4, 32, 256), BF16),
            pltpu.VMEM((4, 4, 32, 256), BF16),
            pltpu.VMEM((4, FEAT, D), BF16),
            pltpu.VMEM((4, 32, OUTW), BF16),
            pltpu.VMEM((128, OUTW), F32),
            pltpu.VMEM((3, 32, OUTW), BF16),
            pltpu.SemaphoreType.DMA((N_MSG,)),
            pltpu.SemaphoreType.DMA((N_MSG,)),
            pltpu.SemaphoreType.DMA,
        ],
        compiler_params=pltpu.CompilerParams(
            collective_id=0, has_side_effects=True, vmem_limit_bytes=60 * 2**20
        ),
        name="layer",
    )(
        token_prompt.reshape(DP, 4, 128), request_prompt, dt_bias, a_log, skip_gain, hidden,
        in_gain, w_zx, w_bc, w_dt.T, conv_x, conv_bc, out_gain.reshape(1, FEAT), w_out,
    )
    layer_out, states = pl.pallas_call(
        write_out,
        out_shape=(
            jax.ShapeDtypeStruct((TOK // HD, D), BF16),
            jax.ShapeDtypeStruct((4, FEAT, NSTATE), F32),
        ),
        in_specs=[vmem, vmem],
        out_specs=(vmem, vmem),
        name="write_out",
    )(layer_out, states)
    return layer_out, states.reshape(4, HEADS, 64, NSTATE)


def solution(mesh):
    in_specs = (
        P("dp", None), P(), P("dp"), P(), P("dp", None, "head"), P("dp", None), P("dp", "head"),
        P("head"), P("head"), P(None, "head"), P(), P("head"), P("head"), P("head", None),
    )
    out_specs = (P(("dp", "head"), None), P("dp", "head", None, None))
    return jax.shard_map(on_device, mesh=mesh, in_specs=in_specs, out_specs=out_specs, check_vma=False)
```

```python
import jax
import jax.numpy as jnp
from jax import lax
from jax.experimental import pallas as pl
from jax.experimental.pallas import tpu as pltpu
from jax.sharding import PartitionSpec as P

MESH = pl.DeviceIdType.MESH
F32 = jnp.float32
BF16 = jnp.bfloat16
EPSILON = 1e-05

DP = 16
HD = 16
D = 1536
TOK = 512
EXT = TOK + 16
ROWS = 96
HEADS = 3
FEAT = 192
NSTATE = 128
PROMPTS = 8
OUTW = D + 128

W_IDS = 0
T_IDS = 15
F_IDS = 30
HALO = 45
INFO_UP = 46
INFO_DN = 50
STATE = 54
WO = 58
WO_MATE = 61
TAB0 = 64
TABZ = 65
TABX = 66
A2A = 69
RSZ = 72
BCZ = 75
BCY = 78
N_MSG = 81


def dot(a, b):
    return lax.dot_general(a, b, (((1,), (0,)), ((), ())), preferred_element_type=F32)


def dot_t(a, b):
    return lax.dot_general(a, b, (((1,), (1,)), ((), ())), preferred_element_type=F32)


def lane_cumsum(v):
    width = v.shape[1]
    lane = lax.broadcasted_iota(jnp.int32, v.shape, 1)
    step = 1
    while step < width:
        v = v + jnp.where(lane >= step, pltpu.roll(v, step, 1), 0.0)
        step *= 2
    return v


def run_end(v, ids):
    width = v.shape[1]
    lane = lax.broadcasted_iota(jnp.int32, v.shape, 1)
    step = 1
    while step < width:
        same = (pltpu.roll(ids, width - step, 1) == ids) & (lane < width - step)
        v = jnp.where(same, pltpu.roll(v, width - step, 1), v)
        step *= 2
    return v


SCOPE = []


def phase(name):
    if SCOPE:
        SCOPE.pop().__exit__(None, None, None)
    if name and TRACE:
        SCOPE.append(jax.named_scope(name))
        SCOPE[-1].__enter__()


TRACE = False


def body(
    req_ref, dtb_ref, alog_ref, skip_ref, wzx_in, wbc_in, wdt_in, ids_in, hid_in, gain_in,
    cx_in, cbc_in, og_in, wout_in, out_ref, st_ref,
    wzx_ref, wbc_ref, wdt_ref, ids_ref, hid_ref, gain_ref, cx_ref, cbc_ref, og_ref,
    w_buf, wst, bc_t, sm_t, small, wdt_mat, bc_parts, halo, nrm, idc, u_buf, taps, x_t, x_b, b_b, c_b, b_all,
    info_tx, info_rx, l_tx, l_rx, s_in, cols, smask, loc, tab0, tabs, tabz, tabm, tabx, fin,
    g_send, a_rx, wo, part, own_acc, rs_rx, send_sem, recv_sem, local_sem,
):
    dp = lax.axis_index("dp")
    hd = lax.axis_index("head")
    zh = dp // 8
    x = (dp // 2) % 4
    c = dp % 2
    zl = hd // 4
    y = hd % 4

    def dev(z_, x_, c_):
        return z_ * 8 + lax.rem(x_ + 8, 4) * 2 + c_

    across = dev(1 - zh, x, c)
    mate = dev(zh, x, 1 - c)

    def dpid(d):
        return {"dp": d}

    def hdid(z_, y_):
        return {"head": z_ * 4 + y_}

    def msg(m, src, dst, to):
        return pltpu.make_async_remote_copy(
            src_ref=src, dst_ref=dst, send_sem=send_sem.at[m], recv_sem=recv_sem.at[m],
            device_id=to, device_id_type=MESH,
        )

    pending = []

    def send(m, src, dst, to, cond=None):
        if cond is None:
            msg(m, src, dst, to).start()
        else:
            @pl.when(cond)
            def _():
                msg(m, src, dst, to).start()
        pending.append((m, src, dst, to, cond))

    def recv(m, dst, to, cond=None):
        if cond is None:
            msg(m, dst, dst, to).wait_recv()
        else:
            @pl.when(cond)
            def _():
                msg(m, dst, dst, to).wait_recv()

    class Gather:
        def __init__(self, families):
            self.families = families

        def send(self, k, owner, to):
            for base, ref_of in self.families:
                r = ref_of(owner)
                send(base + k, r, r, dpid(to))

        def recv(self, k, owner):
            for base, ref_of in self.families:
                recv(base + k, ref_of(owner), dpid(mate))

        def own(self):
            self.send(3, dp, across)
            self.send(2, dp, dev(zh, x + 2, c))
            self.send(0, dp, dev(zh, x + 1, c))
            self.send(1, dp, dev(zh, x - 1, c))
            self.send(7, dp, mate)

        def cross(self):
            o = 1 - zh
            self.recv(3, dev(o, x, c))
            self.send(6, dev(o, x, c), dev(zh, x + 2, c))
            self.send(4, dev(o, x, c), dev(zh, x + 1, c))
            self.send(5, dev(o, x, c), dev(zh, x - 1, c))
            self.send(11, dev(o, x, c), mate)

        def near(self):
            for k, step in ((0, -1), (1, 1), (2, 2)):
                self.recv(k, dev(zh, x + step, c))
                self.send(8 + k, dev(zh, x + step, c), mate)

        def near_rest(self):
            for k, step in ((7, 0), (8, -1), (9, 1), (10, 2)):
                self.recv(k, dev(zh, x + step, 1 - c))

        def far(self):
            o = 1 - zh
            for k, step in ((4, -1), (5, 1), (6, 2)):
                self.recv(k, dev(o, x + step, c))
                self.send(8 + k, dev(o, x + step, c), mate)
            for k, step in ((11, 0), (12, -1), (13, 1), (14, 2)):
                self.recv(k, dev(o, x + step, 1 - c))

    phase("entry")
    barrier = pltpu.get_barrier_semaphore()
    for k in range(1, DP):
        pl.semaphore_signal(
            barrier, inc=1, device_id=dpid(lax.rem(dp + k, DP)), device_id_type=MESH
        )
    for k in range(1, 4):
        pl.semaphore_signal(
            barrier, inc=1, device_id=hdid(zl, lax.rem(y + k, 4)), device_id_type=MESH
        )
        pl.semaphore_signal(
            barrier, inc=1, device_id=hdid(lax.rem(zl + k, 4), y), device_id_type=MESH
        )

    loads = [
        pltpu.make_async_copy(src, dst, local_sem.at[i])
        for i, (src, dst) in enumerate(
            [
                (wzx_in, wzx_ref), (wbc_in, wbc_ref), (wdt_in, wdt_ref), (ids_in, ids_ref),
                (hid_in, hid_ref), (gain_in, gain_ref), (cx_in, cx_ref), (cbc_in, cbc_ref),
                (og_in, og_ref), (wout_in, wo.at[y]),
            ]
        )
    ]
    for load in loads:
        load.start()

    for load in loads[0:3]:
        load.wait()
    bc_t[:, 0:ROWS] = jnp.concatenate([wbc_ref[...], jnp.zeros((32, 256), F32)], axis=0).T[:, 0:ROWS]
    sm_t[...] = jnp.zeros((32, 128), F32)
    sm_t[0:16, 0:ROWS] = bc_t[pl.ds(pl.multiple_of(hd * 16, 16), 16), 0:ROWS]
    sm_t[16:19, 0:ROWS] = wdt_ref[...]
    small[dp] = sm_t[...].astype(BF16)
    zw = wzx_ref[:, 0, :]
    xw = wzx_ref[:, 1, :]
    wst[:, 0:128] = xw[:, 0:128]
    wst[:, 128:256] = jnp.concatenate([xw[:, 128:192], zw[:, 128:192]], axis=1)
    wst[:, 256:384] = zw[:, 0:128]
    own_rows = pl.multiple_of(dp * ROWS, ROWS)
    w_buf[pl.ds(own_rows, ROWS), :] = wst[...].astype(BF16)

    def w_rows(owner):
        return w_buf.at[pl.ds(pl.multiple_of(owner * ROWS, ROWS), ROWS), :]

    weights = Gather([(W_IDS, w_rows)])

    @pl.when(dp == 0)
    def _():
        halo[...] = jnp.zeros_like(halo)

    for j in range(4):
        @pl.when(dp < j + 1)
        def _():
            info_rx[j] = jnp.zeros((16, 128), F32)
            l_rx[j] = jnp.zeros((FEAT, NSTATE), BF16)

        @pl.when(dp + j + 1 > DP - 1)
        def _():
            info_rx[4 + j] = jnp.zeros((16, 128), F32)

    pl.semaphore_wait(barrier, DP - 1 + 6)

    for k in (8, 7, 9, 6, 10, 5, 11, 12, 4, 13, 3, 14, 2, 15, 1):
        send(T_IDS + k - 1, small.at[dp], small.at[dp], dpid(lax.rem(dp + k, DP)))
    weights.own()
    for load in loads[3:9]:
        load.wait()
    send(HALO, hid_ref.at[pl.ds(TOK - 16, 16), :], halo, dpid(lax.rem(dp + 1, DP)), dp < DP - 1)

    phase("ids")
    def wo_rows(y_, c_):
        return wo.at[lax.rem(y_ + 4, 4), pl.ds(pl.multiple_of(c_ * 96, 96), 96), :]

    own_ids = ids_ref[dp].astype(F32)
    prev_ids = ids_ref[jnp.maximum(dp - 1, 0)].astype(F32)
    prev_col = jnp.broadcast_to(prev_ids[3:4, :], (128, 128)).T[112:128, :]
    first_dev = jnp.zeros((16, 128), jnp.int32) + dp == 0
    idc[0:16, :] = jnp.where(first_dev, -1.0, prev_col)
    for q in range(4):
        idc[16 + 128 * q : 144 + 128 * q, :] = jnp.broadcast_to(own_ids[q : q + 1, :], (128, 128)).T
    id_row = jnp.concatenate([own_ids[q : q + 1, :] for q in range(4)], axis=1)

    taps[...] = jnp.zeros_like(taps)
    taps[0:4, 0:128] = cx_ref[:, 0:128]
    taps[0:4, 128:192] = cx_ref[:, 128:192]
    taps[0:4, 256:512] = cbc_ref[...]

    phase("norm")
    gain = gain_ref[...].reshape(1, D)

    def norm_rows(rows):
        h = rows.astype(F32)
        scale = lax.rsqrt(jnp.mean(h * h, axis=1, keepdims=True) + EPSILON)
        return (h * scale * gain).astype(BF16)

    def norm_step(i, carry):
        r = pl.multiple_of(i * 32, 32)
        nrm[pl.ds(pl.multiple_of(16 + r, 16), 32), :] = norm_rows(hid_ref[pl.ds(r, 32), :])
        return carry

    lax.fori_loop(0, TOK // 32, norm_step, 0)
    phase("halo_wait")
    recv(HALO, halo, dpid(mate), dp > 0)
    nrm[0:16, :] = norm_rows(halo[...])

    phase("w_near")
    phase("dt")
    for k in range(1, DP):
        owner = lax.rem(dp + DP - k, DP)
        recv(T_IDS + k - 1, small.at[owner], dpid(owner))
    for j in range(DP):
        rows = jnp.concatenate([small[j].astype(F32), jnp.zeros((96, 128), F32)], axis=0).T
        wdt_mat[ROWS * j : ROWS * j + ROWS, :] = rows[0:ROWS, :].astype(BF16)
    bc_cols = dot(nrm[...], wdt_mat[...])
    bc_rows = jnp.concatenate([bc_cols[16:EXT, :].T, bc_cols[0:128, :].T], axis=1)
    bc_parts[y, zl] = bc_rows[0:16, :].astype(BF16)
    for k in (2, 1, 3):
        zt = lax.rem(zl + k, 4)
        send(BCZ + k - 1, bc_parts.at[y, zl], bc_parts.at[y, zl], hdid(zt, y))
    dt_rows = bc_rows[16:24, 0:TOK].astype(BF16).astype(F32)
    sub = lax.broadcasted_iota(jnp.int32, (8, TOK), 0)
    lane = lax.broadcasted_iota(jnp.int32, (8, TOK), 1)

    def by_head(ref, s):
        return jnp.where(s == 0, ref[0], jnp.where(s == 1, ref[1], ref[2]))

    pre = dt_rows + by_head(dtb_ref, sub)
    step_rows = jnp.maximum(pre, 0.0) + jnp.log1p(jnp.exp(-jnp.abs(pre)))
    rate_rows = -step_rows * jnp.exp(by_head(alog_ref, sub))
    prefix = lane_cumsum(rate_rows)
    id8 = jnp.broadcast_to(id_row, (8, TOK))
    at_end = run_end(prefix, id8)
    first_end = at_end[:, 0:1]
    total = prefix[:, TOK - 1 : TOK]
    info_tx[0:8, :] = jnp.broadcast_to(first_end, (8, 128))
    info_tx[8:16, :] = jnp.broadcast_to(total, (8, 128))
    for j in range(4):
        send(INFO_UP + j, info_tx, info_rx.at[j], dpid(lax.rem(dp + j + 1, DP)), dp + j + 1 < DP)
        send(INFO_DN + j, info_tx, info_rx.at[4 + j], dpid(lax.rem(dp - j - 1 + DP, DP)), dp >= j + 1)

    to_end = jnp.exp(at_end - prefix) * step_rows
    cols[...] = jnp.concatenate([prefix, jnp.zeros((120, TOK), F32)], axis=0).T

    phase("w_cross")
    weights.cross()
    phase("bcz")
    for k in range(1, 4):
        zs = lax.rem(zl + 4 - k, 4)
        recv(BCZ + k - 1, bc_parts.at[y, zs], hdid(zs, y))
    for k in (2, 1, 3):
        send(BCY + k - 1, bc_parts.at[y], bc_parts.at[y], hdid(zl, lax.rem(y + k, 4)))

    def wo_rows(y_, c_):
        return wo.at[lax.rem(y_ + 4, 4), pl.ds(pl.multiple_of(c_ * 96, 96), 96), :]

    loads[9].wait()
    for k in (1, 3, 2):
        send(WO + k - 1, wo_rows(y, c), wo_rows(y, c), hdid(zl, lax.rem(y + k, 4)))

    phase("w_near_rest")
    weights.near()
    weights.near_rest()
    phase("mm1")
    k_half = D // 2
    k_own = pl.multiple_of(zh * k_half, k_half)
    k_far = pl.multiple_of((1 - zh) * k_half, k_half)
    for n in range(0, 384, 128):
        u_buf[:, n : n + 128] = dot(nrm[:, pl.ds(k_own, k_half)], w_buf[pl.ds(k_own, k_half), n : n + 128])

    phase("bc_wait")
    for k in range(1, 4):
        ys = lax.rem(y + 4 - k, 4)
        recv(BCY + k - 1, bc_parts.at[ys], hdid(zl, ys))
    for half in range(2):
        rows = jnp.concatenate(
            [bc_parts[h % 4, h // 4].astype(F32) for h in range(8 * half, 8 * half + 8)], axis=0
        )
        col = 384 + 128 * half
        u_buf[0:16, col : col + 128] = rows[:, TOK : TOK + 128].T[0:16, :]
        u_buf[16:EXT, col : col + 128] = rows[:, 0:TOK].T

    phase("w_far")
    weights.far()
    phase("mm2")
    for n in range(0, 384, 128):
        u_buf[:, n : n + 128] += dot(nrm[:, pl.ds(k_far, k_half)], w_buf[pl.ds(k_far, k_half), n : n + 128])

    phase("conv")
    for r in range(0, EXT, 176):
        u_buf[r : r + 176, 0:384] = u_buf[r : r + 176, 0:384].astype(BF16).astype(F32)

    for q in range(4):
        r = 128 * q
        now = idc[16 + r : 144 + r, :]
        same = [jnp.where(idc[13 + k + r : 141 + k + r, :] == now, 1.0, 0.0) for k in range(3)]

        def conv(col, tap):
            acc = taps[3:4, tap : tap + 128] * u_buf[16 + r : 144 + r, col : col + 128]
            for k in range(3):
                acc = acc + same[k] * (
                    taps[k : k + 1, tap : tap + 128] * u_buf[13 + k + r : 141 + k + r, col : col + 128]
                )
            return (acc * jax.nn.sigmoid(acc)).astype(BF16)

        x0 = conv(0, 0)
        x1 = conv(128, 128)
        x_b[r : r + 128, 0:128] = x0
        x_b[r : r + 128, 128:256] = x1
        x_t[0:128, r : r + 128] = x0.astype(F32).T
        x_t[128:192, r : r + 128] = x1.astype(F32).T[0:64, :]
        b_b[r : r + 128, :] = conv(384, 256)
        c_b[r : r + 128, :] = conv(512, 384)

    phase("lstate")
    last_id = id_row[:, TOK - 1 : TOK]
    is_last = id8 == jnp.broadcast_to(last_id, (8, TOK))

    def weighted_x(weight):
        return jnp.concatenate(
            [x_t[64 * h : 64 * h + 64, :] * weight[h : h + 1, :] for h in range(HEADS)], axis=0
        ).astype(BF16)

    l_tx[...] = dot(weighted_x(jnp.where(is_last, to_end, 0.0)), b_b[...]).astype(BF16)
    for j in range(4):
        send(STATE + j, l_tx, l_rx.at[j], dpid(lax.rem(dp + j + 1, DP)), dp + j + 1 < DP)

    phase("table_loc")
    def first_id(k):
        return ids_ref[jnp.clip(k, 0, DP - 1)][0:1, 0:1]

    def final_id(k):
        return ids_ref[jnp.clip(k, 0, DP - 1)][3:4, 127:128]

    one = jnp.zeros((1, 1), jnp.int32)
    for j in range(4):
        recv(INFO_DN + j, info_rx.at[4 + j], dpid(mate), dp + j + 1 < DP)
    after = jnp.zeros((8, 128), F32)
    for j in range(4):
        goes_on = (first_id(dp + j + 1) == final_id(dp)) & (one + dp + j + 1 < DP)
        after = after + jnp.where(goes_on, info_rx[4 + j, 0:8, :], 0.0)
    carry_on = jnp.broadcast_to(jnp.exp(after)[:, 0:1], (8, TOK))
    xw_end = weighted_x(to_end * jnp.where(is_last, carry_on, 1.0))
    for g in range(PROMPTS):
        mine = jnp.where(idc[16:EXT, :] == float(g), 1.0, 0.0).astype(BF16)
        b_all[:, 128 * g : 128 * g + 128] = b_b[...] * mine
    for g in range(PROMPTS):
        loc[g] = dot(xw_end, b_all[:, 128 * g : 128 * g + 128]).astype(BF16)
    mate_half = pl.multiple_of((1 - c) * 96, 96)
    send(TAB0, loc.at[:, pl.ds(mate_half, 96), :], tab0, dpid(mate))

    phase("wo_mate")
    for k in (1, 3, 2):
        recv(WO + k - 1, wo_rows(y - k, c), dpid(mate))
        send(WO_MATE + k - 1, wo_rows(y - k, c), wo_rows(y - k, c), dpid(mate))
    phase("scores")
    scol = lax.broadcasted_iota(jnp.int32, (128, TOK), 1)
    srow = lax.broadcasted_iota(jnp.int32, (128, TOK), 0)
    for q in range(4):
        r = 128 * q
        w = r + 128
        scores = dot_t(c_b[r:w, :], b_b[0:w, :])
        ok = (jnp.broadcast_to(idc[16 + r : 16 + w, 0:1], (128, w)) == jnp.broadcast_to(id_row[:, 0:w], (128, w))) & (
            scol[:, 0:w] <= srow[:, 0:w] + r
        )
        scores = jnp.where(ok, scores, 0.0)
        parts = []
        for h in range(HEADS):
            gap = jnp.broadcast_to(cols[r:w, h : h + 1], (128, w)) - prefix[h : h + 1, 0:w]
            mix = (scores * (jnp.exp(jnp.minimum(gap, 0.0)) * step_rows[h : h + 1, 0:w])).astype(BF16)
            col = 0 if h < 2 else 128
            parts.append(dot(mix, x_b[0:w, col : col + 128]))
        low = lax.broadcasted_iota(jnp.int32, (128, 128), 1) < 64
        smask[r:w, 0:128] = jnp.where(low, parts[0], parts[1])
        smask[r:w, 128:256] = parts[2]

    phase("tab0_wait")
    my_half = pl.multiple_of(c * 96, 96)
    recv(TAB0, tab0, dpid(mate))
    for g in range(PROMPTS):
        tabs[g] = (loc[g, pl.ds(my_half, 96), :].astype(F32) + tab0[g].astype(F32)).astype(BF16)
    send(TABZ, tabs.at[pl.ds(4 - 2 * zh, 2)], tabz, dpid(across))

    phase("state_wait")
    for j in range(4):
        recv(INFO_UP + j, info_rx.at[j], dpid(mate), dp >= j + 1)
        recv(STATE + j, l_rx.at[j], dpid(mate), dp >= j + 1)
    state = l_rx[3].astype(F32)
    for j in (2, 1, 0):
        joined = (final_id(dp - j - 1) == final_id(dp - j - 2)) & (one + dp - j - 2 >= 0)
        gain_j = jnp.where(joined, jnp.exp(info_rx[j, 8:16, :]), 0.0)
        rows = jnp.concatenate(
            [jnp.broadcast_to(gain_j[h : h + 1, :], (64, 128)) for h in range(HEADS)], axis=0
        )
        state = l_rx[j].astype(F32) + rows * state
    s_in[0:FEAT, :] = state.astype(BF16)
    s_in[FEAT:256, :] = jnp.zeros((64, NSTATE), BF16)

    phase("yinter")
    before_id = jnp.where(one + dp > 0, final_id(dp - 1), -1).astype(F32)
    lane1 = lax.broadcasted_iota(jnp.int32, (128, 128), 1)
    low = lane1 < 64
    skip0 = jnp.where(low, skip_ref[0], skip_ref[1])
    skip1 = jnp.where(low, skip_ref[2], 0.0)
    og0 = og_ref[:, 0:128]
    og1 = jnp.concatenate([og_ref[:, 128:192], jnp.zeros((1, 64), F32)], axis=1)
    for q in range(4):
        r = 128 * q
        w = r + 128
        inter = dot_t(c_b[r:w, :], s_in[...])
        enters = jnp.where(idc[16 + r : 16 + w, :] == before_id, 1.0, 0.0)
        decay = jnp.exp(cols[r:w, :])
        e0 = jnp.broadcast_to(decay[:, 0:1], (128, 128))
        e1 = jnp.broadcast_to(decay[:, 1:2], (128, 128))
        e2 = jnp.broadcast_to(decay[:, 2:3], (128, 128))
        y0 = smask[r:w, 0:128] + enters * jnp.where(low, e0, e1) * inter[:, 0:128]
        y1 = smask[r:w, 128:256] + enters * e2 * inter[:, 128:256]
        y0 = y0 + skip0 * x_b[r:w, 0:128].astype(F32)
        y1 = y1 + skip1 * x_b[r:w, 128:256].astype(F32)
        z0 = u_buf[16 + r : 16 + w, 256:384]
        z1 = jnp.where(low, pltpu.roll(u_buf[16 + r : 16 + w, 128:256], 64, 1), 0.0)
        g0 = y0 * (z0 * jax.nn.sigmoid(z0))
        g1 = y1 * (z1 * jax.nn.sigmoid(z1))
        sq = jnp.sum(g0 * g0 + g1 * g1, axis=1, keepdims=True)
        hi = sq.astype(BF16).astype(F32)
        g_send[q, :, :, 0:128] = (g0 * og0).astype(BF16).reshape(4, 32, 128)
        g_send[q, :, :, 128:256] = jnp.where(
            low, g1 * og1, jnp.where(lane1 == 64, hi, jnp.where(lane1 == 65, sq - hi, 0.0))
        ).astype(BF16).reshape(4, 32, 128)
    for k in (2, 1, 3):
        yt = lax.rem(y + k, 4)
        send(A2A + k - 1, g_send.at[:, yt], a_rx.at[y], hdid(zl, yt))
    a_rx[y] = g_send[:, y]

    phase("tabz_wait")
    recv(TABZ, tabz, dpid(across))
    tabm[...] = tabs[pl.ds(4 * zh, 4)]
    mid = 2 - 2 * zh
    tabm[pl.ds(mid, 2)] = (tabs[pl.ds(4 * zh + mid, 2)].astype(F32) + tabz[...].astype(F32)).astype(BF16)
    for k in range(1, 4):
        xt = lax.rem(x + k, 4)
        send(TABX + k - 1, tabm.at[xt], tabx.at[k - 1], dpid(dev(zh, xt, c)))

    phase("tabx_wait")
    for k in range(1, 4):
        recv(TABX + k - 1, tabx.at[k - 1], dpid(mate))
    done = tabm[x].astype(F32)
    for k in range(3):
        done = done + tabx[k].astype(F32)
    fin[dp // 2, pl.ds(my_half, 96), :] = done.astype(BF16)

    def f_rows(owner):
        return fin.at[owner // 2, pl.ds(pl.multiple_of(lax.rem(owner, 2) * 96, 96), 96), :]

    phase("fin_own")
    finals = Gather([(F_IDS, f_rows)])
    finals.own()

    phase("wo_finish")
    for k in (1, 3, 2):
        recv(WO_MATE + k - 1, wo_rows(y - k, 1 - c), dpid(mate))

    phase("a2a_wait")
    for k in range(1, 4):
        ys = lax.rem(y + 4 - k, 4)
        recv(A2A + k - 1, a_rx.at[ys], hdid(zl, ys))
    phase("outproj")
    sq = jnp.zeros((128, 1), F32)
    picked = (lane1 == 64) | (lane1 == 65)
    for y_ in range(4):
        tails = a_rx[y_, :, :, 128:256].reshape(128, 128).astype(F32)
        sq = sq + jnp.sum(jnp.where(picked, tails, 0.0), axis=1, keepdims=True)
    hi = sq.astype(BF16).astype(F32)
    tail = jnp.where(lane1 == 0, hi, jnp.where(lane1 == 1, sq - hi, 0.0))
    own_acc[:, D : D + 128] = tail
    part[:, :, D : D + 128] = tail.astype(BF16).reshape(4, 32, 128)
    for n in range(0, D, 256):
        acc = jnp.zeros((128, 256), F32)
        for y_ in range(4):
            acc = acc + dot(a_rx[y_, :, :, 0:FEAT].reshape(128, FEAT), wo[y_, :, n : n + 256])
        own_acc[:, n : n + 256] = acc
        part[:, :, n : n + 256] = acc.astype(BF16).reshape(4, 32, 256)
    for k in (2, 1, 3):
        zt = lax.rem(zl + k, 4)
        send(RSZ + k - 1, part.at[zt], rs_rx.at[k - 1], hdid(zt, y))

    phase("fin_near")
    finals.cross()
    phase("fin_cross")
    finals.near()
    phase("fin_nearrest")
    finals.near_rest()
    phase("fin_far")
    finals.far()
    phase("rsy_wait")
    for k in range(1, 4):
        recv(RSZ + k - 1, rs_rx.at[k - 1], hdid(lax.rem(zl + 4 - k, 4), y))
    phase("out")
    z_rows = pl.ds(pl.multiple_of(zl * 32, 32), 32)
    sq = own_acc[z_rows, D : D + 128]
    for k in range(3):
        sq = sq + rs_rx[k, :, D : D + 128].astype(F32)
    scale = lax.rsqrt(jnp.sum(sq, axis=1, keepdims=True) / (FEAT * HD) + EPSILON)
    acc = own_acc[z_rows, 0:D]
    for k in range(3):
        acc = acc + rs_rx[k, :, 0:D].astype(F32)
    resid = hid_ref[pl.ds(pl.multiple_of(hd * 32, 32), 32), :].astype(F32)
    out_ref[...] = (resid + scale * acc).astype(BF16)

    phase("st_out")
    for r in range(4):
        st_ref[r] = fin[req_ref[r]]

    phase("drain")
    for m, src, dst, to, cond in pending:
        if cond is None:
            msg(m, src, dst, to).wait_send()
        else:
            @pl.when(cond)
            def _():
                msg(m, src, dst, to).wait_send()
    phase(None)


def write_out(rows_ref, states_ref, out_ref, st_ref):
    out_ref[...] = rows_ref[...]
    st_ref[...] = states_ref[...].astype(F32)


def on_device(
    hidden, token_prompt, request_prompt, in_gain, w_zx, w_bc, w_dt, dt_bias, a_log, conv_x,
    conv_bc, skip_gain, out_gain, w_out,
):
    vmem = pl.BlockSpec(memory_space=pltpu.VMEM)
    smem = pl.BlockSpec(memory_space=pltpu.SMEM)
    layer_out, states = pl.pallas_call(
        body,
        out_shape=(
            jax.ShapeDtypeStruct((TOK // HD, D), BF16),
            jax.ShapeDtypeStruct((4, FEAT, NSTATE), BF16),
        ),
        in_specs=[smem] * 4 + [pl.BlockSpec(memory_space=pl.ANY)] * 10,
        out_specs=(vmem, vmem),
        scratch_shapes=[
            pltpu.VMEM((ROWS, 2, FEAT), F32),
            pltpu.VMEM((ROWS, 256), F32),
            pltpu.VMEM((HEADS, ROWS), F32),
            pltpu.VMEM((DP, 4, 128), jnp.int32),
            pltpu.VMEM((TOK, D), BF16),
            pltpu.VMEM((D,), F32),
            pltpu.VMEM((4, FEAT), F32),
            pltpu.VMEM((4, 256), F32),
            pltpu.VMEM((1, FEAT), F32),
            pltpu.VMEM((D, 384), BF16),
            pltpu.VMEM((ROWS, 384), F32),
            pltpu.VMEM((256, 128), F32),
            pltpu.VMEM((32, 128), F32),
            pltpu.VMEM((DP, 32, 128), BF16),
            pltpu.VMEM((D, 128), BF16),
            pltpu.VMEM((4, 4, 16, 640), BF16),
            pltpu.VMEM((16, D), BF16),
            pltpu.VMEM((EXT, D), BF16),
            pltpu.VMEM((EXT, 128), F32),
            pltpu.VMEM((EXT, 640), F32),
            pltpu.VMEM((8, 512), F32),
            pltpu.VMEM((FEAT, TOK), F32),
            pltpu.VMEM((TOK, 256), BF16),
            pltpu.VMEM((TOK, 128), BF16),
            pltpu.VMEM((TOK, 128), BF16),
            pltpu.VMEM((TOK, 128 * PROMPTS), BF16),
            pltpu.VMEM((16, 128), F32),
            pltpu.VMEM((8, 16, 128), F32),
            pltpu.VMEM((FEAT, NSTATE), BF16),
            pltpu.VMEM((4, FEAT, NSTATE), BF16),
            pltpu.VMEM((256, NSTATE), BF16),
            pltpu.VMEM((TOK, 128), F32),
            pltpu.VMEM((TOK, 256), F32),
            pltpu.VMEM((PROMPTS, FEAT, NSTATE), BF16),
            pltpu.VMEM((PROMPTS, 96, NSTATE), BF16),
            pltpu.VMEM((PROMPTS, 96, NSTATE), BF16),
            pltpu.VMEM((2, 96, NSTATE), BF16),
            pltpu.VMEM((4, 96, NSTATE), BF16),
            pltpu.VMEM((3, 96, NSTATE), BF16),
            pltpu.VMEM((PROMPTS, FEAT, NSTATE), BF16),
            pltpu.VMEM((4, 4, 32, 256), BF16),
            pltpu.VMEM((4, 4, 32, 256), BF16),
            pltpu.VMEM((4, FEAT, D), BF16),
            pltpu.VMEM((4, 32, OUTW), BF16),
            pltpu.VMEM((128, OUTW), F32),
            pltpu.VMEM((3, 32, OUTW), BF16),
            pltpu.SemaphoreType.DMA((N_MSG,)),
            pltpu.SemaphoreType.DMA((N_MSG,)),
            pltpu.SemaphoreType.DMA((10,)),
        ],
        compiler_params=pltpu.CompilerParams(
            collective_id=0, has_side_effects=True, vmem_limit_bytes=60 * 2**20
        ),
        name="layer",
    )(
        request_prompt, dt_bias, a_log, skip_gain, w_zx, w_bc, w_dt.T,
        token_prompt.reshape(DP, 4, 128), hidden, in_gain, conv_x, conv_bc,
        out_gain.reshape(1, FEAT), w_out,
    )
    layer_out, states = pl.pallas_call(
        write_out,
        out_shape=(
            jax.ShapeDtypeStruct((TOK // HD, D), BF16),
            jax.ShapeDtypeStruct((4, FEAT, NSTATE), F32),
        ),
        in_specs=[vmem, vmem],
        out_specs=(vmem, vmem),
        name="write_out",
    )(layer_out, states)
    return layer_out, states.reshape(4, HEADS, 64, NSTATE)


def solution(mesh):
    in_specs = (
        P("dp", None), P(), P("dp"), P(), P("dp", None, "head"), P("dp", None), P("dp", "head"),
        P("head"), P("head"), P(None, "head"), P(), P("head"), P("head"), P("head", None),
    )
    out_specs = (P(("dp", "head"), None), P("dp", "head", None, None))
    return jax.shard_map(on_device, mesh=mesh, in_specs=in_specs, out_specs=out_specs, check_vma=False)
```

```python
import jax
import jax.numpy as jnp
from jax import lax
from jax.experimental import pallas as pl
from jax.experimental.pallas import tpu as pltpu
from jax.sharding import PartitionSpec as P

MESH = pl.DeviceIdType.MESH
F32 = jnp.float32
BF16 = jnp.bfloat16
EPSILON = 1e-05

DP = 16
HD = 16
D = 1536
TOK = 512
EXT = TOK + 16
ROWS = 96
HEADS = 3
FEAT = 192
NSTATE = 128
PROMPTS = 8
OUTW = D + 128

W_IDS = 0
T_IDS = 15
F_IDS = 30
HALO = 45
INFO_UP = 46
INFO_DN = 50
STATE = 54
WO = 58
WO_MATE = 61
TAB0 = 64
TABZ = 65
TABX = 66
A2A = 69
RSZ = 72
BCZ = 75
BCY = 78
TABC = 81
N_MSG = 89


def dot(a, b):
    return lax.dot_general(a, b, (((1,), (0,)), ((), ())), preferred_element_type=F32)


def dot_t(a, b):
    return lax.dot_general(a, b, (((1,), (1,)), ((), ())), preferred_element_type=F32)


def lane_cumsum(v):
    width = v.shape[1]
    lane = lax.broadcasted_iota(jnp.int32, v.shape, 1)
    step = 1
    while step < width:
        v = v + jnp.where(lane >= step, pltpu.roll(v, step, 1), 0.0)
        step *= 2
    return v


def run_end(v, ids):
    width = v.shape[1]
    lane = lax.broadcasted_iota(jnp.int32, v.shape, 1)
    step = 1
    while step < width:
        same = (pltpu.roll(ids, width - step, 1) == ids) & (lane < width - step)
        v = jnp.where(same, pltpu.roll(v, width - step, 1), v)
        step *= 2
    return v


SCOPE = []


def phase(name):
    if SCOPE:
        SCOPE.pop().__exit__(None, None, None)
    if name and TRACE:
        SCOPE.append(jax.named_scope(name))
        SCOPE[-1].__enter__()


TRACE = False


def body(
    req_ref, dtb_ref, alog_ref, skip_ref, wzx_in, wbc_in, wdt_in, ids_in, hid_in, gain_in,
    cx_in, cbc_in, og_in, wout_in, out_ref, st_ref,
    wzx_ref, wbc_ref, wdt_ref, ids_ref, hid_ref, gain_ref, cx_ref, cbc_ref, og_ref,
    w_buf, wst, bc_t, sm_t, small, wdt_mat, bc_parts, halo, nrm, idc, u_buf, taps, x_t, x_b, b_b, c_b, b_all,
    info_tx, info_rx, l_tx, l_rx, s_in, cols, smask, loc, tab0, tabs, tabz, tabx, fin,
    g_send, a_rx, wo, part, own_acc, rs_rx, send_sem, recv_sem, local_sem,
):
    dp = lax.axis_index("dp")
    hd = lax.axis_index("head")
    zh = dp // 8
    x = (dp // 2) % 4
    c = dp % 2
    zl = hd // 4
    y = hd % 4

    def dev(z_, x_, c_):
        return z_ * 8 + lax.rem(x_ + 8, 4) * 2 + c_

    across = dev(1 - zh, x, c)
    mate = dev(zh, x, 1 - c)

    def dpid(d):
        return {"dp": d}

    def hdid(z_, y_):
        return {"head": z_ * 4 + y_}

    def msg(m, src, dst, to):
        return pltpu.make_async_remote_copy(
            src_ref=src, dst_ref=dst, send_sem=send_sem.at[m], recv_sem=recv_sem.at[m],
            device_id=to, device_id_type=MESH,
        )

    pending = []

    def send(m, src, dst, to, cond=None):
        if cond is None:
            msg(m, src, dst, to).start()
        else:
            @pl.when(cond)
            def _():
                msg(m, src, dst, to).start()
        pending.append((m, src, dst, to, cond))

    def recv(m, dst, to, cond=None):
        if cond is None:
            msg(m, dst, dst, to).wait_recv()
        else:
            @pl.when(cond)
            def _():
                msg(m, dst, dst, to).wait_recv()

    class Gather:
        def __init__(self, families):
            self.families = families

        def send(self, k, owner, to):
            for base, ref_of in self.families:
                r = ref_of(owner)
                send(base + k, r, r, dpid(to))

        def recv(self, k, owner):
            for base, ref_of in self.families:
                recv(base + k, ref_of(owner), dpid(mate))

        def own(self):
            self.send(3, dp, across)
            self.send(2, dp, dev(zh, x + 2, c))
            self.send(0, dp, dev(zh, x + 1, c))
            self.send(1, dp, dev(zh, x - 1, c))
            self.send(7, dp, mate)

        def cross(self):
            o = 1 - zh
            self.recv(3, dev(o, x, c))
            self.send(6, dev(o, x, c), dev(zh, x + 2, c))
            self.send(4, dev(o, x, c), dev(zh, x + 1, c))
            self.send(5, dev(o, x, c), dev(zh, x - 1, c))
            self.send(11, dev(o, x, c), mate)

        def near(self):
            for k, step in ((0, -1), (1, 1), (2, 2)):
                self.recv(k, dev(zh, x + step, c))
                self.send(8 + k, dev(zh, x + step, c), mate)

        def near_rest(self):
            for k, step in ((7, 0), (8, -1), (9, 1), (10, 2)):
                self.recv(k, dev(zh, x + step, 1 - c))

        def far(self):
            o = 1 - zh
            for k, step in ((4, -1), (5, 1), (6, 2)):
                self.recv(k, dev(o, x + step, c))
                self.send(8 + k, dev(o, x + step, c), mate)
            for k, step in ((11, 0), (12, -1), (13, 1), (14, 2)):
                self.recv(k, dev(o, x + step, 1 - c))

    phase("entry")
    barrier = pltpu.get_barrier_semaphore()
    for k in range(1, DP):
        pl.semaphore_signal(
            barrier, inc=1, device_id=dpid(lax.rem(dp + k, DP)), device_id_type=MESH
        )
    for k in range(1, 4):
        pl.semaphore_signal(
            barrier, inc=1, device_id=hdid(zl, lax.rem(y + k, 4)), device_id_type=MESH
        )
        pl.semaphore_signal(
            barrier, inc=1, device_id=hdid(lax.rem(zl + k, 4), y), device_id_type=MESH
        )

    loads = [
        pltpu.make_async_copy(src, dst, local_sem.at[i])
        for i, (src, dst) in enumerate(
            [
                (wzx_in, wzx_ref), (wbc_in, wbc_ref), (wdt_in, wdt_ref), (ids_in, ids_ref),
                (hid_in, hid_ref), (gain_in, gain_ref), (cx_in, cx_ref), (cbc_in, cbc_ref),
                (og_in, og_ref), (wout_in, wo.at[y]),
            ]
        )
    ]
    for load in loads:
        load.start()

    for load in loads[0:3]:
        load.wait()
    bc_t[:, 0:ROWS] = jnp.concatenate([wbc_ref[...], jnp.zeros((32, 256), F32)], axis=0).T[:, 0:ROWS]
    sm_t[...] = jnp.zeros((32, 128), F32)
    sm_t[0:16, 0:ROWS] = bc_t[pl.ds(pl.multiple_of(hd * 16, 16), 16), 0:ROWS]
    sm_t[16:19, 0:ROWS] = wdt_ref[...]
    small[dp] = sm_t[...].astype(BF16)
    zw = wzx_ref[:, 0, :]
    xw = wzx_ref[:, 1, :]
    wst[:, 0:128] = xw[:, 0:128]
    wst[:, 128:256] = jnp.concatenate([xw[:, 128:192], zw[:, 128:192]], axis=1)
    wst[:, 256:384] = zw[:, 0:128]
    own_rows = pl.multiple_of(dp * ROWS, ROWS)
    w_buf[pl.ds(own_rows, ROWS), :] = wst[...].astype(BF16)

    def w_rows(owner):
        return w_buf.at[pl.ds(pl.multiple_of(owner * ROWS, ROWS), ROWS), :]

    weights = Gather([(W_IDS, w_rows)])

    @pl.when(dp == 0)
    def _():
        halo[...] = jnp.zeros_like(halo)

    @pl.when(x // 2 == zh)
    def _():
        tabz[...] = jnp.zeros_like(tabz)

    for j in range(4):
        @pl.when(dp < j + 1)
        def _():
            info_rx[j] = jnp.zeros((16, 128), F32)
            l_rx[j] = jnp.zeros((FEAT, NSTATE), BF16)

        @pl.when(dp + j + 1 > DP - 1)
        def _():
            info_rx[4 + j] = jnp.zeros((16, 128), F32)

    pl.semaphore_wait(barrier, DP - 1 + 6)

    for k in (8, 7, 9, 6, 10, 5, 11, 12, 4, 13, 3, 14, 2, 15, 1):
        send(T_IDS + k - 1, small.at[dp], small.at[dp], dpid(lax.rem(dp + k, DP)))
    weights.own()
    for load in loads[3:9]:
        load.wait()
    send(HALO, hid_ref.at[pl.ds(TOK - 16, 16), :], halo, dpid(lax.rem(dp + 1, DP)), dp < DP - 1)

    phase("ids")
    def wo_rows(y_, c_):
        return wo.at[lax.rem(y_ + 4, 4), pl.ds(pl.multiple_of(c_ * 96, 96), 96), :]

    own_ids = ids_ref[dp].astype(F32)
    prev_ids = ids_ref[jnp.maximum(dp - 1, 0)].astype(F32)
    prev_col = jnp.broadcast_to(prev_ids[3:4, :], (128, 128)).T[112:128, :]
    first_dev = jnp.zeros((16, 128), jnp.int32) + dp == 0
    idc[0:16, :] = jnp.where(first_dev, -1.0, prev_col)
    for q in range(4):
        idc[16 + 128 * q : 144 + 128 * q, :] = jnp.broadcast_to(own_ids[q : q + 1, :], (128, 128)).T
    id_row = jnp.concatenate([own_ids[q : q + 1, :] for q in range(4)], axis=1)

    taps[...] = jnp.zeros_like(taps)
    taps[0:4, 0:128] = cx_ref[:, 0:128]
    taps[0:4, 128:192] = cx_ref[:, 128:192]
    taps[0:4, 256:512] = cbc_ref[...]

    phase("norm")
    gain = gain_ref[...].reshape(1, D)

    def norm_rows(rows):
        h = rows.astype(F32)
        scale = lax.rsqrt(jnp.mean(h * h, axis=1, keepdims=True) + EPSILON)
        return (h * scale * gain).astype(BF16)

    def norm_step(i, carry):
        r = pl.multiple_of(i * 32, 32)
        nrm[pl.ds(pl.multiple_of(16 + r, 16), 32), :] = norm_rows(hid_ref[pl.ds(r, 32), :])
        return carry

    lax.fori_loop(0, TOK // 32, norm_step, 0)
    phase("halo_wait")
    recv(HALO, halo, dpid(mate), dp > 0)
    nrm[0:16, :] = norm_rows(halo[...])

    phase("w_near")
    phase("dt")
    for k in range(1, DP):
        owner = lax.rem(dp + DP - k, DP)
        recv(T_IDS + k - 1, small.at[owner], dpid(owner))
    for j in range(DP):
        rows = jnp.concatenate([small[j].astype(F32), jnp.zeros((96, 128), F32)], axis=0).T
        wdt_mat[ROWS * j : ROWS * j + ROWS, :] = rows[0:ROWS, :].astype(BF16)
    bc_cols = dot(nrm[...], wdt_mat[...])
    bc_rows = jnp.concatenate([bc_cols[16:EXT, :].T, bc_cols[0:128, :].T], axis=1)
    bc_parts[y, zl] = bc_rows[0:16, :].astype(BF16)
    for k in (2, 1, 3):
        zt = lax.rem(zl + k, 4)
        send(BCZ + k - 1, bc_parts.at[y, zl], bc_parts.at[y, zl], hdid(zt, y))
    dt_rows = bc_rows[16:24, 0:TOK].astype(BF16).astype(F32)
    sub = lax.broadcasted_iota(jnp.int32, (8, TOK), 0)
    lane = lax.broadcasted_iota(jnp.int32, (8, TOK), 1)

    def by_head(ref, s):
        return jnp.where(s == 0, ref[0], jnp.where(s == 1, ref[1], ref[2]))

    pre = dt_rows + by_head(dtb_ref, sub)
    step_rows = jnp.maximum(pre, 0.0) + jnp.log1p(jnp.exp(-jnp.abs(pre)))
    rate_rows = -step_rows * jnp.exp(by_head(alog_ref, sub))
    prefix = lane_cumsum(rate_rows)
    id8 = jnp.broadcast_to(id_row, (8, TOK))
    at_end = run_end(prefix, id8)
    first_end = at_end[:, 0:1]
    total = prefix[:, TOK - 1 : TOK]
    info_tx[0:8, :] = jnp.broadcast_to(first_end, (8, 128))
    info_tx[8:16, :] = jnp.broadcast_to(total, (8, 128))
    for j in range(4):
        send(INFO_UP + j, info_tx, info_rx.at[j], dpid(lax.rem(dp + j + 1, DP)), dp + j + 1 < DP)
        send(INFO_DN + j, info_tx, info_rx.at[4 + j], dpid(lax.rem(dp - j - 1 + DP, DP)), dp >= j + 1)

    to_end = jnp.exp(at_end - prefix) * step_rows
    cols[...] = jnp.concatenate([prefix, jnp.zeros((120, TOK), F32)], axis=0).T

    phase("w_cross")
    weights.cross()
    phase("bcz")
    for k in range(1, 4):
        zs = lax.rem(zl + 4 - k, 4)
        recv(BCZ + k - 1, bc_parts.at[y, zs], hdid(zs, y))
    for k in (2, 1, 3):
        send(BCY + k - 1, bc_parts.at[y], bc_parts.at[y], hdid(zl, lax.rem(y + k, 4)))

    def wo_rows(y_, c_):
        return wo.at[lax.rem(y_ + 4, 4), pl.ds(pl.multiple_of(c_ * 96, 96), 96), :]

    loads[9].wait()
    for k in (1, 3, 2):
        send(WO + k - 1, wo_rows(y, c), wo_rows(y, c), hdid(zl, lax.rem(y + k, 4)))

    phase("w_near_rest")
    weights.near()
    weights.near_rest()
    phase("mm1")
    k_half = D // 2
    k_own = pl.multiple_of(zh * k_half, k_half)
    k_far = pl.multiple_of((1 - zh) * k_half, k_half)
    for n in range(0, 384, 128):
        u_buf[:, n : n + 128] = dot(nrm[:, pl.ds(k_own, k_half)], w_buf[pl.ds(k_own, k_half), n : n + 128])

    phase("bc_wait")
    for k in range(1, 4):
        ys = lax.rem(y + 4 - k, 4)
        recv(BCY + k - 1, bc_parts.at[ys], hdid(zl, ys))
    for half in range(2):
        rows = jnp.concatenate(
            [bc_parts[h % 4, h // 4].astype(F32) for h in range(8 * half, 8 * half + 8)], axis=0
        )
        col = 384 + 128 * half
        u_buf[0:16, col : col + 128] = rows[:, TOK : TOK + 128].T[0:16, :]
        u_buf[16:EXT, col : col + 128] = rows[:, 0:TOK].T

    phase("w_far")
    weights.far()
    phase("mm2")
    for n in range(0, 384, 128):
        u_buf[:, n : n + 128] += dot(nrm[:, pl.ds(k_far, k_half)], w_buf[pl.ds(k_far, k_half), n : n + 128])

    phase("conv")
    for r in range(0, EXT, 176):
        u_buf[r : r + 176, 0:384] = u_buf[r : r + 176, 0:384].astype(BF16).astype(F32)

    for q in range(4):
        r = 128 * q
        now = idc[16 + r : 144 + r, :]
        same = [jnp.where(idc[13 + k + r : 141 + k + r, :] == now, 1.0, 0.0) for k in range(3)]

        def conv(col, tap):
            acc = taps[3:4, tap : tap + 128] * u_buf[16 + r : 144 + r, col : col + 128]
            for k in range(3):
                acc = acc + same[k] * (
                    taps[k : k + 1, tap : tap + 128] * u_buf[13 + k + r : 141 + k + r, col : col + 128]
                )
            return (acc * jax.nn.sigmoid(acc)).astype(BF16)

        x0 = conv(0, 0)
        x1 = conv(128, 128)
        x_b[r : r + 128, 0:128] = x0
        x_b[r : r + 128, 128:256] = x1
        x_t[0:128, r : r + 128] = x0.astype(F32).T
        x_t[128:192, r : r + 128] = x1.astype(F32).T[0:64, :]
        b_b[r : r + 128, :] = conv(384, 256)
        c_b[r : r + 128, :] = conv(512, 384)

    phase("lstate")
    last_id = id_row[:, TOK - 1 : TOK]
    is_last = id8 == jnp.broadcast_to(last_id, (8, TOK))

    def weighted_x(weight):
        return jnp.concatenate(
            [x_t[64 * h : 64 * h + 64, :] * weight[h : h + 1, :] for h in range(HEADS)], axis=0
        ).astype(BF16)

    l_tx[...] = dot(weighted_x(jnp.where(is_last, to_end, 0.0)), b_b[...]).astype(BF16)
    for j in range(4):
        send(STATE + j, l_tx, l_rx.at[j], dpid(lax.rem(dp + j + 1, DP)), dp + j + 1 < DP)

    phase("table_loc")
    def first_id(k):
        return ids_ref[jnp.clip(k, 0, DP - 1)][0:1, 0:1]

    def final_id(k):
        return ids_ref[jnp.clip(k, 0, DP - 1)][3:4, 127:128]

    one = jnp.zeros((1, 1), jnp.int32)
    for j in range(4):
        recv(INFO_DN + j, info_rx.at[4 + j], dpid(mate), dp + j + 1 < DP)
    after = jnp.zeros((8, 128), F32)
    for j in range(4):
        goes_on = (first_id(dp + j + 1) == final_id(dp)) & (one + dp + j + 1 < DP)
        after = after + jnp.where(goes_on, info_rx[4 + j, 0:8, :], 0.0)
    carry_on = jnp.broadcast_to(jnp.exp(after)[:, 0:1], (8, TOK))
    xw_end = weighted_x(to_end * jnp.where(is_last, carry_on, 1.0))
    for g in range(PROMPTS):
        mine = jnp.where(idc[16:EXT, :] == float(g), 1.0, 0.0).astype(BF16)
        b_all[:, 128 * g : 128 * g + 128] = b_b[...] * mine
    for g in range(PROMPTS):
        loc[g] = dot(xw_end, b_all[:, 128 * g : 128 * g + 128]).astype(BF16)
    mate_half = pl.multiple_of((1 - c) * 96, 96)
    send(TAB0, loc.at[:, pl.ds(mate_half, 96), :], tab0, dpid(mate))

    phase("scores")
    scol = lax.broadcasted_iota(jnp.int32, (128, TOK), 1)
    srow = lax.broadcasted_iota(jnp.int32, (128, TOK), 0)
    for q in range(4):
        r = 128 * q
        w = r + 128
        scores = dot_t(c_b[r:w, :], b_b[0:w, :])
        ok = (jnp.broadcast_to(idc[16 + r : 16 + w, 0:1], (128, w)) == jnp.broadcast_to(id_row[:, 0:w], (128, w))) & (
            scol[:, 0:w] <= srow[:, 0:w] + r
        )
        scores = jnp.where(ok, scores, 0.0)
        parts = []
        for h in range(HEADS):
            gap = jnp.broadcast_to(cols[r:w, h : h + 1], (128, w)) - prefix[h : h + 1, 0:w]
            mix = (scores * (jnp.exp(jnp.minimum(gap, 0.0)) * step_rows[h : h + 1, 0:w])).astype(BF16)
            col = 0 if h < 2 else 128
            parts.append(dot(mix, x_b[0:w, col : col + 128]))
        low = lax.broadcasted_iota(jnp.int32, (128, 128), 1) < 64
        smask[r:w, 0:128] = jnp.where(low, parts[0], parts[1])
        smask[r:w, 128:256] = parts[2]

    phase("tab0_wait")
    my_half = pl.multiple_of(c * 96, 96)
    recv(TAB0, tab0, dpid(mate))
    for g in range(PROMPTS):
        tabs[g] = (loc[g, pl.ds(my_half, 96), :].astype(F32) + tab0[g].astype(F32)).astype(BF16)
    for t in range(2):
        send(TABC + 2 * x + t, tabs.at[4 - 2 * zh + t], tabz.at[x], dpid(dev(1 - zh, 2 * zh + t, c)))
    for k in (2, 1, 3):
        xt = lax.rem(x + k, 4)
        send(TABX + k - 1, tabs.at[4 * zh + xt], tabx.at[k - 1], dpid(dev(zh, xt, c)))

    phase("wo_mate")
    for k in (1, 3, 2):
        recv(WO + k - 1, wo_rows(y - k, c), dpid(mate))
        send(WO_MATE + k - 1, wo_rows(y - k, c), wo_rows(y - k, c), dpid(mate))
    phase("state_wait")
    for j in range(4):
        recv(INFO_UP + j, info_rx.at[j], dpid(mate), dp >= j + 1)
        recv(STATE + j, l_rx.at[j], dpid(mate), dp >= j + 1)
    state = l_rx[3].astype(F32)
    for j in (2, 1, 0):
        joined = (final_id(dp - j - 1) == final_id(dp - j - 2)) & (one + dp - j - 2 >= 0)
        gain_j = jnp.where(joined, jnp.exp(info_rx[j, 8:16, :]), 0.0)
        rows = jnp.concatenate(
            [jnp.broadcast_to(gain_j[h : h + 1, :], (64, 128)) for h in range(HEADS)], axis=0
        )
        state = l_rx[j].astype(F32) + rows * state
    s_in[0:FEAT, :] = state.astype(BF16)
    s_in[FEAT:256, :] = jnp.zeros((64, NSTATE), BF16)

    phase("yinter")
    before_id = jnp.where(one + dp > 0, final_id(dp - 1), -1).astype(F32)
    lane1 = lax.broadcasted_iota(jnp.int32, (128, 128), 1)
    low = lane1 < 64
    skip0 = jnp.where(low, skip_ref[0], skip_ref[1])
    skip1 = jnp.where(low, skip_ref[2], 0.0)
    og0 = og_ref[:, 0:128]
    og1 = jnp.concatenate([og_ref[:, 128:192], jnp.zeros((1, 64), F32)], axis=1)
    for q in range(4):
        r = 128 * q
        w = r + 128
        inter = dot_t(c_b[r:w, :], s_in[...])
        enters = jnp.where(idc[16 + r : 16 + w, :] == before_id, 1.0, 0.0)
        decay = jnp.exp(cols[r:w, :])
        e0 = jnp.broadcast_to(decay[:, 0:1], (128, 128))
        e1 = jnp.broadcast_to(decay[:, 1:2], (128, 128))
        e2 = jnp.broadcast_to(decay[:, 2:3], (128, 128))
        y0 = smask[r:w, 0:128] + enters * jnp.where(low, e0, e1) * inter[:, 0:128]
        y1 = smask[r:w, 128:256] + enters * e2 * inter[:, 128:256]
        y0 = y0 + skip0 * x_b[r:w, 0:128].astype(F32)
        y1 = y1 + skip1 * x_b[r:w, 128:256].astype(F32)
        z0 = u_buf[16 + r : 16 + w, 256:384]
        z1 = jnp.where(low, pltpu.roll(u_buf[16 + r : 16 + w, 128:256], 64, 1), 0.0)
        g0 = y0 * (z0 * jax.nn.sigmoid(z0))
        g1 = y1 * (z1 * jax.nn.sigmoid(z1))
        sq = jnp.sum(g0 * g0 + g1 * g1, axis=1, keepdims=True)
        hi = sq.astype(BF16).astype(F32)
        g_send[q, :, :, 0:128] = (g0 * og0).astype(BF16).reshape(4, 32, 128)
        g_send[q, :, :, 128:256] = jnp.where(
            low, g1 * og1, jnp.where(lane1 == 64, hi, jnp.where(lane1 == 65, sq - hi, 0.0))
        ).astype(BF16).reshape(4, 32, 128)
    for k in (2, 1, 3):
        yt = lax.rem(y + k, 4)
        send(A2A + k - 1, g_send.at[:, yt], a_rx.at[y], hdid(zl, yt))
    a_rx[y] = g_send[:, y]

    phase("tabx_wait")
    for k in range(1, 4):
        recv(TABX + k - 1, tabx.at[k - 1], dpid(mate))
    shared = x // 2 == 1 - zh
    for j in range(4):
        recv(TABC + 2 * j + lax.rem(x, 2), tabz.at[j], dpid(mate), shared)
    done = tabs[4 * zh + x].astype(F32)
    for k in range(3):
        done = done + tabx[k].astype(F32)
    for j in range(4):
        done = done + tabz[j].astype(F32)
    fin[dp // 2, pl.ds(my_half, 96), :] = done.astype(BF16)

    def f_rows(owner):
        return fin.at[owner // 2, pl.ds(pl.multiple_of(lax.rem(owner, 2) * 96, 96), 96), :]

    phase("fin_own")
    finals = Gather([(F_IDS, f_rows)])
    finals.own()

    phase("wo_finish")
    for k in (1, 3, 2):
        recv(WO_MATE + k - 1, wo_rows(y - k, 1 - c), dpid(mate))

    phase("a2a_wait")
    for k in range(1, 4):
        ys = lax.rem(y + 4 - k, 4)
        recv(A2A + k - 1, a_rx.at[ys], hdid(zl, ys))
    phase("outproj")
    sq = jnp.zeros((128, 1), F32)
    picked = (lane1 == 64) | (lane1 == 65)
    for y_ in range(4):
        tails = a_rx[y_, :, :, 128:256].reshape(128, 128).astype(F32)
        sq = sq + jnp.sum(jnp.where(picked, tails, 0.0), axis=1, keepdims=True)
    hi = sq.astype(BF16).astype(F32)
    tail = jnp.where(lane1 == 0, hi, jnp.where(lane1 == 1, sq - hi, 0.0))
    own_acc[:, D : D + 128] = tail
    part[:, :, D : D + 128] = tail.astype(BF16).reshape(4, 32, 128)
    for n in range(0, D, 256):
        acc = jnp.zeros((128, 256), F32)
        for y_ in range(4):
            acc = acc + dot(a_rx[y_, :, :, 0:FEAT].reshape(128, FEAT), wo[y_, :, n : n + 256])
        own_acc[:, n : n + 256] = acc
        part[:, :, n : n + 256] = acc.astype(BF16).reshape(4, 32, 256)
    for k in (2, 1, 3):
        zt = lax.rem(zl + k, 4)
        send(RSZ + k - 1, part.at[zt], rs_rx.at[k - 1], hdid(zt, y))

    phase("fin_near")
    finals.cross()
    phase("fin_cross")
    finals.near()
    phase("fin_nearrest")
    finals.near_rest()
    phase("fin_far")
    finals.far()
    phase("rsy_wait")
    for k in range(1, 4):
        recv(RSZ + k - 1, rs_rx.at[k - 1], hdid(lax.rem(zl + 4 - k, 4), y))
    phase("out")
    z_rows = pl.ds(pl.multiple_of(zl * 32, 32), 32)
    sq = own_acc[z_rows, D : D + 128]
    for k in range(3):
        sq = sq + rs_rx[k, :, D : D + 128].astype(F32)
    scale = lax.rsqrt(jnp.sum(sq, axis=1, keepdims=True) / (FEAT * HD) + EPSILON)
    acc = own_acc[z_rows, 0:D]
    for k in range(3):
        acc = acc + rs_rx[k, :, 0:D].astype(F32)
    resid = hid_ref[pl.ds(pl.multiple_of(hd * 32, 32), 32), :].astype(F32)
    out_ref[...] = (resid + scale * acc).astype(BF16)

    phase("st_out")
    for r in range(4):
        st_ref[r] = fin[req_ref[r]]

    phase("drain")
    for m, src, dst, to, cond in pending:
        if cond is None:
            msg(m, src, dst, to).wait_send()
        else:
            @pl.when(cond)
            def _():
                msg(m, src, dst, to).wait_send()
    phase(None)


def write_out(rows_ref, states_ref, out_ref, st_ref):
    out_ref[...] = rows_ref[...]
    st_ref[...] = states_ref[...].astype(F32)


def on_device(
    hidden, token_prompt, request_prompt, in_gain, w_zx, w_bc, w_dt, dt_bias, a_log, conv_x,
    conv_bc, skip_gain, out_gain, w_out,
):
    vmem = pl.BlockSpec(memory_space=pltpu.VMEM)
    smem = pl.BlockSpec(memory_space=pltpu.SMEM)
    layer_out, states = pl.pallas_call(
        body,
        out_shape=(
            jax.ShapeDtypeStruct((TOK // HD, D), BF16),
            jax.ShapeDtypeStruct((4, FEAT, NSTATE), BF16),
        ),
        in_specs=[smem] * 4 + [pl.BlockSpec(memory_space=pl.ANY)] * 10,
        out_specs=(vmem, vmem),
        scratch_shapes=[
            pltpu.VMEM((ROWS, 2, FEAT), F32),
            pltpu.VMEM((ROWS, 256), F32),
            pltpu.VMEM((HEADS, ROWS), F32),
            pltpu.VMEM((DP, 4, 128), jnp.int32),
            pltpu.VMEM((TOK, D), BF16),
            pltpu.VMEM((D,), F32),
            pltpu.VMEM((4, FEAT), F32),
            pltpu.VMEM((4, 256), F32),
            pltpu.VMEM((1, FEAT), F32),
            pltpu.VMEM((D, 384), BF16),
            pltpu.VMEM((ROWS, 384), F32),
            pltpu.VMEM((256, 128), F32),
            pltpu.VMEM((32, 128), F32),
            pltpu.VMEM((DP, 32, 128), BF16),
            pltpu.VMEM((D, 128), BF16),
            pltpu.VMEM((4, 4, 16, 640), BF16),
            pltpu.VMEM((16, D), BF16),
            pltpu.VMEM((EXT, D), BF16),
            pltpu.VMEM((EXT, 128), F32),
            pltpu.VMEM((EXT, 640), F32),
            pltpu.VMEM((8, 512), F32),
            pltpu.VMEM((FEAT, TOK), F32),
            pltpu.VMEM((TOK, 256), BF16),
            pltpu.VMEM((TOK, 128), BF16),
            pltpu.VMEM((TOK, 128), BF16),
            pltpu.VMEM((TOK, 128 * PROMPTS), BF16),
            pltpu.VMEM((16, 128), F32),
            pltpu.VMEM((8, 16, 128), F32),
            pltpu.VMEM((FEAT, NSTATE), BF16),
            pltpu.VMEM((4, FEAT, NSTATE), BF16),
            pltpu.VMEM((256, NSTATE), BF16),
            pltpu.VMEM((TOK, 128), F32),
            pltpu.VMEM((TOK, 256), F32),
            pltpu.VMEM((PROMPTS, FEAT, NSTATE), BF16),
            pltpu.VMEM((PROMPTS, 96, NSTATE), BF16),
            pltpu.VMEM((PROMPTS, 96, NSTATE), BF16),
            pltpu.VMEM((4, 96, NSTATE), BF16),
            pltpu.VMEM((3, 96, NSTATE), BF16),
            pltpu.VMEM((PROMPTS, FEAT, NSTATE), BF16),
            pltpu.VMEM((4, 4, 32, 256), BF16),
            pltpu.VMEM((4, 4, 32, 256), BF16),
            pltpu.VMEM((4, FEAT, D), BF16),
            pltpu.VMEM((4, 32, OUTW), BF16),
            pltpu.VMEM((128, OUTW), F32),
            pltpu.VMEM((3, 32, OUTW), BF16),
            pltpu.SemaphoreType.DMA((N_MSG,)),
            pltpu.SemaphoreType.DMA((N_MSG,)),
            pltpu.SemaphoreType.DMA((10,)),
        ],
        compiler_params=pltpu.CompilerParams(
            collective_id=0, has_side_effects=True, vmem_limit_bytes=60 * 2**20
        ),
        name="layer",
    )(
        request_prompt, dt_bias, a_log, skip_gain, w_zx, w_bc, w_dt.T,
        token_prompt.reshape(DP, 4, 128), hidden, in_gain, conv_x, conv_bc,
        out_gain.reshape(1, FEAT), w_out,
    )
    layer_out, states = pl.pallas_call(
        write_out,
        out_shape=(
            jax.ShapeDtypeStruct((TOK // HD, D), BF16),
            jax.ShapeDtypeStruct((4, FEAT, NSTATE), F32),
        ),
        in_specs=[vmem, vmem],
        out_specs=(vmem, vmem),
        name="write_out",
    )(layer_out, states)
    return layer_out, states.reshape(4, HEADS, 64, NSTATE)


def solution(mesh):
    in_specs = (
        P("dp", None), P(), P("dp"), P(), P("dp", None, "head"), P("dp", None), P("dp", "head"),
        P("head"), P("head"), P(None, "head"), P(), P("head"), P("head"), P("head", None),
    )
    out_specs = (P(("dp", "head"), None), P("dp", "head", None, None))
    return jax.shard_map(on_device, mesh=mesh, in_specs=in_specs, out_specs=out_specs, check_vma=False)
```

```python
import jax
import jax.numpy as jnp
from jax import lax
from jax.experimental import pallas as pl
from jax.experimental.pallas import tpu as pltpu
from jax.sharding import PartitionSpec as P

MESH = pl.DeviceIdType.MESH
F32 = jnp.float32
BF16 = jnp.bfloat16
EPSILON = 1e-05

DP = 16
HD = 16
D = 1536
TOK = 512
EXT = TOK + 16
ROWS = 96
HEADS = 3
FEAT = 192
NSTATE = 128
PROMPTS = 8
OUTW = D + 128

W_IDS = 0
T_IDS = 15
F_IDS = 30
HALO = 45
INFO_UP = 46
INFO_DN = 50
STATE = 54
WO = 58
WO_MATE = 61
TAB0 = 64
TABZ = 65
TABX = 66
A2A = 69
RSZ = 72
BCZ = 75
BCY = 78
TABC = 81
N_MSG = 89


def dot(a, b):
    return lax.dot_general(a, b, (((1,), (0,)), ((), ())), preferred_element_type=F32)


def dot_t(a, b):
    return lax.dot_general(a, b, (((1,), (1,)), ((), ())), preferred_element_type=F32)


def lane_cumsum(v):
    width = v.shape[1]
    lane = lax.broadcasted_iota(jnp.int32, v.shape, 1)
    step = 1
    while step < width:
        v = v + jnp.where(lane >= step, pltpu.roll(v, step, 1), 0.0)
        step *= 2
    return v


def run_end(v, ids):
    width = v.shape[1]
    lane = lax.broadcasted_iota(jnp.int32, v.shape, 1)
    step = 1
    while step < width:
        same = (pltpu.roll(ids, width - step, 1) == ids) & (lane < width - step)
        v = jnp.where(same, pltpu.roll(v, width - step, 1), v)
        step *= 2
    return v


SCOPE = []


def phase(name):
    if SCOPE:
        SCOPE.pop().__exit__(None, None, None)
    if name and TRACE:
        SCOPE.append(jax.named_scope(name))
        SCOPE[-1].__enter__()


TRACE = False


def body(
    req_ref, dtb_ref, alog_ref, skip_ref, wzx_in, wbc_in, wdt_in, ids_in, hid_in, gain_in,
    cx_in, cbc_in, og_in, wout_in, out_ref, st_ref,
    wzx_ref, wbc_ref, wdt_ref, ids_ref, hid_ref, gain_ref, cx_ref, cbc_ref, og_ref,
    w_buf, wst, bc_t, sm_t, small, wdt_mat, bc_parts, halo, nrm, idc, u_buf, taps, x_t, x_b, b_b, c_b, b_all,
    info_tx, info_rx, l_tx, l_rx, s_in, cols, smask, loc, tab0, tabs, tabz, tabx, fin,
    g_send, a_rx, wo, part, own_acc, rs_rx, send_sem, recv_sem, local_sem,
):
    dp = lax.axis_index("dp")
    hd = lax.axis_index("head")
    zh = dp // 8
    x = (dp // 2) % 4
    c = dp % 2
    zl = hd // 4
    y = hd % 4

    def dev(z_, x_, c_):
        return z_ * 8 + lax.rem(x_ + 8, 4) * 2 + c_

    across = dev(1 - zh, x, c)
    mate = dev(zh, x, 1 - c)

    def dpid(d):
        return {"dp": d}

    def hdid(z_, y_):
        return {"head": z_ * 4 + y_}

    def msg(m, src, dst, to):
        return pltpu.make_async_remote_copy(
            src_ref=src, dst_ref=dst, send_sem=send_sem.at[m], recv_sem=recv_sem.at[m],
            device_id=to, device_id_type=MESH,
        )

    pending = []

    def send(m, src, dst, to, cond=None):
        if cond is None:
            msg(m, src, dst, to).start()
        else:
            @pl.when(cond)
            def _():
                msg(m, src, dst, to).start()
        pending.append((m, src, dst, to, cond))

    def recv(m, dst, to, cond=None):
        if cond is None:
            msg(m, dst, dst, to).wait_recv()
        else:
            @pl.when(cond)
            def _():
                msg(m, dst, dst, to).wait_recv()

    class Gather:
        def __init__(self, families):
            self.families = families

        def send(self, k, owner, to):
            for base, ref_of in self.families:
                r = ref_of(owner)
                send(base + k, r, r, dpid(to))

        def recv(self, k, owner):
            for base, ref_of in self.families:
                recv(base + k, ref_of(owner), dpid(mate))

        def own(self):
            self.send(3, dp, across)
            self.send(2, dp, dev(zh, x + 2, c))
            self.send(0, dp, dev(zh, x + 1, c))
            self.send(1, dp, dev(zh, x - 1, c))
            self.send(7, dp, mate)

        def cross(self):
            o = 1 - zh
            self.recv(3, dev(o, x, c))
            self.send(6, dev(o, x, c), dev(zh, x + 2, c))
            self.send(4, dev(o, x, c), dev(zh, x + 1, c))
            self.send(5, dev(o, x, c), dev(zh, x - 1, c))
            self.send(11, dev(o, x, c), mate)

        def near(self):
            for k, step in ((0, -1), (1, 1), (2, 2)):
                self.recv(k, dev(zh, x + step, c))
                self.send(8 + k, dev(zh, x + step, c), mate)

        def near_rest(self):
            for k, step in ((7, 0), (8, -1), (9, 1), (10, 2)):
                self.recv(k, dev(zh, x + step, 1 - c))

        def far(self):
            o = 1 - zh
            for k, step in ((4, -1), (5, 1), (6, 2)):
                self.recv(k, dev(o, x + step, c))
                self.send(8 + k, dev(o, x + step, c), mate)
            for k, step in ((11, 0), (12, -1), (13, 1), (14, 2)):
                self.recv(k, dev(o, x + step, 1 - c))

    phase("entry")
    barrier = pltpu.get_barrier_semaphore()
    for k in range(1, DP):
        pl.semaphore_signal(
            barrier, inc=1, device_id=dpid(lax.rem(dp + k, DP)), device_id_type=MESH
        )
    for k in range(1, 4):
        pl.semaphore_signal(
            barrier, inc=1, device_id=hdid(zl, lax.rem(y + k, 4)), device_id_type=MESH
        )
        pl.semaphore_signal(
            barrier, inc=1, device_id=hdid(lax.rem(zl + k, 4), y), device_id_type=MESH
        )

    loads = [
        pltpu.make_async_copy(src, dst, local_sem.at[i])
        for i, (src, dst) in enumerate(
            [
                (wzx_in, wzx_ref), (wbc_in, wbc_ref), (wdt_in, wdt_ref), (ids_in, ids_ref),
                (hid_in, hid_ref), (gain_in, gain_ref), (cx_in, cx_ref), (cbc_in, cbc_ref),
                (og_in, og_ref), (wout_in, wo.at[y]),
            ]
        )
    ]
    for load in loads:
        load.start()

    for load in loads[0:3]:
        load.wait()
    bc_t[:, 0:ROWS] = jnp.concatenate([wbc_ref[...], jnp.zeros((32, 256), F32)], axis=0).T[:, 0:ROWS]
    sm_t[...] = jnp.zeros((32, 128), F32)
    sm_t[0:16, 0:ROWS] = bc_t[pl.ds(pl.multiple_of(hd * 16, 16), 16), 0:ROWS]
    sm_t[16:19, 0:ROWS] = wdt_ref[...]
    small[dp] = sm_t[...].astype(BF16)
    zw = wzx_ref[:, 0, :]
    xw = wzx_ref[:, 1, :]
    wst[:, 0:128] = xw[:, 0:128]
    wst[:, 128:256] = jnp.concatenate([xw[:, 128:192], zw[:, 128:192]], axis=1)
    wst[:, 256:384] = zw[:, 0:128]
    own_rows = pl.multiple_of(dp * ROWS, ROWS)
    w_buf[pl.ds(own_rows, ROWS), :] = wst[...].astype(BF16)

    def w_rows(owner):
        return w_buf.at[pl.ds(pl.multiple_of(owner * ROWS, ROWS), ROWS), :]

    weights = Gather([(W_IDS, w_rows)])

    @pl.when(dp == 0)
    def _():
        halo[...] = jnp.zeros_like(halo)

    @pl.when(x // 2 == zh)
    def _():
        tabz[...] = jnp.zeros_like(tabz)

    for j in range(4):
        @pl.when(dp < j + 1)
        def _():
            info_rx[j] = jnp.zeros((16, 128), F32)
            l_rx[j] = jnp.zeros((FEAT, NSTATE), BF16)

        @pl.when(dp + j + 1 > DP - 1)
        def _():
            info_rx[4 + j] = jnp.zeros((16, 128), F32)

    pl.semaphore_wait(barrier, DP - 1 + 6)

    for k in (8, 7, 9, 6, 10, 5, 11, 12, 4, 13, 3, 14, 2, 15, 1):
        send(T_IDS + k - 1, small.at[dp], small.at[dp], dpid(lax.rem(dp + k, DP)))
    weights.own()
    for load in loads[3:9]:
        load.wait()
    send(HALO, hid_ref.at[pl.ds(TOK - 16, 16), :], halo, dpid(lax.rem(dp + 1, DP)), dp < DP - 1)

    phase("ids")
    def wo_rows(y_, c_):
        return wo.at[lax.rem(y_ + 4, 4), pl.ds(pl.multiple_of(c_ * 96, 96), 96), :]

    own_ids = ids_ref[dp].astype(F32)
    prev_ids = ids_ref[jnp.maximum(dp - 1, 0)].astype(F32)
    prev_col = jnp.broadcast_to(prev_ids[3:4, :], (128, 128)).T[112:128, :]
    first_dev = jnp.zeros((16, 128), jnp.int32) + dp == 0
    idc[0:16, :] = jnp.where(first_dev, -1.0, prev_col)
    for q in range(4):
        idc[16 + 128 * q : 144 + 128 * q, :] = jnp.broadcast_to(own_ids[q : q + 1, :], (128, 128)).T
    id_row = jnp.concatenate([own_ids[q : q + 1, :] for q in range(4)], axis=1)

    taps[...] = jnp.zeros_like(taps)
    taps[0:4, 0:128] = cx_ref[:, 0:128]
    taps[0:4, 128:192] = cx_ref[:, 128:192]
    taps[0:4, 256:512] = cbc_ref[...]

    phase("norm")
    gain = gain_ref[...].reshape(1, D)

    def norm_rows(rows):
        h = rows.astype(F32)
        scale = lax.rsqrt(jnp.mean(h * h, axis=1, keepdims=True) + EPSILON)
        return (h * scale * gain).astype(BF16)

    def norm_step(i, carry):
        r = pl.multiple_of(i * 32, 32)
        nrm[pl.ds(pl.multiple_of(16 + r, 16), 32), :] = norm_rows(hid_ref[pl.ds(r, 32), :])
        return carry

    lax.fori_loop(0, TOK // 32, norm_step, 0)
    phase("halo_wait")
    recv(HALO, halo, dpid(mate), dp > 0)
    nrm[0:16, :] = norm_rows(halo[...])

    phase("w_near")
    phase("dt")
    for k in range(1, DP):
        owner = lax.rem(dp + DP - k, DP)
        recv(T_IDS + k - 1, small.at[owner], dpid(owner))
    for j in range(DP):
        rows = jnp.concatenate([small[j].astype(F32), jnp.zeros((96, 128), F32)], axis=0).T
        wdt_mat[ROWS * j : ROWS * j + ROWS, :] = rows[0:ROWS, :].astype(BF16)
    bc_cols = dot(nrm[...], wdt_mat[...])
    bc_rows = jnp.concatenate([bc_cols[16:EXT, :].T, bc_cols[0:128, :].T], axis=1)
    bc_parts[y, zl] = bc_rows[0:16, :].astype(BF16)
    for k in (2, 1, 3):
        zt = lax.rem(zl + k, 4)
        send(BCZ + k - 1, bc_parts.at[y, zl], bc_parts.at[y, zl], hdid(zt, y))
    dt_rows = bc_rows[16:24, 0:TOK].astype(BF16).astype(F32)
    sub = lax.broadcasted_iota(jnp.int32, (8, TOK), 0)
    lane = lax.broadcasted_iota(jnp.int32, (8, TOK), 1)

    def by_head(ref, s):
        return jnp.where(s == 0, ref[0], jnp.where(s == 1, ref[1], ref[2]))

    pre = dt_rows + by_head(dtb_ref, sub)
    step_rows = jnp.maximum(pre, 0.0) + jnp.log1p(jnp.exp(-jnp.abs(pre)))
    rate_rows = -step_rows * jnp.exp(by_head(alog_ref, sub))
    prefix = lane_cumsum(rate_rows)
    id8 = jnp.broadcast_to(id_row, (8, TOK))
    at_end = run_end(prefix, id8)
    first_end = at_end[:, 0:1]
    total = prefix[:, TOK - 1 : TOK]
    info_tx[0:8, :] = jnp.broadcast_to(first_end, (8, 128))
    info_tx[8:16, :] = jnp.broadcast_to(total, (8, 128))
    for j in range(4):
        send(INFO_UP + j, info_tx, info_rx.at[j], dpid(lax.rem(dp + j + 1, DP)), dp + j + 1 < DP)
        send(INFO_DN + j, info_tx, info_rx.at[4 + j], dpid(lax.rem(dp - j - 1 + DP, DP)), dp >= j + 1)

    to_end = jnp.exp(at_end - prefix) * step_rows
    cols[...] = jnp.concatenate([prefix, jnp.zeros((120, TOK), F32)], axis=0).T

    phase("w_cross")
    weights.cross()
    phase("bcz")
    for k in range(1, 4):
        zs = lax.rem(zl + 4 - k, 4)
        recv(BCZ + k - 1, bc_parts.at[y, zs], hdid(zs, y))
    for k in (2, 1, 3):
        send(BCY + k - 1, bc_parts.at[y], bc_parts.at[y], hdid(zl, lax.rem(y + k, 4)))

    def wo_rows(y_, c_):
        return wo.at[lax.rem(y_ + 4, 4), pl.ds(pl.multiple_of(c_ * 96, 96), 96), :]

    loads[9].wait()
    for k in (1, 3, 2):
        send(WO + k - 1, wo_rows(y, c), wo_rows(y, c), hdid(zl, lax.rem(y + k, 4)))

    phase("w_near_rest")
    weights.near()
    weights.near_rest()
    phase("mm1")
    k_half = D // 2
    k_own = pl.multiple_of(zh * k_half, k_half)
    k_far = pl.multiple_of((1 - zh) * k_half, k_half)
    for n in range(0, 384, 128):
        u_buf[:, n : n + 128] = dot(nrm[:, pl.ds(k_own, k_half)], w_buf[pl.ds(k_own, k_half), n : n + 128])

    phase("bc_wait")
    for k in range(1, 4):
        ys = lax.rem(y + 4 - k, 4)
        recv(BCY + k - 1, bc_parts.at[ys], hdid(zl, ys))
    for half in range(2):
        rows = jnp.concatenate(
            [bc_parts[h % 4, h // 4].astype(F32) for h in range(8 * half, 8 * half + 8)], axis=0
        )
        col = 384 + 128 * half
        u_buf[0:16, col : col + 128] = rows[:, TOK : TOK + 128].T[0:16, :]
        u_buf[16:EXT, col : col + 128] = rows[:, 0:TOK].T

    phase("w_far")
    weights.far()
    phase("mm2")
    for n in range(0, 384, 128):
        u_buf[:, n : n + 128] += dot(nrm[:, pl.ds(k_far, k_half)], w_buf[pl.ds(k_far, k_half), n : n + 128])

    phase("conv")
    for r in range(0, EXT, 176):
        u_buf[r : r + 176, 0:384] = u_buf[r : r + 176, 0:384].astype(BF16).astype(F32)

    for q in range(4):
        r = 128 * q
        now = idc[16 + r : 144 + r, :]
        same = [jnp.where(idc[13 + k + r : 141 + k + r, :] == now, 1.0, 0.0) for k in range(3)]

        def conv(col, tap):
            acc = taps[3:4, tap : tap + 128] * u_buf[16 + r : 144 + r, col : col + 128]
            for k in range(3):
                acc = acc + same[k] * (
                    taps[k : k + 1, tap : tap + 128] * u_buf[13 + k + r : 141 + k + r, col : col + 128]
                )
            return (acc * jax.nn.sigmoid(acc)).astype(BF16)

        x0 = conv(0, 0)
        x1 = conv(128, 128)
        x_b[r : r + 128, 0:128] = x0
        x_b[r : r + 128, 128:256] = x1
        x_t[0:128, r : r + 128] = x0.astype(F32).T
        x_t[128:192, r : r + 128] = x1.astype(F32).T[0:64, :]
        b_b[r : r + 128, :] = conv(384, 256)
        c_b[r : r + 128, :] = conv(512, 384)

    phase("lstate")
    last_id = id_row[:, TOK - 1 : TOK]
    is_last = id8 == jnp.broadcast_to(last_id, (8, TOK))

    def weighted_x(weight):
        return jnp.concatenate(
            [x_t[64 * h : 64 * h + 64, :] * weight[h : h + 1, :] for h in range(HEADS)], axis=0
        ).astype(BF16)

    phase("table_loc")
    def first_id(k):
        return ids_ref[jnp.clip(k, 0, DP - 1)][0:1, 0:1]

    def final_id(k):
        return ids_ref[jnp.clip(k, 0, DP - 1)][3:4, 127:128]

    one = jnp.zeros((1, 1), jnp.int32)
    for j in range(4):
        recv(INFO_DN + j, info_rx.at[4 + j], dpid(mate), dp + j + 1 < DP)
    after = jnp.zeros((8, 128), F32)
    for j in range(4):
        goes_on = (first_id(dp + j + 1) == final_id(dp)) & (one + dp + j + 1 < DP)
        after = after + jnp.where(goes_on, info_rx[4 + j, 0:8, :], 0.0)
    carry_on = jnp.broadcast_to(jnp.exp(after)[:, 0:1], (8, TOK))
    xw_end = weighted_x(to_end * jnp.where(is_last, carry_on, 1.0))
    for g in range(PROMPTS):
        mine = jnp.where(idc[16:EXT, :] == float(g), 1.0, 0.0).astype(BF16)
        b_all[:, 128 * g : 128 * g + 128] = b_b[...] * mine
    for g in range(PROMPTS):
        loc[g] = dot(xw_end, b_all[:, 128 * g : 128 * g + 128]).astype(BF16)
    mate_half = pl.multiple_of((1 - c) * 96, 96)
    send(TAB0, loc.at[:, pl.ds(mate_half, 96), :], tab0, dpid(mate))

    l_tx[...] = dot(weighted_x(jnp.where(is_last, to_end, 0.0)), b_b[...]).astype(BF16)
    for j in range(4):
        send(STATE + j, l_tx, l_rx.at[j], dpid(lax.rem(dp + j + 1, DP)), dp + j + 1 < DP)

    phase("scores")
    scol = lax.broadcasted_iota(jnp.int32, (128, TOK), 1)
    srow = lax.broadcasted_iota(jnp.int32, (128, TOK), 0)
    for q in range(4):
        r = 128 * q
        w = r + 128
        scores = dot_t(c_b[r:w, :], b_b[0:w, :])
        ok = (jnp.broadcast_to(idc[16 + r : 16 + w, 0:1], (128, w)) == jnp.broadcast_to(id_row[:, 0:w], (128, w))) & (
            scol[:, 0:w] <= srow[:, 0:w] + r
        )
        scores = jnp.where(ok, scores, 0.0)
        parts = []
        for h in range(HEADS):
            gap = jnp.broadcast_to(cols[r:w, h : h + 1], (128, w)) - prefix[h : h + 1, 0:w]
            mix = (scores * (jnp.exp(jnp.minimum(gap, 0.0)) * step_rows[h : h + 1, 0:w])).astype(BF16)
            col = 0 if h < 2 else 128
            parts.append(dot(mix, x_b[0:w, col : col + 128]))
        low = lax.broadcasted_iota(jnp.int32, (128, 128), 1) < 64
        smask[r:w, 0:128] = jnp.where(low, parts[0], parts[1])
        smask[r:w, 128:256] = parts[2]

    phase("tab0_wait")
    my_half = pl.multiple_of(c * 96, 96)
    recv(TAB0, tab0, dpid(mate))
    for g in range(PROMPTS):
        tabs[g] = (loc[g, pl.ds(my_half, 96), :].astype(F32) + tab0[g].astype(F32)).astype(BF16)
    for t in range(2):
        send(TABC + 2 * x + t, tabs.at[4 - 2 * zh + t], tabz.at[x], dpid(dev(1 - zh, 2 * zh + t, c)))
    for k in (2, 1, 3):
        xt = lax.rem(x + k, 4)
        send(TABX + k - 1, tabs.at[4 * zh + xt], tabx.at[k - 1], dpid(dev(zh, xt, c)))

    phase("wo_mate")
    for k in (1, 3, 2):
        recv(WO + k - 1, wo_rows(y - k, c), dpid(mate))
        send(WO_MATE + k - 1, wo_rows(y - k, c), wo_rows(y - k, c), dpid(mate))
    phase("state_wait")
    for j in range(4):
        recv(INFO_UP + j, info_rx.at[j], dpid(mate), dp >= j + 1)
        recv(STATE + j, l_rx.at[j], dpid(mate), dp >= j + 1)
    state = l_rx[3].astype(F32)
    for j in (2, 1, 0):
        joined = (final_id(dp - j - 1) == final_id(dp - j - 2)) & (one + dp - j - 2 >= 0)
        gain_j = jnp.where(joined, jnp.exp(info_rx[j, 8:16, :]), 0.0)
        rows = jnp.concatenate(
            [jnp.broadcast_to(gain_j[h : h + 1, :], (64, 128)) for h in range(HEADS)], axis=0
        )
        state = l_rx[j].astype(F32) + rows * state
    s_in[0:FEAT, :] = state.astype(BF16)
    s_in[FEAT:256, :] = jnp.zeros((64, NSTATE), BF16)

    phase("yinter")
    before_id = jnp.where(one + dp > 0, final_id(dp - 1), -1).astype(F32)
    lane1 = lax.broadcasted_iota(jnp.int32, (128, 128), 1)
    low = lane1 < 64
    skip0 = jnp.where(low, skip_ref[0], skip_ref[1])
    skip1 = jnp.where(low, skip_ref[2], 0.0)
    og0 = og_ref[:, 0:128]
    og1 = jnp.concatenate([og_ref[:, 128:192], jnp.zeros((1, 64), F32)], axis=1)
    for q in range(4):
        r = 128 * q
        w = r + 128
        inter = dot_t(c_b[r:w, :], s_in[...])
        enters = jnp.where(idc[16 + r : 16 + w, :] == before_id, 1.0, 0.0)
        decay = jnp.exp(cols[r:w, :])
        e0 = jnp.broadcast_to(decay[:, 0:1], (128, 128))
        e1 = jnp.broadcast_to(decay[:, 1:2], (128, 128))
        e2 = jnp.broadcast_to(decay[:, 2:3], (128, 128))
        y0 = smask[r:w, 0:128] + enters * jnp.where(low, e0, e1) * inter[:, 0:128]
        y1 = smask[r:w, 128:256] + enters * e2 * inter[:, 128:256]
        y0 = y0 + skip0 * x_b[r:w, 0:128].astype(F32)
        y1 = y1 + skip1 * x_b[r:w, 128:256].astype(F32)
        z0 = u_buf[16 + r : 16 + w, 256:384]
        z1 = jnp.where(low, pltpu.roll(u_buf[16 + r : 16 + w, 128:256], 64, 1), 0.0)
        g0 = y0 * (z0 * jax.nn.sigmoid(z0))
        g1 = y1 * (z1 * jax.nn.sigmoid(z1))
        sq = jnp.sum(g0 * g0 + g1 * g1, axis=1, keepdims=True)
        hi = sq.astype(BF16).astype(F32)
        g_send[q, :, :, 0:128] = (g0 * og0).astype(BF16).reshape(4, 32, 128)
        g_send[q, :, :, 128:256] = jnp.where(
            low, g1 * og1, jnp.where(lane1 == 64, hi, jnp.where(lane1 == 65, sq - hi, 0.0))
        ).astype(BF16).reshape(4, 32, 128)
    for k in (2, 1, 3):
        yt = lax.rem(y + k, 4)
        send(A2A + k - 1, g_send.at[:, yt], a_rx.at[y], hdid(zl, yt))
    a_rx[y] = g_send[:, y]

    phase("tabx_wait")
    for k in range(1, 4):
        recv(TABX + k - 1, tabx.at[k - 1], dpid(mate))
    shared = x // 2 == 1 - zh
    for j in range(4):
        recv(TABC + 2 * j + lax.rem(x, 2), tabz.at[j], dpid(mate), shared)
    done = tabs[4 * zh + x].astype(F32)
    for k in range(3):
        done = done + tabx[k].astype(F32)
    for j in range(4):
        done = done + tabz[j].astype(F32)
    fin[dp // 2, pl.ds(my_half, 96), :] = done.astype(BF16)

    def f_rows(owner):
        return fin.at[owner // 2, pl.ds(pl.multiple_of(lax.rem(owner, 2) * 96, 96), 96), :]

    phase("fin_own")
    finals = Gather([(F_IDS, f_rows)])
    finals.own()

    phase("wo_finish")
    for k in (1, 3, 2):
        recv(WO_MATE + k - 1, wo_rows(y - k, 1 - c), dpid(mate))

    phase("a2a_wait")
    for k in range(1, 4):
        ys = lax.rem(y + 4 - k, 4)
        recv(A2A + k - 1, a_rx.at[ys], hdid(zl, ys))
    phase("outproj")
    sq = jnp.zeros((128, 1), F32)
    picked = (lane1 == 64) | (lane1 == 65)
    for y_ in range(4):
        tails = a_rx[y_, :, :, 128:256].reshape(128, 128).astype(F32)
        sq = sq + jnp.sum(jnp.where(picked, tails, 0.0), axis=1, keepdims=True)
    hi = sq.astype(BF16).astype(F32)
    tail = jnp.where(lane1 == 0, hi, jnp.where(lane1 == 1, sq - hi, 0.0))
    own_acc[:, D : D + 128] = tail
    part[:, :, D : D + 128] = tail.astype(BF16).reshape(4, 32, 128)
    for n in range(0, D, 256):
        acc = jnp.zeros((128, 256), F32)
        for y_ in range(4):
            acc = acc + dot(a_rx[y_, :, :, 0:FEAT].reshape(128, FEAT), wo[y_, :, n : n + 256])
        own_acc[:, n : n + 256] = acc
        part[:, :, n : n + 256] = acc.astype(BF16).reshape(4, 32, 256)
    for k in (2, 1, 3):
        zt = lax.rem(zl + k, 4)
        send(RSZ + k - 1, part.at[zt], rs_rx.at[k - 1], hdid(zt, y))

    phase("fin_near")
    finals.cross()
    phase("fin_cross")
    finals.near()
    phase("fin_nearrest")
    finals.near_rest()
    phase("fin_far")
    finals.far()
    phase("rsy_wait")
    for k in range(1, 4):
        recv(RSZ + k - 1, rs_rx.at[k - 1], hdid(lax.rem(zl + 4 - k, 4), y))
    phase("out")
    z_rows = pl.ds(pl.multiple_of(zl * 32, 32), 32)
    sq = own_acc[z_rows, D : D + 128]
    for k in range(3):
        sq = sq + rs_rx[k, :, D : D + 128].astype(F32)
    scale = lax.rsqrt(jnp.sum(sq, axis=1, keepdims=True) / (FEAT * HD) + EPSILON)
    acc = own_acc[z_rows, 0:D]
    for k in range(3):
        acc = acc + rs_rx[k, :, 0:D].astype(F32)
    resid = hid_ref[pl.ds(pl.multiple_of(hd * 32, 32), 32), :].astype(F32)
    out_ref[...] = (resid + scale * acc).astype(BF16)

    phase("st_out")
    for r in range(4):
        st_ref[r] = fin[req_ref[r]]

    phase("drain")
    for m, src, dst, to, cond in pending:
        if cond is None:
            msg(m, src, dst, to).wait_send()
        else:
            @pl.when(cond)
            def _():
                msg(m, src, dst, to).wait_send()
    phase(None)


def write_out(rows_ref, states_ref, out_ref, st_ref):
    out_ref[...] = rows_ref[...]
    st_ref[...] = states_ref[...].astype(F32)


def on_device(
    hidden, token_prompt, request_prompt, in_gain, w_zx, w_bc, w_dt, dt_bias, a_log, conv_x,
    conv_bc, skip_gain, out_gain, w_out,
):
    vmem = pl.BlockSpec(memory_space=pltpu.VMEM)
    smem = pl.BlockSpec(memory_space=pltpu.SMEM)
    layer_out, states = pl.pallas_call(
        body,
        out_shape=(
            jax.ShapeDtypeStruct((TOK // HD, D), BF16),
            jax.ShapeDtypeStruct((4, FEAT, NSTATE), BF16),
        ),
        in_specs=[smem] * 4 + [pl.BlockSpec(memory_space=pl.ANY)] * 10,
        out_specs=(vmem, vmem),
        scratch_shapes=[
            pltpu.VMEM((ROWS, 2, FEAT), F32),
            pltpu.VMEM((ROWS, 256), F32),
            pltpu.VMEM((HEADS, ROWS), F32),
            pltpu.VMEM((DP, 4, 128), jnp.int32),
            pltpu.VMEM((TOK, D), BF16),
            pltpu.VMEM((D,), F32),
            pltpu.VMEM((4, FEAT), F32),
            pltpu.VMEM((4, 256), F32),
            pltpu.VMEM((1, FEAT), F32),
            pltpu.VMEM((D, 384), BF16),
            pltpu.VMEM((ROWS, 384), F32),
            pltpu.VMEM((256, 128), F32),
            pltpu.VMEM((32, 128), F32),
            pltpu.VMEM((DP, 32, 128), BF16),
            pltpu.VMEM((D, 128), BF16),
            pltpu.VMEM((4, 4, 16, 640), BF16),
            pltpu.VMEM((16, D), BF16),
            pltpu.VMEM((EXT, D), BF16),
            pltpu.VMEM((EXT, 128), F32),
            pltpu.VMEM((EXT, 640), F32),
            pltpu.VMEM((8, 512), F32),
            pltpu.VMEM((FEAT, TOK), F32),
            pltpu.VMEM((TOK, 256), BF16),
            pltpu.VMEM((TOK, 128), BF16),
            pltpu.VMEM((TOK, 128), BF16),
            pltpu.VMEM((TOK, 128 * PROMPTS), BF16),
            pltpu.VMEM((16, 128), F32),
            pltpu.VMEM((8, 16, 128), F32),
            pltpu.VMEM((FEAT, NSTATE), BF16),
            pltpu.VMEM((4, FEAT, NSTATE), BF16),
            pltpu.VMEM((256, NSTATE), BF16),
            pltpu.VMEM((TOK, 128), F32),
            pltpu.VMEM((TOK, 256), F32),
            pltpu.VMEM((PROMPTS, FEAT, NSTATE), BF16),
            pltpu.VMEM((PROMPTS, 96, NSTATE), BF16),
            pltpu.VMEM((PROMPTS, 96, NSTATE), BF16),
            pltpu.VMEM((4, 96, NSTATE), BF16),
            pltpu.VMEM((3, 96, NSTATE), BF16),
            pltpu.VMEM((PROMPTS, FEAT, NSTATE), BF16),
            pltpu.VMEM((4, 4, 32, 256), BF16),
            pltpu.VMEM((4, 4, 32, 256), BF16),
            pltpu.VMEM((4, FEAT, D), BF16),
            pltpu.VMEM((4, 32, OUTW), BF16),
            pltpu.VMEM((128, OUTW), F32),
            pltpu.VMEM((3, 32, OUTW), BF16),
            pltpu.SemaphoreType.DMA((N_MSG,)),
            pltpu.SemaphoreType.DMA((N_MSG,)),
            pltpu.SemaphoreType.DMA((10,)),
        ],
        compiler_params=pltpu.CompilerParams(
            collective_id=0, has_side_effects=True, vmem_limit_bytes=60 * 2**20
        ),
        name="layer",
    )(
        request_prompt, dt_bias, a_log, skip_gain, w_zx, w_bc, w_dt.T,
        token_prompt.reshape(DP, 4, 128), hidden, in_gain, conv_x, conv_bc,
        out_gain.reshape(1, FEAT), w_out,
    )
    layer_out, states = pl.pallas_call(
        write_out,
        out_shape=(
            jax.ShapeDtypeStruct((TOK // HD, D), BF16),
            jax.ShapeDtypeStruct((4, FEAT, NSTATE), F32),
        ),
        in_specs=[vmem, vmem],
        out_specs=(vmem, vmem),
        name="write_out",
    )(layer_out, states)
    return layer_out, states.reshape(4, HEADS, 64, NSTATE)


def solution(mesh):
    in_specs = (
        P("dp", None), P(), P("dp"), P(), P("dp", None, "head"), P("dp", None), P("dp", "head"),
        P("head"), P("head"), P(None, "head"), P(), P("head"), P("head"), P("head", None),
    )
    out_specs = (P(("dp", "head"), None), P("dp", "head", None, None))
    return jax.shard_map(on_device, mesh=mesh, in_specs=in_specs, out_specs=out_specs, check_vma=False)
```

```python
import jax
import jax.numpy as jnp
from jax import lax
from jax.experimental import pallas as pl
from jax.experimental.pallas import tpu as pltpu
from jax.sharding import PartitionSpec as P

MESH = pl.DeviceIdType.MESH
F32 = jnp.float32
BF16 = jnp.bfloat16
EPSILON = 1e-05

DP = 16
HD = 16
D = 1536
TOK = 512
EXT = TOK + 16
ROWS = 96
HEADS = 3
FEAT = 192
NSTATE = 128
PROMPTS = 8
OUTW = D + 128

W_IDS = 0
T_IDS = 15
F_IDS = 30
HALO = 45
INFO_UP = 46
INFO_DN = 50
STATE = 54
WO = 58
WO_MATE = 61
TAB0 = 64
TABZ = 65
TABX = 66
A2A = 69
RSZ = 72
BCZ = 75
BCY = 78
TABC = 81
N_MSG = 89


def dot(a, b):
    return lax.dot_general(a, b, (((1,), (0,)), ((), ())), preferred_element_type=F32)


def dot_t(a, b):
    return lax.dot_general(a, b, (((1,), (1,)), ((), ())), preferred_element_type=F32)


def lane_cumsum(v):
    width = v.shape[1]
    lane = lax.broadcasted_iota(jnp.int32, v.shape, 1)
    step = 1
    while step < width:
        v = v + jnp.where(lane >= step, pltpu.roll(v, step, 1), 0.0)
        step *= 2
    return v


def run_end(v, ids):
    width = v.shape[1]
    lane = lax.broadcasted_iota(jnp.int32, v.shape, 1)
    step = 1
    while step < width:
        same = (pltpu.roll(ids, width - step, 1) == ids) & (lane < width - step)
        v = jnp.where(same, pltpu.roll(v, width - step, 1), v)
        step *= 2
    return v


SCOPE = []


def phase(name):
    if SCOPE:
        SCOPE.pop().__exit__(None, None, None)
    if name and TRACE:
        SCOPE.append(jax.named_scope(name))
        SCOPE[-1].__enter__()


TRACE = False


def body(
    req_ref, dtb_ref, alog_ref, skip_ref, wzx_in, wbc_in, wdt_in, ids_in, hid_in, gain_in,
    cx_in, cbc_in, og_in, wout_in, out_ref, st_ref,
    wzx_ref, wbc_ref, wdt_ref, ids_ref, hid_ref, gain_ref, cx_ref, cbc_ref, og_ref,
    w_buf, wst, bc_t, sm_t, small, wdt_mat, bc_parts, halo, nrm, idc, u_buf, taps, x_t, x_b, b_b, c_b, b_all,
    info_tx, info_rx, l_tx, l_rx, s_in, cols, smask, loc, tab0, tabs, tabz, tabx, fin,
    g_send, a_rx, wo, part, own_acc, rs_rx, send_sem, recv_sem, local_sem,
):
    dp = lax.axis_index("dp")
    hd = lax.axis_index("head")
    zh = dp // 8
    x = (dp // 2) % 4
    c = dp % 2
    zl = hd // 4
    y = hd % 4

    def dev(z_, x_, c_):
        return z_ * 8 + lax.rem(x_ + 8, 4) * 2 + c_

    across = dev(1 - zh, x, c)
    mate = dev(zh, x, 1 - c)

    def dpid(d):
        return {"dp": d}

    def hdid(z_, y_):
        return {"head": z_ * 4 + y_}

    def msg(m, src, dst, to):
        return pltpu.make_async_remote_copy(
            src_ref=src, dst_ref=dst, send_sem=send_sem.at[m], recv_sem=recv_sem.at[m],
            device_id=to, device_id_type=MESH,
        )

    pending = []

    def send(m, src, dst, to, cond=None):
        if cond is None:
            msg(m, src, dst, to).start()
        else:
            @pl.when(cond)
            def _():
                msg(m, src, dst, to).start()
        pending.append((m, src, dst, to, cond))

    def recv(m, dst, to, cond=None):
        if cond is None:
            msg(m, dst, dst, to).wait_recv()
        else:
            @pl.when(cond)
            def _():
                msg(m, dst, dst, to).wait_recv()

    class Gather:
        def __init__(self, families):
            self.families = families

        def send(self, k, owner, to):
            for base, ref_of in self.families:
                r = ref_of(owner)
                send(base + k, r, r, dpid(to))

        def recv(self, k, owner):
            for base, ref_of in self.families:
                recv(base + k, ref_of(owner), dpid(mate))

        def own(self):
            self.send(3, dp, across)
            self.send(2, dp, dev(zh, x + 2, c))
            self.send(0, dp, dev(zh, x + 1, c))
            self.send(1, dp, dev(zh, x - 1, c))
            self.send(7, dp, mate)

        def cross(self):
            o = 1 - zh
            self.recv(3, dev(o, x, c))
            self.send(6, dev(o, x, c), dev(zh, x + 2, c))
            self.send(4, dev(o, x, c), dev(zh, x + 1, c))
            self.send(5, dev(o, x, c), dev(zh, x - 1, c))
            self.send(11, dev(o, x, c), mate)

        def near(self):
            for k, step in ((0, -1), (1, 1), (2, 2)):
                self.recv(k, dev(zh, x + step, c))
                self.send(8 + k, dev(zh, x + step, c), mate)

        def near_rest(self):
            for k, step in ((7, 0), (8, -1), (9, 1), (10, 2)):
                self.recv(k, dev(zh, x + step, 1 - c))

        def far(self):
            o = 1 - zh
            for k, step in ((4, -1), (5, 1), (6, 2)):
                self.recv(k, dev(o, x + step, c))
                self.send(8 + k, dev(o, x + step, c), mate)
            for k, step in ((11, 0), (12, -1), (13, 1), (14, 2)):
                self.recv(k, dev(o, x + step, 1 - c))

    phase("entry")
    barrier = pltpu.get_barrier_semaphore()
    for k in range(1, DP):
        pl.semaphore_signal(
            barrier, inc=1, device_id=dpid(lax.rem(dp + k, DP)), device_id_type=MESH
        )
    for k in range(1, 4):
        pl.semaphore_signal(
            barrier, inc=1, device_id=hdid(zl, lax.rem(y + k, 4)), device_id_type=MESH
        )
        pl.semaphore_signal(
            barrier, inc=1, device_id=hdid(lax.rem(zl + k, 4), y), device_id_type=MESH
        )

    loads = [
        pltpu.make_async_copy(src, dst, local_sem.at[i])
        for i, (src, dst) in enumerate(
            [
                (wzx_in, wzx_ref), (wbc_in, wbc_ref), (wdt_in, wdt_ref), (ids_in, ids_ref),
                (hid_in, hid_ref), (gain_in, gain_ref), (cx_in, cx_ref), (cbc_in, cbc_ref),
                (og_in, og_ref), (wout_in, wo.at[y]),
            ]
        )
    ]
    for load in loads:
        load.start()

    for load in loads[0:3]:
        load.wait()
    bc_t[:, 0:ROWS] = jnp.concatenate([wbc_ref[...], jnp.zeros((32, 256), F32)], axis=0).T[:, 0:ROWS]
    sm_t[...] = jnp.zeros((32, 128), F32)
    sm_t[0:16, 0:ROWS] = bc_t[pl.ds(pl.multiple_of(hd * 16, 16), 16), 0:ROWS]
    sm_t[16:19, 0:ROWS] = wdt_ref[...]
    small[dp] = sm_t[...].astype(BF16)
    zw = wzx_ref[:, 0, :]
    xw = wzx_ref[:, 1, :]
    wst[:, 0:128] = xw[:, 0:128]
    wst[:, 128:256] = jnp.concatenate([xw[:, 128:192], zw[:, 128:192]], axis=1)
    wst[:, 256:384] = zw[:, 0:128]
    own_rows = pl.multiple_of(dp * ROWS, ROWS)
    w_buf[pl.ds(own_rows, ROWS), :] = wst[...].astype(BF16)

    def w_rows(owner):
        return w_buf.at[pl.ds(pl.multiple_of(owner * ROWS, ROWS), ROWS), :]

    weights = Gather([(W_IDS, w_rows)])

    @pl.when(dp == 0)
    def _():
        halo[...] = jnp.zeros_like(halo)

    @pl.when(x // 2 == zh)
    def _():
        tabz[...] = jnp.zeros_like(tabz)

    for j in range(4):
        @pl.when(dp < j + 1)
        def _():
            info_rx[j] = jnp.zeros((16, 128), F32)
            l_rx[j] = jnp.zeros((FEAT, NSTATE), BF16)

        @pl.when(dp + j + 1 > DP - 1)
        def _():
            info_rx[4 + j] = jnp.zeros((16, 128), F32)

    pl.semaphore_wait(barrier, DP - 1 + 6)

    for k in (8, 7, 9, 6, 10, 5, 11, 12, 4, 13, 3, 14, 2, 15, 1):
        send(T_IDS + k - 1, small.at[dp], small.at[dp], dpid(lax.rem(dp + k, DP)))
    weights.own()
    for load in loads[3:9]:
        load.wait()
    send(HALO, hid_ref.at[pl.ds(TOK - 16, 16), :], halo, dpid(lax.rem(dp + 1, DP)), dp < DP - 1)

    phase("ids")
    def wo_rows(y_, c_):
        return wo.at[lax.rem(y_ + 4, 4), pl.ds(pl.multiple_of(c_ * 96, 96), 96), :]

    own_ids = ids_ref[dp].astype(F32)
    prev_ids = ids_ref[jnp.maximum(dp - 1, 0)].astype(F32)
    prev_col = jnp.broadcast_to(prev_ids[3:4, :], (128, 128)).T[112:128, :]
    first_dev = jnp.zeros((16, 128), jnp.int32) + dp == 0
    idc[0:16, :] = jnp.where(first_dev, -1.0, prev_col)
    for q in range(4):
        idc[16 + 128 * q : 144 + 128 * q, :] = jnp.broadcast_to(own_ids[q : q + 1, :], (128, 128)).T
    id_row = jnp.concatenate([own_ids[q : q + 1, :] for q in range(4)], axis=1)

    taps[...] = jnp.zeros_like(taps)
    taps[0:4, 0:128] = cx_ref[:, 0:128]
    taps[0:4, 128:192] = cx_ref[:, 128:192]
    taps[0:4, 256:512] = cbc_ref[...]

    phase("norm")
    gain = gain_ref[...].reshape(1, D)

    def norm_rows(rows):
        h = rows.astype(F32)
        scale = lax.rsqrt(jnp.mean(h * h, axis=1, keepdims=True) + EPSILON)
        return (h * scale * gain).astype(BF16)

    def norm_step(i, carry):
        r = pl.multiple_of(i * 32, 32)
        nrm[pl.ds(pl.multiple_of(16 + r, 16), 32), :] = norm_rows(hid_ref[pl.ds(r, 32), :])
        return carry

    lax.fori_loop(0, TOK // 32, norm_step, 0)
    phase("halo_wait")
    recv(HALO, halo, dpid(mate), dp > 0)
    nrm[0:16, :] = norm_rows(halo[...])

    phase("w_near")
    phase("dt")
    for k in range(1, DP):
        owner = lax.rem(dp + DP - k, DP)
        recv(T_IDS + k - 1, small.at[owner], dpid(owner))
    phase("w_cross")
    weights.cross()
    for j in range(DP):
        rows = jnp.concatenate([small[j].astype(F32), jnp.zeros((96, 128), F32)], axis=0).T
        wdt_mat[ROWS * j : ROWS * j + ROWS, :] = rows[0:ROWS, :].astype(BF16)
    bc_cols = dot(nrm[...], wdt_mat[...])
    bc_rows = jnp.concatenate([bc_cols[16:EXT, :].T, bc_cols[0:128, :].T], axis=1)
    bc_parts[y, zl] = bc_rows[0:16, :].astype(BF16)
    for k in (2, 1, 3):
        zt = lax.rem(zl + k, 4)
        send(BCZ + k - 1, bc_parts.at[y, zl], bc_parts.at[y, zl], hdid(zt, y))
    dt_rows = bc_rows[16:24, 0:TOK].astype(BF16).astype(F32)
    sub = lax.broadcasted_iota(jnp.int32, (8, TOK), 0)
    lane = lax.broadcasted_iota(jnp.int32, (8, TOK), 1)

    def by_head(ref, s):
        return jnp.where(s == 0, ref[0], jnp.where(s == 1, ref[1], ref[2]))

    pre = dt_rows + by_head(dtb_ref, sub)
    step_rows = jnp.maximum(pre, 0.0) + jnp.log1p(jnp.exp(-jnp.abs(pre)))
    rate_rows = -step_rows * jnp.exp(by_head(alog_ref, sub))
    prefix = lane_cumsum(rate_rows)
    id8 = jnp.broadcast_to(id_row, (8, TOK))
    at_end = run_end(prefix, id8)
    first_end = at_end[:, 0:1]
    total = prefix[:, TOK - 1 : TOK]
    info_tx[0:8, :] = jnp.broadcast_to(first_end, (8, 128))
    info_tx[8:16, :] = jnp.broadcast_to(total, (8, 128))
    for j in range(4):
        send(INFO_UP + j, info_tx, info_rx.at[j], dpid(lax.rem(dp + j + 1, DP)), dp + j + 1 < DP)
        send(INFO_DN + j, info_tx, info_rx.at[4 + j], dpid(lax.rem(dp - j - 1 + DP, DP)), dp >= j + 1)

    to_end = jnp.exp(at_end - prefix) * step_rows
    cols[...] = jnp.concatenate([prefix, jnp.zeros((120, TOK), F32)], axis=0).T

    phase("bcz")
    for k in range(1, 4):
        zs = lax.rem(zl + 4 - k, 4)
        recv(BCZ + k - 1, bc_parts.at[y, zs], hdid(zs, y))
    for k in (2, 1, 3):
        send(BCY + k - 1, bc_parts.at[y], bc_parts.at[y], hdid(zl, lax.rem(y + k, 4)))

    def wo_rows(y_, c_):
        return wo.at[lax.rem(y_ + 4, 4), pl.ds(pl.multiple_of(c_ * 96, 96), 96), :]

    loads[9].wait()
    for k in (1, 3, 2):
        send(WO + k - 1, wo_rows(y, c), wo_rows(y, c), hdid(zl, lax.rem(y + k, 4)))

    phase("w_near_rest")
    weights.near()
    weights.near_rest()
    phase("mm1")
    k_half = D // 2
    k_own = pl.multiple_of(zh * k_half, k_half)
    k_far = pl.multiple_of((1 - zh) * k_half, k_half)
    for n in range(0, 384, 128):
        u_buf[:, n : n + 128] = dot(nrm[:, pl.ds(k_own, k_half)], w_buf[pl.ds(k_own, k_half), n : n + 128])

    phase("bc_wait")
    for k in range(1, 4):
        ys = lax.rem(y + 4 - k, 4)
        recv(BCY + k - 1, bc_parts.at[ys], hdid(zl, ys))
    for half in range(2):
        rows = jnp.concatenate(
            [bc_parts[h % 4, h // 4].astype(F32) for h in range(8 * half, 8 * half + 8)], axis=0
        )
        col = 384 + 128 * half
        u_buf[0:16, col : col + 128] = rows[:, TOK : TOK + 128].T[0:16, :]
        u_buf[16:EXT, col : col + 128] = rows[:, 0:TOK].T

    phase("w_far")
    weights.far()
    phase("mm2")
    for n in range(0, 384, 128):
        u_buf[:, n : n + 128] += dot(nrm[:, pl.ds(k_far, k_half)], w_buf[pl.ds(k_far, k_half), n : n + 128])

    phase("conv")
    for r in range(0, EXT, 176):
        u_buf[r : r + 176, 0:384] = u_buf[r : r + 176, 0:384].astype(BF16).astype(F32)

    for q in range(4):
        r = 128 * q
        now = idc[16 + r : 144 + r, :]
        same = [jnp.where(idc[13 + k + r : 141 + k + r, :] == now, 1.0, 0.0) for k in range(3)]

        def conv(col, tap):
            acc = taps[3:4, tap : tap + 128] * u_buf[16 + r : 144 + r, col : col + 128]
            for k in range(3):
                acc = acc + same[k] * (
                    taps[k : k + 1, tap : tap + 128] * u_buf[13 + k + r : 141 + k + r, col : col + 128]
                )
            return (acc * jax.nn.sigmoid(acc)).astype(BF16)

        x0 = conv(0, 0)
        x1 = conv(128, 128)
        x_b[r : r + 128, 0:128] = x0
        x_b[r : r + 128, 128:256] = x1
        x_t[0:128, r : r + 128] = x0.astype(F32).T
        x_t[128:192, r : r + 128] = x1.astype(F32).T[0:64, :]
        b_b[r : r + 128, :] = conv(384, 256)
        c_b[r : r + 128, :] = conv(512, 384)

    phase("lstate")
    last_id = id_row[:, TOK - 1 : TOK]
    is_last = id8 == jnp.broadcast_to(last_id, (8, TOK))

    def weighted_x(weight):
        return jnp.concatenate(
            [x_t[64 * h : 64 * h + 64, :] * weight[h : h + 1, :] for h in range(HEADS)], axis=0
        ).astype(BF16)

    l_tx[...] = dot(weighted_x(jnp.where(is_last, to_end, 0.0)), b_b[...]).astype(BF16)
    for j in range(4):
        send(STATE + j, l_tx, l_rx.at[j], dpid(lax.rem(dp + j + 1, DP)), dp + j + 1 < DP)

    phase("table_loc")
    def first_id(k):
        return ids_ref[jnp.clip(k, 0, DP - 1)][0:1, 0:1]

    def final_id(k):
        return ids_ref[jnp.clip(k, 0, DP - 1)][3:4, 127:128]

    one = jnp.zeros((1, 1), jnp.int32)
    for j in range(4):
        recv(INFO_DN + j, info_rx.at[4 + j], dpid(mate), dp + j + 1 < DP)
    after = jnp.zeros((8, 128), F32)
    for j in range(4):
        goes_on = (first_id(dp + j + 1) == final_id(dp)) & (one + dp + j + 1 < DP)
        after = after + jnp.where(goes_on, info_rx[4 + j, 0:8, :], 0.0)
    carry_on = jnp.broadcast_to(jnp.exp(after)[:, 0:1], (8, TOK))
    xw_end = weighted_x(to_end * jnp.where(is_last, carry_on, 1.0))
    for g in range(PROMPTS):
        mine = jnp.where(idc[16:EXT, :] == float(g), 1.0, 0.0).astype(BF16)
        b_all[:, 128 * g : 128 * g + 128] = b_b[...] * mine
    for g in range(PROMPTS):
        loc[g] = dot(xw_end, b_all[:, 128 * g : 128 * g + 128]).astype(BF16)
    mate_half = pl.multiple_of((1 - c) * 96, 96)
    send(TAB0, loc.at[:, pl.ds(mate_half, 96), :], tab0, dpid(mate))

    phase("scores")
    scol = lax.broadcasted_iota(jnp.int32, (128, TOK), 1)
    srow = lax.broadcasted_iota(jnp.int32, (128, TOK), 0)
    for q in range(4):
        r = 128 * q
        w = r + 128
        scores = dot_t(c_b[r:w, :], b_b[0:w, :])
        ok = (jnp.broadcast_to(idc[16 + r : 16 + w, 0:1], (128, w)) == jnp.broadcast_to(id_row[:, 0:w], (128, w))) & (
            scol[:, 0:w] <= srow[:, 0:w] + r
        )
        scores = jnp.where(ok, scores, 0.0)
        parts = []
        for h in range(HEADS):
            gap = jnp.broadcast_to(cols[r:w, h : h + 1], (128, w)) - prefix[h : h + 1, 0:w]
            mix = (scores * (jnp.exp(jnp.minimum(gap, 0.0)) * step_rows[h : h + 1, 0:w])).astype(BF16)
            col = 0 if h < 2 else 128
            parts.append(dot(mix, x_b[0:w, col : col + 128]))
        low = lax.broadcasted_iota(jnp.int32, (128, 128), 1) < 64
        smask[r:w, 0:128] = jnp.where(low, parts[0], parts[1])
        smask[r:w, 128:256] = parts[2]

    phase("tab0_wait")
    my_half = pl.multiple_of(c * 96, 96)
    recv(TAB0, tab0, dpid(mate))
    for g in range(PROMPTS):
        tabs[g] = (loc[g, pl.ds(my_half, 96), :].astype(F32) + tab0[g].astype(F32)).astype(BF16)
    for t in range(2):
        send(TABC + 2 * x + t, tabs.at[4 - 2 * zh + t], tabz.at[x], dpid(dev(1 - zh, 2 * zh + t, c)))
    for k in (2, 1, 3):
        xt = lax.rem(x + k, 4)
        send(TABX + k - 1, tabs.at[4 * zh + xt], tabx.at[k - 1], dpid(dev(zh, xt, c)))

    phase("wo_mate")
    for k in (1, 3, 2):
        recv(WO + k - 1, wo_rows(y - k, c), dpid(mate))
        send(WO_MATE + k - 1, wo_rows(y - k, c), wo_rows(y - k, c), dpid(mate))
    phase("state_wait")
    for j in range(4):
        recv(INFO_UP + j, info_rx.at[j], dpid(mate), dp >= j + 1)
        recv(STATE + j, l_rx.at[j], dpid(mate), dp >= j + 1)
    state = l_rx[3].astype(F32)
    for j in (2, 1, 0):
        joined = (final_id(dp - j - 1) == final_id(dp - j - 2)) & (one + dp - j - 2 >= 0)
        gain_j = jnp.where(joined, jnp.exp(info_rx[j, 8:16, :]), 0.0)
        rows = jnp.concatenate(
            [jnp.broadcast_to(gain_j[h : h + 1, :], (64, 128)) for h in range(HEADS)], axis=0
        )
        state = l_rx[j].astype(F32) + rows * state
    s_in[0:FEAT, :] = state.astype(BF16)
    s_in[FEAT:256, :] = jnp.zeros((64, NSTATE), BF16)

    phase("yinter")
    before_id = jnp.where(one + dp > 0, final_id(dp - 1), -1).astype(F32)
    lane1 = lax.broadcasted_iota(jnp.int32, (128, 128), 1)
    low = lane1 < 64
    skip0 = jnp.where(low, skip_ref[0], skip_ref[1])
    skip1 = jnp.where(low, skip_ref[2], 0.0)
    og0 = og_ref[:, 0:128]
    og1 = jnp.concatenate([og_ref[:, 128:192], jnp.zeros((1, 64), F32)], axis=1)
    for q in range(4):
        r = 128 * q
        w = r + 128
        inter = dot_t(c_b[r:w, :], s_in[...])
        enters = jnp.where(idc[16 + r : 16 + w, :] == before_id, 1.0, 0.0)
        decay = jnp.exp(cols[r:w, :])
        e0 = jnp.broadcast_to(decay[:, 0:1], (128, 128))
        e1 = jnp.broadcast_to(decay[:, 1:2], (128, 128))
        e2 = jnp.broadcast_to(decay[:, 2:3], (128, 128))
        y0 = smask[r:w, 0:128] + enters * jnp.where(low, e0, e1) * inter[:, 0:128]
        y1 = smask[r:w, 128:256] + enters * e2 * inter[:, 128:256]
        y0 = y0 + skip0 * x_b[r:w, 0:128].astype(F32)
        y1 = y1 + skip1 * x_b[r:w, 128:256].astype(F32)
        z0 = u_buf[16 + r : 16 + w, 256:384]
        z1 = jnp.where(low, pltpu.roll(u_buf[16 + r : 16 + w, 128:256], 64, 1), 0.0)
        g0 = y0 * (z0 * jax.nn.sigmoid(z0))
        g1 = y1 * (z1 * jax.nn.sigmoid(z1))
        sq = jnp.sum(g0 * g0 + g1 * g1, axis=1, keepdims=True)
        hi = sq.astype(BF16).astype(F32)
        g_send[q, :, :, 0:128] = (g0 * og0).astype(BF16).reshape(4, 32, 128)
        g_send[q, :, :, 128:256] = jnp.where(
            low, g1 * og1, jnp.where(lane1 == 64, hi, jnp.where(lane1 == 65, sq - hi, 0.0))
        ).astype(BF16).reshape(4, 32, 128)
    for k in (2, 1, 3):
        yt = lax.rem(y + k, 4)
        send(A2A + k - 1, g_send.at[:, yt], a_rx.at[y], hdid(zl, yt))
    a_rx[y] = g_send[:, y]

    phase("tabx_wait")
    for k in range(1, 4):
        recv(TABX + k - 1, tabx.at[k - 1], dpid(mate))
    shared = x // 2 == 1 - zh
    for j in range(4):
        recv(TABC + 2 * j + lax.rem(x, 2), tabz.at[j], dpid(mate), shared)
    done = tabs[4 * zh + x].astype(F32)
    for k in range(3):
        done = done + tabx[k].astype(F32)
    for j in range(4):
        done = done + tabz[j].astype(F32)
    fin[dp // 2, pl.ds(my_half, 96), :] = done.astype(BF16)

    def f_rows(owner):
        return fin.at[owner // 2, pl.ds(pl.multiple_of(lax.rem(owner, 2) * 96, 96), 96), :]

    phase("fin_own")
    finals = Gather([(F_IDS, f_rows)])
    finals.own()

    phase("wo_finish")
    for k in (1, 3, 2):
        recv(WO_MATE + k - 1, wo_rows(y - k, 1 - c), dpid(mate))

    phase("a2a_wait")
    for k in range(1, 4):
        ys = lax.rem(y + 4 - k, 4)
        recv(A2A + k - 1, a_rx.at[ys], hdid(zl, ys))
    phase("outproj")
    sq = jnp.zeros((128, 1), F32)
    picked = (lane1 == 64) | (lane1 == 65)
    for y_ in range(4):
        tails = a_rx[y_, :, :, 128:256].reshape(128, 128).astype(F32)
        sq = sq + jnp.sum(jnp.where(picked, tails, 0.0), axis=1, keepdims=True)
    hi = sq.astype(BF16).astype(F32)
    tail = jnp.where(lane1 == 0, hi, jnp.where(lane1 == 1, sq - hi, 0.0))
    own_acc[:, D : D + 128] = tail
    part[:, :, D : D + 128] = tail.astype(BF16).reshape(4, 32, 128)
    for n in range(0, D, 256):
        acc = jnp.zeros((128, 256), F32)
        for y_ in range(4):
            acc = acc + dot(a_rx[y_, :, :, 0:FEAT].reshape(128, FEAT), wo[y_, :, n : n + 256])
        own_acc[:, n : n + 256] = acc
        part[:, :, n : n + 256] = acc.astype(BF16).reshape(4, 32, 256)
    for k in (2, 1, 3):
        zt = lax.rem(zl + k, 4)
        send(RSZ + k - 1, part.at[zt], rs_rx.at[k - 1], hdid(zt, y))

    phase("fin_near")
    finals.cross()
    phase("fin_cross")
    finals.near()
    phase("fin_nearrest")
    finals.near_rest()
    phase("fin_far")
    finals.far()
    phase("rsy_wait")
    for k in range(1, 4):
        recv(RSZ + k - 1, rs_rx.at[k - 1], hdid(lax.rem(zl + 4 - k, 4), y))
    phase("out")
    z_rows = pl.ds(pl.multiple_of(zl * 32, 32), 32)
    sq = own_acc[z_rows, D : D + 128]
    for k in range(3):
        sq = sq + rs_rx[k, :, D : D + 128].astype(F32)
    scale = lax.rsqrt(jnp.sum(sq, axis=1, keepdims=True) / (FEAT * HD) + EPSILON)
    acc = own_acc[z_rows, 0:D]
    for k in range(3):
        acc = acc + rs_rx[k, :, 0:D].astype(F32)
    resid = hid_ref[pl.ds(pl.multiple_of(hd * 32, 32), 32), :].astype(F32)
    out_ref[...] = (resid + scale * acc).astype(BF16)

    phase("st_out")
    for r in range(4):
        st_ref[r] = fin[req_ref[r]]

    phase("drain")
    for m, src, dst, to, cond in pending:
        if cond is None:
            msg(m, src, dst, to).wait_send()
        else:
            @pl.when(cond)
            def _():
                msg(m, src, dst, to).wait_send()
    phase(None)


def write_out(rows_ref, states_ref, out_ref, st_ref):
    out_ref[...] = rows_ref[...]
    st_ref[...] = states_ref[...].astype(F32)


def on_device(
    hidden, token_prompt, request_prompt, in_gain, w_zx, w_bc, w_dt, dt_bias, a_log, conv_x,
    conv_bc, skip_gain, out_gain, w_out,
):
    vmem = pl.BlockSpec(memory_space=pltpu.VMEM)
    smem = pl.BlockSpec(memory_space=pltpu.SMEM)
    layer_out, states = pl.pallas_call(
        body,
        out_shape=(
            jax.ShapeDtypeStruct((TOK // HD, D), BF16),
            jax.ShapeDtypeStruct((4, FEAT, NSTATE), BF16),
        ),
        in_specs=[smem] * 4 + [pl.BlockSpec(memory_space=pl.ANY)] * 10,
        out_specs=(vmem, vmem),
        scratch_shapes=[
            pltpu.VMEM((ROWS, 2, FEAT), F32),
            pltpu.VMEM((ROWS, 256), F32),
            pltpu.VMEM((HEADS, ROWS), F32),
            pltpu.VMEM((DP, 4, 128), jnp.int32),
            pltpu.VMEM((TOK, D), BF16),
            pltpu.VMEM((D,), F32),
            pltpu.VMEM((4, FEAT), F32),
            pltpu.VMEM((4, 256), F32),
            pltpu.VMEM((1, FEAT), F32),
            pltpu.VMEM((D, 384), BF16),
            pltpu.VMEM((ROWS, 384), F32),
            pltpu.VMEM((256, 128), F32),
            pltpu.VMEM((32, 128), F32),
            pltpu.VMEM((DP, 32, 128), BF16),
            pltpu.VMEM((D, 128), BF16),
            pltpu.VMEM((4, 4, 16, 640), BF16),
            pltpu.VMEM((16, D), BF16),
            pltpu.VMEM((EXT, D), BF16),
            pltpu.VMEM((EXT, 128), F32),
            pltpu.VMEM((EXT, 640), F32),
            pltpu.VMEM((8, 512), F32),
            pltpu.VMEM((FEAT, TOK), F32),
            pltpu.VMEM((TOK, 256), BF16),
            pltpu.VMEM((TOK, 128), BF16),
            pltpu.VMEM((TOK, 128), BF16),
            pltpu.VMEM((TOK, 128 * PROMPTS), BF16),
            pltpu.VMEM((16, 128), F32),
            pltpu.VMEM((8, 16, 128), F32),
            pltpu.VMEM((FEAT, NSTATE), BF16),
            pltpu.VMEM((4, FEAT, NSTATE), BF16),
            pltpu.VMEM((256, NSTATE), BF16),
            pltpu.VMEM((TOK, 128), F32),
            pltpu.VMEM((TOK, 256), F32),
            pltpu.VMEM((PROMPTS, FEAT, NSTATE), BF16),
            pltpu.VMEM((PROMPTS, 96, NSTATE), BF16),
            pltpu.VMEM((PROMPTS, 96, NSTATE), BF16),
            pltpu.VMEM((4, 96, NSTATE), BF16),
            pltpu.VMEM((3, 96, NSTATE), BF16),
            pltpu.VMEM((PROMPTS, FEAT, NSTATE), BF16),
            pltpu.VMEM((4, 4, 32, 256), BF16),
            pltpu.VMEM((4, 4, 32, 256), BF16),
            pltpu.VMEM((4, FEAT, D), BF16),
            pltpu.VMEM((4, 32, OUTW), BF16),
            pltpu.VMEM((128, OUTW), F32),
            pltpu.VMEM((3, 32, OUTW), BF16),
            pltpu.SemaphoreType.DMA((N_MSG,)),
            pltpu.SemaphoreType.DMA((N_MSG,)),
            pltpu.SemaphoreType.DMA((10,)),
        ],
        compiler_params=pltpu.CompilerParams(
            collective_id=0, has_side_effects=True, vmem_limit_bytes=60 * 2**20
        ),
        name="layer",
    )(
        request_prompt, dt_bias, a_log, skip_gain, w_zx, w_bc, w_dt.T,
        token_prompt.reshape(DP, 4, 128), hidden, in_gain, conv_x, conv_bc,
        out_gain.reshape(1, FEAT), w_out,
    )
    layer_out, states = pl.pallas_call(
        write_out,
        out_shape=(
            jax.ShapeDtypeStruct((TOK // HD, D), BF16),
            jax.ShapeDtypeStruct((4, FEAT, NSTATE), F32),
        ),
        in_specs=[vmem, vmem],
        out_specs=(vmem, vmem),
        name="write_out",
    )(layer_out, states)
    return layer_out, states.reshape(4, HEADS, 64, NSTATE)


def solution(mesh):
    in_specs = (
        P("dp", None), P(), P("dp"), P(), P("dp", None, "head"), P("dp", None), P("dp", "head"),
        P("head"), P("head"), P(None, "head"), P(), P("head"), P("head"), P("head", None),
    )
    out_specs = (P(("dp", "head"), None), P("dp", "head", None, None))
    return jax.shard_map(on_device, mesh=mesh, in_specs=in_specs, out_specs=out_specs, check_vma=False)
```
